32 devices in a mesh: grp: 2 (over x), chan: 4 (over y, core), ctx: 4 (over z).
Axes of the slice: x: 2, y: 2, z: 4, core: 2. Of those that a mesh axis runs over, the one named last changes fastest.
Arguments:
- features: bfloat16 [4096, 4096], P(('grp', 'ctx'), 'chan'), parts along dimension 0, may hold values from -6 to 6
- filter_taps: bfloat16 [2048, 4096], P(None, 'chan'), may hold values from -0.125 to 0.125
- skip_gain: float32 [4096], P('chan'), may hold values from -4 to 4
- in_weight: bfloat16 [4096, 3, 4096], P(None, None, 'chan'), may hold values from -0.09375 to 0.09375
- out_weight: bfloat16 [4096, 4096], P(None, 'chan'), may hold values from -0.125 to 0.125
Outputs:
- layer_out: bfloat16 [4096, 4096], P(('grp', 'ctx'), 'chan'), parts along dimension 0
The draws below stay inside these ranges and needn't reach their ends.
There are 2 independent parts, one for each index of `grp`. The reference program is written for one: setup_inputs(seed, part) draws one part's arguments, and reference() takes and returns one part's arrays. A program takes and returns all parts, laid end to end along the dimension named above; an argument that names none is the same for every part. Nothing has to cross between parts.
All inputs are finite; a program needn't handle non-finite values.
Results may differ from the reference program's by a relative error of at most 0.013.
Values may be sent and summed in bfloat16 or wider, within the bound.
No kernel may reach another device: no remote copies, remote signals or barrier semaphores. Data moves between devices by JAX's collectives and lax.ppermute only.
A program may use at most 320 MiB of HBM per device.

```python
import math
import jax
import jax.numpy as jnp
from jax import lax

D = 4096
P_SIZE = 128
LENGTH = 2048


def spiked(values, rng, source, target, parts, factor):
    owner, partner = [(jnp.arange(values.shape[position]) // (values.shape[position] // parts)).reshape([-1 if axis == position else 1 for axis in range(values.ndim)]) for position in (source, target)]
    chosen = jax.random.permutation(rng, parts)[partner]
    strong = (owner == chosen) | (owner == (partner + parts // 2) % parts)
    return jnp.where(strong, factor * values, values)


def block_levels(stream_key, extent, cuts, least, largest):
    factor_of, own = 1.0, jax.random.fold_in(stream_key, 6)
    for position, parts in cuts:
        heights = jnp.exp(jax.random.uniform(jax.random.fold_in(own, position), (parts,), jnp.float32, least / len(cuts), largest / len(cuts)))
        factor_of = factor_of * jnp.repeat(heights, extent[position] // parts).reshape([-1 if axis == position else 1 for axis in range(len(extent))])
    return factor_of


def normal_values(rng, extent, scale, most, pieces=(), held_as=jnp.bfloat16):
    entries = jax.random.normal(rng, extent, jnp.float32) * scale
    if len(pieces) > 0:
        entries = block_levels(rng, extent, pieces, -0.22, 0.18) * entries
    return jnp.clip(entries, min=-most, max=most).astype(held_as)


def bell_draw_with(own_key, extent, scale, limit, shards, heavy, held_as=jnp.bfloat16):
    array = scale * jax.random.normal(own_key, extent, jnp.float32)
    if shards:
        array = array * block_levels(own_key, extent, shards, -0.22, 0.18)
    return jnp.clip(spiked(array, jax.random.fold_in(own_key, 3), *heavy), -limit, limit).astype(held_as)


def setup_inputs(seed: int = 0, part: int = 0) -> dict:
    key_list = jax.random.split(jax.random.key(seed), 6)
    part_keys = jax.random.split(jax.random.fold_in(key_list[5], part), 6)
    features = normal_values(part_keys[0], (LENGTH, D), 1.0, 6.0, ((0, 4), (1, 4)))
    filter_taps = normal_values(key_list[1], (LENGTH, D), LENGTH ** -0.5, 0.125, ((1, 4),))
    skip_gain = normal_values(key_list[2], (D,), 1.0, 4.0, ((0, 4),), jnp.float32)
    in_weight = normal_values(key_list[3], (D, 3, D), D ** -0.5, 0.09375, ((2, 4),))
    out_weight = bell_draw_with(key_list[4], (D, D), D ** -0.5, 0.125, ((1, 4),), (0, 1, 4, 2.0))
    return dict(features=features, filter_taps=filter_taps, skip_gain=skip_gain, in_weight=in_weight, out_weight=out_weight)


def dft_tables(block_len):
    period = 2 * block_len
    freq_col = jnp.arange(period, dtype=jnp.int32)[:, None]
    place_row = jnp.arange(period, dtype=jnp.int32)[None, :]
    angles = ((freq_col * place_row) % period).astype(jnp.float32) * (2.0 * math.pi / period)
    forward = jnp.concatenate([jnp.cos(angles), -jnp.sin(angles)], axis=0).astype(jnp.bfloat16)
    out_place = jnp.arange(block_len, dtype=jnp.int32)[:, None] + block_len
    angle_out = ((out_place * place_row) % period).astype(jnp.float32) * (2.0 * math.pi / period)
    inverse = (jnp.concatenate([jnp.cos(angle_out), -jnp.sin(angle_out)], axis=1) / period).astype(jnp.bfloat16)
    return forward, inverse


def reference(features, filter_taps, skip_gain, in_weight, out_weight):
    blocks = LENGTH // P_SIZE
    period = 2 * P_SIZE
    highest = lax.Precision.HIGHEST
    forward, inverse = dft_tables(P_SIZE)
    projected = jnp.dot(features, in_weight.reshape(D, 3 * D), preferred_element_type=jnp.float32)
    query_rows = projected[:, :D].astype(jnp.bfloat16)
    mixed_in = (projected[:, D:2 * D] * projected[:, 2 * D:]).astype(jnp.bfloat16)
    kv_blocks = mixed_in.reshape(blocks, P_SIZE, D).astype(jnp.float32)
    input_spectra = jnp.einsum('fp,bpd->bfd', forward[:, :P_SIZE].astype(jnp.float32), kv_blocks, precision=highest).astype(jnp.bfloat16)
    padded = jnp.concatenate([jnp.zeros((P_SIZE, D), jnp.bfloat16), filter_taps], axis=0)
    tap_blocks = padded.reshape(blocks + 1, P_SIZE, D)
    segments = jnp.concatenate([tap_blocks[:-1], tap_blocks[1:]], axis=1).astype(jnp.float32)
    lag_spectra = jnp.einsum('fn,knd->kfd', forward.astype(jnp.float32), segments, precision=highest).astype(jnp.bfloat16)
    flipped = jnp.concatenate([lag_spectra[::-1], jnp.zeros_like(lag_spectra)], axis=0)
    source = input_spectra.astype(jnp.float32)
    source_re = source[:, :period]
    source_im = source[:, period:]

    def one_block(out_block):
        window = lax.dynamic_slice_in_dim(flipped, (blocks - 1 - out_block).astype(jnp.int32), blocks, 0).astype(jnp.float32)
        lag_re = window[:, :period]
        lag_im = window[:, period:]
        out_re = jnp.sum(lag_re * source_re - lag_im * source_im, axis=0)
        out_im = jnp.sum(lag_re * source_im + lag_im * source_re, axis=0)
        return jnp.concatenate([out_re, out_im], axis=0).astype(jnp.bfloat16)

    block_spectra = lax.map(one_block, jnp.arange(blocks, dtype=jnp.int32))
    conv_out = jnp.einsum('tf,bfd->btd', inverse.astype(jnp.float32), block_spectra.astype(jnp.float32), precision=highest).reshape(LENGTH, D)
    gated_rows = (query_rows.astype(jnp.float32) * (conv_out + skip_gain[None, :] * mixed_in.astype(jnp.float32))).astype(jnp.bfloat16)
    return jnp.dot(gated_rows, out_weight, preferred_element_type=jnp.float32).astype(jnp.bfloat16)
```

```python
import functools
import math

import jax
import jax.numpy as jnp
import ml_dtypes
import numpy as np
from jax import lax
from jax.experimental import pallas as pl
from jax.experimental.pallas import tpu as pltpu
from jax.sharding import PartitionSpec as P


BF16 = jnp.bfloat16
F32 = jnp.float32
LANES = 128
CHUNKS = 2


def real_dft_tables(block):
    period = 2 * block
    freq = np.arange(block)[:, None]
    place = np.arange(block)[None, :]
    angle = (freq * place % period) * (2.0 * math.pi / period)
    lower = -np.sin(angle)
    lower[0] = 1.0 - 2.0 * (np.arange(block) % 2)
    forward = np.concatenate([np.cos(angle), lower], axis=0)
    out_place = np.arange(block)[:, None] + block
    freq_row = np.arange(block)[None, :]
    angle_out = (out_place * freq_row % period) * (2.0 * math.pi / period)
    weight = np.where(freq_row == 0, 1.0, 2.0)
    lower_out = -np.sin(angle_out) * weight
    lower_out[:, 0] = 1.0 - 2.0 * (np.arange(block) % 2)
    inverse = np.concatenate([np.cos(angle_out) * weight, lower_out], axis=1) / period
    return forward.astype(ml_dtypes.bfloat16), inverse.astype(ml_dtypes.bfloat16)


def filter_kernel(pos_ref, fwd_ref, taps_ref, out_ref, prev_ref):
    k = pl.program_id(0)
    rows = fwd_ref.shape[0]

    @pl.when(k == 0)
    def _():
        prev_ref[...] = jnp.zeros_like(prev_ref)

    now = jnp.dot(fwd_ref[...], taps_ref[...], preferred_element_type=F32)
    parity = lax.broadcasted_iota(jnp.int32, now.shape, 0) % 2
    out_ref[0] = prev_ref[...] + jnp.where(parity == 0, now, -now)
    prev_ref[...] = now


def filter_spectra(pos, forward, taps, width, block):
    count = taps.shape[0] // block
    rows = 2 * block
    return pl.pallas_call(
        filter_kernel,
        out_shape=jax.ShapeDtypeStruct((count, rows, width), F32),
        grid_spec=pltpu.PrefetchScalarGridSpec(
            num_scalar_prefetch=1,
            grid=(count,),
            in_specs=[
                pl.BlockSpec((rows, block), lambda k, s: (0, 0)),
                pl.BlockSpec((block, width), lambda k, s: (k, s[0])),
            ],
            out_specs=pl.BlockSpec((1, rows, width), lambda k, s: (k, 0, 0)),
            scratch_shapes=[pltpu.VMEM((rows, width), F32)],
        ),
        cost_estimate=pl.CostEstimate(
            flops=2 * count * rows * block * width,
            bytes_accessed=count * width * (rows * 4 + block * 2),
            transcendentals=0,
        ),
        name="filter_spectra",
    )(pos, forward, taps)


def kv_kernel(n_pieces, n_out, pos_ref, *refs):
    pieces = refs[:n_pieces]
    wk_ref, wv_ref = refs[n_pieces : n_pieces + 2]
    outs = refs[n_pieces + 2 :]
    i = pl.program_id(0)
    depth = pieces[0].shape[1]
    key = value = None
    for j, piece in enumerate(pieces):
        rows = pl.ds(pl.multiple_of(pos_ref[1 + j] * depth, depth), depth)
        x = piece[...]
        a = jnp.dot(x, wk_ref[0, rows, :], preferred_element_type=F32)
        b = jnp.dot(x, wv_ref[0, rows, :], preferred_element_type=F32)
        key = a if key is None else key + a
        value = b if value is None else value + b
    mixed = (key * value).astype(BF16)
    for k in range(n_out):

        @pl.when(i == k)
        def _(k=k):
            outs[k][...] = mixed


def mixed_inputs(pos, pieces, chunk, w, n_ctx):
    tokens, depth = pieces[1].shape
    total = w.shape[1]
    width = w.shape[2] // n_ctx
    specs = [pl.BlockSpec((tokens, depth), lambda i, s: (chunk, 0))]
    specs += [pl.BlockSpec((tokens, depth), lambda i, s: (0, 0)) for _ in pieces[1:]]
    specs += [
        pl.BlockSpec((1, total, width), lambda i, s, g=g: (g, 0, (s[0] + i) % n_ctx)) for g in (1, 2)
    ]
    return pl.pallas_call(
        functools.partial(kv_kernel, len(pieces), n_ctx),
        out_shape=[jax.ShapeDtypeStruct((tokens, width), BF16)] * n_ctx,
        grid_spec=pltpu.PrefetchScalarGridSpec(
            num_scalar_prefetch=1,
            grid=(n_ctx,),
            in_specs=specs,
            out_specs=[pl.BlockSpec((tokens, width), lambda i, s: (0, 0))] * n_ctx,
        ),
        cost_estimate=pl.CostEstimate(
            flops=4 * tokens * total * width * n_ctx,
            bytes_accessed=4 * total * width * n_ctx + 2 * tokens * total,
            transcendentals=0,
        ),
        name="kv_projection",
    )(pos, *pieces, w, w)


def query_kernel(n_pieces, chunks, pos_ref, own_ref, *refs):
    others = refs[: (n_pieces - 1) * chunks]
    w_ref, out_ref = refs[-2:]
    tokens, depth = others[0].shape
    for c in range(chunks):
        acc = None
        for j in range(n_pieces):
            rows = pl.ds(pl.multiple_of(pos_ref[1 + j] * depth, depth), depth)
            if j == 0:
                x = own_ref[c * tokens : (c + 1) * tokens, :]
            else:
                x = others[c * (n_pieces - 1) + j - 1][...]
            a = jnp.dot(x, w_ref[0, rows, :], preferred_element_type=F32)
            acc = a if acc is None else acc + a
        out_ref[c * tokens : (c + 1) * tokens, :] = acc.astype(BF16)


def queries(pos, own, received, w, n_ctx):
    chunks = len(received)
    n_pieces = 1 + len(received[0])
    tokens, depth = received[0][0].shape
    total = w.shape[1]
    width = w.shape[2] // n_ctx
    rows = own.shape[0]
    specs = [pl.BlockSpec((rows, depth), lambda i, s: (0, 0))]
    specs += [pl.BlockSpec((tokens, depth), lambda i, s: (0, 0))] * (chunks * (n_pieces - 1))
    specs += [pl.BlockSpec((1, total, width), lambda i, s: (0, 0, (s[0] + i) % n_ctx))]
    return pl.pallas_call(
        functools.partial(query_kernel, n_pieces, chunks),
        out_shape=jax.ShapeDtypeStruct((rows, w.shape[2]), BF16),
        grid_spec=pltpu.PrefetchScalarGridSpec(
            num_scalar_prefetch=1,
            grid=(n_ctx,),
            in_specs=specs,
            out_specs=pl.BlockSpec((rows, width), lambda i, s: (0, i)),
        ),
        cost_estimate=pl.CostEstimate(
            flops=2 * rows * total * width * n_ctx,
            bytes_accessed=2 * total * width * n_ctx + 2 * rows * total,
            transcendentals=0,
        ),
        name="q_projection",
    )(pos, own, *[p for group in received for p in group], w)


def conv_kernel(n_ctx, chunks, pos_ref, fwd_ref, inv_ref, g_ref, *refs):
    n_in = n_ctx * chunks
    ins, outs = refs[:n_in], refs[n_in : 2 * n_in]
    x_ref, y_ref = refs[2 * n_in :]
    me = pos_ref[0]
    blocks = n_in
    block = inv_ref.shape[0]
    width = g_ref.shape[2]
    for k in range(n_ctx):
        source = (me - k + n_ctx) % n_ctx
        for c in range(chunks):
            x_ref[source * chunks + c] = jnp.dot(
                fwd_ref[...], ins[c * n_ctx + k][...], preferred_element_type=F32
            )

    def tile(i, first):
        upper = pl.ds(i * 8, 8) if first else pl.ds(pl.multiple_of(i * 8, 8), 8)
        lower = pl.ds(block + i * 8, 8) if first else pl.ds(pl.multiple_of(block + i * 8, 8), 8)
        for lane in range(width // LANES):
            cols = pl.ds(lane * LANES, LANES)
            g_re = [g_ref[b, upper, cols] for b in range(blocks)]
            g_im = [g_ref[b, lower, cols] for b in range(blocks)]
            x_re = [x_ref[b, upper, cols] for b in range(blocks)]
            x_im = [x_ref[b, lower, cols] for b in range(blocks)]
            if first:
                edge = lax.broadcasted_iota(jnp.int32, (8, LANES), 0) == 0
                g_di = [jnp.where(edge, im, re) for re, im in zip(g_re, g_im)]
                g_im = [jnp.where(edge, 0.0, im) for im in g_im]
            else:
                g_di = g_re
            for b in range(blocks):
                re = g_re[b] * x_re[0] - g_im[b] * x_im[0]
                im = g_di[b] * x_im[0] + g_im[b] * x_re[0]
                for a in range(1, b + 1):
                    re = re + (g_re[b - a] * x_re[a] - g_im[b - a] * x_im[a])
                    im = im + (g_di[b - a] * x_im[a] + g_im[b - a] * x_re[a])
                y_ref[b, upper, cols] = re
                y_ref[b, lower, cols] = im

    tile(0, True)
    pl.loop(1, block // 8)(lambda i: tile(i, False))

    for c in range(chunks):
        for k in range(n_ctx):
            target = (me + k) % n_ctx
            spectrum = y_ref[target * chunks + c].astype(BF16)
            outs[c * n_ctx + k][...] = jnp.dot(
                inv_ref[...], spectrum, preferred_element_type=F32
            ).astype(BF16)


def convolve(pos, forward, inverse, spectra, mixed, n_ctx):
    chunks = len(mixed)
    blocks, rows, width = spectra.shape
    block = rows // 2
    n_in = n_ctx * chunks
    vmem = pl.BlockSpec(memory_space=pltpu.VMEM)
    outs = pl.pallas_call(
        functools.partial(conv_kernel, n_ctx, chunks),
        out_shape=[jax.ShapeDtypeStruct((block, width), BF16)] * n_in,
        in_specs=[pl.BlockSpec(memory_space=pltpu.SMEM)] + [vmem] * (3 + n_in),
        out_specs=[vmem] * n_in,
        scratch_shapes=[pltpu.VMEM((blocks, rows, width), F32)] * 2,
        cost_estimate=pl.CostEstimate(
            flops=4 * blocks * rows * block * width,
            bytes_accessed=blocks * rows * width * 8,
            transcendentals=0,
        ),
        name="block_conv",
    )(pos, forward, inverse, spectra, *[m for group in mixed for m in group])
    return [outs[c * n_ctx : (c + 1) * n_ctx] for c in range(chunks)]


def gate_kernel(n_ctx, pos_ref, skip_ref, q_ref, *refs):
    mixed, conv, out_ref = refs[:n_ctx], refs[n_ctx : 2 * n_ctx], refs[-1]
    width = mixed[0].shape[1]
    for m in range(n_ctx):
        cols = slice(m * width, (m + 1) * width)
        skip = skip_ref[pl.ds((pos_ref[0] + m) % n_ctx, 1), :]
        total = conv[(-m) % n_ctx][...].astype(F32) + skip * mixed[m][...].astype(F32)
        out_ref[:, cols] = (q_ref[:, cols].astype(F32) * total).astype(BF16)


def gate(pos, skip, query, mixed, conv, chunk, n_ctx):
    tokens, width = mixed[0].shape
    spec = pl.BlockSpec((tokens, width), lambda i, s: (0, 0))
    return pl.pallas_call(
        functools.partial(gate_kernel, n_ctx),
        out_shape=jax.ShapeDtypeStruct((tokens, query.shape[1]), BF16),
        grid_spec=pltpu.PrefetchScalarGridSpec(
            num_scalar_prefetch=1,
            grid=(1,),
            in_specs=[
                pl.BlockSpec((n_ctx, width), lambda i, s: (0, 0)),
                pl.BlockSpec((tokens, query.shape[1]), lambda i, s: (chunk, 0)),
            ]
            + [spec] * (2 * n_ctx),
            out_specs=pl.BlockSpec((tokens, query.shape[1]), lambda i, s: (0, 0)),
        ),
        cost_estimate=pl.CostEstimate(
            flops=3 * tokens * query.shape[1],
            bytes_accessed=8 * tokens * query.shape[1],
            transcendentals=0,
        ),
        name="gate",
    )(pos, skip, query, *mixed, *conv)


def out_kernel(n_pieces, n_ctx, pos_ref, *refs):
    pieces, w_ref, out_ref = refs[:n_pieces], refs[n_pieces], refs[-1]
    width = pieces[0].shape[1] // n_ctx
    acc = None
    for j, piece in enumerate(pieces):
        for m in range(n_ctx):
            first = (pos_ref[1 + j] * n_ctx + (pos_ref[0] + m) % n_ctx) * width
            w = w_ref[pl.ds(pl.multiple_of(first, width), width), :]
            a = jnp.dot(piece[:, m * width : (m + 1) * width], w, preferred_element_type=F32)
            acc = a if acc is None else acc + a
    out_ref[...] = acc.astype(BF16)


def project_out(pos, pieces, w, chunk, rows, before, n_ctx, columns=256):
    tokens, depth = pieces[0].shape
    total, out_width = w.shape
    specs = [pl.BlockSpec((tokens, depth), lambda i, s: (0, 0))] * len(pieces)
    specs += [pl.BlockSpec((total, columns), lambda i, s: (0, i))]
    operands = [*pieces, w]
    aliases = {}
    if before is not None:
        specs.append(pl.BlockSpec(memory_space=pl.ANY))
        aliases = {1 + len(operands): 0}
        operands.append(before)
    return pl.pallas_call(
        functools.partial(out_kernel, len(pieces), n_ctx),
        out_shape=jax.ShapeDtypeStruct((rows, out_width), BF16),
        grid_spec=pltpu.PrefetchScalarGridSpec(
            num_scalar_prefetch=1,
            grid=(out_width // columns,),
            in_specs=specs,
            out_specs=pl.BlockSpec((tokens, columns), lambda i, s: (chunk, i)),
        ),
        input_output_aliases=aliases,
        cost_estimate=pl.CostEstimate(
            flops=2 * tokens * total * out_width,
            bytes_accessed=2 * total * out_width + 2 * tokens * (total + out_width),
            transcendentals=0,
        ),
        name="out_projection",
    )(pos, *operands)


def gather_chan(x, peer, n_chan):
    pieces = []
    for hop in range(1, n_chan // 2):
        far = lax.ppermute(x, "chan", [(i, (i + 2 * hop) % n_chan) for i in range(n_chan)])
        pieces += [far, lax.ppermute(far, "chan", peer)]
    return pieces


def layer(features, filter_taps, skip_gain, in_weight, out_weight):
    n_ctx, n_chan = lax.axis_size("ctx"), lax.axis_size("chan")
    me, chan = lax.axis_index("ctx"), lax.axis_index("chan")
    rows, channels = features.shape[0], in_weight.shape[2]
    width = channels // n_ctx
    block = rows // CHUNKS
    peer = [(i, i ^ 1) for i in range(n_chan)]
    sources = [chan, chan ^ 1]
    for hop in range(1, n_chan // 2):
        far = (chan - 2 * hop + n_chan) % n_chan
        sources += [far, far ^ 1]
    pos = jnp.stack([me, *sources]).astype(jnp.int32)
    forward, inverse = (jnp.asarray(t) for t in real_dft_tables(block))
    w = in_weight.transpose(1, 0, 2)
    skip = skip_gain.reshape(n_ctx, width)

    received = []
    for c in range(CHUNKS):
        part = features[c * block : (c + 1) * block]
        received.append([lax.ppermute(part, "chan", peer), *gather_chan(part, peer, n_chan)])
    spectra = filter_spectra(pos, forward, filter_taps, width, block)

    mixed, arrived = [], []
    for c in range(CHUNKS):
        own = mixed_inputs(pos, [features, *received[c]], c, w, n_ctx)
        mixed.append(own)
        arrived.append(
            [own[0]]
            + [
                lax.ppermute(own[k], "ctx", [(i, (i + k) % n_ctx) for i in range(n_ctx)])
                for k in range(1, n_ctx)
            ]
        )
    query = queries(pos, features, received, w, n_ctx)
    conv = convolve(pos, forward, inverse, spectra, arrived, n_ctx)

    out = None
    for c in range(CHUNKS):
        back = [conv[c][0]] + [
            lax.ppermute(conv[c][k], "ctx", [(i, (i + k) % n_ctx) for i in range(n_ctx)])
            for k in range(1, n_ctx)
        ]
        gated = gate(pos, skip, query, mixed[c], back, c, n_ctx)
        pieces = [gated, lax.ppermute(gated, "chan", peer), *gather_chan(gated, peer, n_chan)]
        out = project_out(pos, pieces, out_weight, c, rows, out, n_ctx)
    return out


P_SIZE = 128


def dft_tables(block_len):
    period = 2 * block_len
    freq_col = jnp.arange(period, dtype=jnp.int32)[:, None]
    place_row = jnp.arange(period, dtype=jnp.int32)[None, :]
    angles = (freq_col * place_row % period).astype(F32) * (2.0 * math.pi / period)
    forward = jnp.concatenate([jnp.cos(angles), -jnp.sin(angles)], axis=0).astype(BF16)
    out_place = jnp.arange(block_len, dtype=jnp.int32)[:, None] + block_len
    angle_out = (out_place * place_row % period).astype(F32) * (2.0 * math.pi / period)
    inverse = (jnp.concatenate([jnp.cos(angle_out), -jnp.sin(angle_out)], axis=1) / period).astype(BF16)
    return (forward, inverse)


def plain_layer(features, filter_taps, skip_gain, in_weight, out_weight):
    forward, inverse = dft_tables(P_SIZE)
    channels = in_weight.shape[2]
    tok_rows = features.shape[0]
    per_dev = tok_rows // P_SIZE
    period = 2 * P_SIZE
    total_blocks = per_dev * lax.axis_size("ctx")
    first_mine = lax.axis_index("ctx") * per_dev
    padded = jnp.concatenate([jnp.zeros((P_SIZE, channels), BF16), filter_taps], axis=0)
    tap_blocks = padded.reshape(total_blocks + 1, P_SIZE, channels)
    segments = jnp.concatenate([tap_blocks[:-1], tap_blocks[1:]], axis=1)
    lag = jnp.einsum("fn,knc->kfc", forward, segments, preferred_element_type=F32).astype(BF16)
    flipped = jnp.concatenate([lag[::-1], jnp.zeros_like(lag)], axis=0)
    gathered = lax.all_gather(features, "chan", axis=1, tiled=True)
    w = in_weight.transpose(1, 0, 2)
    q, k, v = (jnp.dot(gathered, w[s], preferred_element_type=F32) for s in range(3))
    query = q.astype(BF16)
    mixed = (k * v).astype(BF16)
    everyone = lax.all_gather(mixed, "ctx", axis=0, tiled=True).reshape(total_blocks, P_SIZE, channels)
    source = jnp.einsum("fp,bpc->bfc", forward[:, :P_SIZE], everyone, preferred_element_type=F32)
    source = source.astype(BF16).astype(F32)
    source_re, source_im = source[:, :period], source[:, period:]
    outputs = []
    for out_block in range(per_dev):
        start = total_blocks - 1 - (first_mine + out_block)
        window = lax.dynamic_slice_in_dim(flipped, start, total_blocks, 0).astype(F32)
        lag_re, lag_im = window[:, :period], window[:, period:]
        out_re = jnp.sum(lag_re * source_re - lag_im * source_im, axis=0)
        out_im = jnp.sum(lag_re * source_im + lag_im * source_re, axis=0)
        outputs.append(jnp.concatenate([out_re, out_im], axis=0))
    spectra = jnp.stack(outputs).astype(BF16)
    conv = jnp.einsum("tf,bfc->btc", inverse, spectra, preferred_element_type=F32)
    conv = conv.reshape(tok_rows, channels)
    gated = (query.astype(F32) * (conv + skip_gain[None, :] * mixed.astype(F32))).astype(BF16)
    everything = lax.all_gather(gated, "chan", axis=1, tiled=True)
    return jnp.dot(everything, out_weight, preferred_element_type=F32).astype(BF16)


def shards(features, filter_taps, skip_gain, in_weight, out_weight):
    slices = in_weight.shape[2] % (lax.axis_size("ctx") * LANES) == 0
    paired = lax.axis_size("chan") % 2 == 0
    blocks = features.shape[0] % (CHUNKS * LANES) == 0
    chosen = layer if slices and paired and blocks else plain_layer
    return chosen(features, filter_taps, skip_gain, in_weight, out_weight)


def solution(mesh):
    return jax.shard_map(
        shards,
        mesh=mesh,
        in_specs=(
            P(("grp", "ctx"), "chan"),
            P(None, "chan"),
            P("chan"),
            P(None, None, "chan"),
            P(None, "chan"),
        ),
        out_specs=P(("grp", "ctx"), "chan"),
        check_vma=False,
    )
```

```python
import functools
import math

import jax
import jax.numpy as jnp
import ml_dtypes
import numpy as np
from jax import lax
from jax.experimental import pallas as pl
from jax.experimental.pallas import tpu as pltpu
from jax.sharding import PartitionSpec as P


BF16 = jnp.bfloat16
F32 = jnp.float32
LANES = 128
MIB = 1 << 20
CHUNKS = 2
BLOCK = 256
VMEM = pl.BlockSpec(memory_space=pltpu.VMEM)


def real_dft_tables(block):
    period = 2 * block
    freq = np.arange(block)[:, None]
    place = np.arange(block)[None, :]
    angle = (freq * place % period) * (2.0 * math.pi / period)
    lower = -np.sin(angle)
    lower[0] = 1.0 - 2.0 * (np.arange(block) % 2)
    forward = np.concatenate([np.cos(angle), lower], axis=0)
    out_place = np.arange(block)[:, None] + block
    freq_row = np.arange(block)[None, :]
    angle_out = (out_place * freq_row % period) * (2.0 * math.pi / period)
    weight = np.where(freq_row == 0, 1.0, 2.0)
    lower_out = -np.sin(angle_out) * weight
    lower_out[:, 0] = 1.0 - 2.0 * (np.arange(block) % 2)
    inverse = np.concatenate([np.cos(angle_out) * weight, lower_out], axis=1) / period
    return forward.astype(ml_dtypes.bfloat16), inverse.astype(ml_dtypes.bfloat16)


def call(kernel, out, operands, limit, flops, moved, scratch=()):
    return pl.pallas_call(
        kernel,
        out_shape=out,
        in_specs=[VMEM] * len(operands),
        out_specs=jax.tree.map(lambda _: VMEM, out),
        scratch_shapes=scratch,
        compiler_params=pltpu.CompilerParams(vmem_limit_bytes=limit * MIB),
        cost_estimate=pl.CostEstimate(flops=flops, bytes_accessed=moved, transcendentals=0),
    )(*operands)


def chan_sources():
    n_chan, chan = lax.axis_size("chan"), lax.axis_index("chan")
    sources = [chan, chan ^ 1]
    for hop in range(1, n_chan // 2):
        far = (chan - 2 * hop + n_chan) % n_chan
        sources += [far, far ^ 1]
    return sources


def rows_at(first, count):
    return pl.ds(pl.multiple_of(first * count, count), count)


def prologue_kernel(
    width, fwd_ref, skip_ref, taps_ref, w_ref, kv_ref, query_ref, out_ref, skip_out, taps_in, prev_ref, sems
):
    block = fwd_ref.shape[1]
    cols = rows_at(lax.axis_index("ctx"), width)
    copies = [
        pltpu.make_async_copy(taps_ref.at[:, cols], taps_in, sems.at[0]),
        pltpu.make_async_copy(w_ref.at[1:3], kv_ref, sems.at[1]),
        pltpu.make_async_copy(w_ref.at[0], query_ref, sems.at[2]),
    ]
    for copy in copies:
        copy.start()
    prev_ref[...] = jnp.zeros_like(prev_ref)
    skip_out[...] = skip_ref[...]
    copies[0].wait()

    @pl.loop(0, out_ref.shape[0])
    def _(k):
        now = jnp.dot(fwd_ref[...], taps_in[rows_at(k, block), :], preferred_element_type=F32)
        parity = lax.broadcasted_iota(jnp.int32, now.shape, 0) % 2
        out_ref[k] = prev_ref[...] + jnp.where(parity == 0, now, -now)
        prev_ref[...] = now

    for copy in copies[1:]:
        copy.wait()


def prologue(forward, skip, taps, w, width):
    rows, block = forward.shape
    count = taps.shape[0] // block
    out = [
        jax.ShapeDtypeStruct((2, *w.shape[1:]), BF16),
        jax.ShapeDtypeStruct(w.shape[1:], BF16),
        jax.ShapeDtypeStruct((count, rows, width), F32),
        jax.ShapeDtypeStruct(skip.shape, F32),
    ]
    hbm = pl.BlockSpec(memory_space=pl.ANY)
    return pl.pallas_call(
        functools.partial(prologue_kernel, width),
        out_shape=out,
        in_specs=[VMEM, VMEM, hbm, hbm],
        out_specs=[VMEM] * 4,
        scratch_shapes=[
            pltpu.VMEM((taps.shape[0], width), BF16),
            pltpu.VMEM((rows, width), F32),
            pltpu.SemaphoreType.DMA((3,)),
        ],
        compiler_params=pltpu.CompilerParams(vmem_limit_bytes=6 * MIB),
        cost_estimate=pl.CostEstimate(
            flops=2 * count * rows * block * width,
            bytes_accessed=2 * w.size + count * width * (rows * 4 + block * 2),
            transcendentals=0,
        ),
        name="prologue",
    )(forward, skip, taps, w)


def kv_kernel(n_pieces, n_out, starts, w_ref, *refs):
    pieces, outs = refs[:n_pieces], refs[n_pieces:]
    tokens, width = outs[0].shape
    depth = pieces[0].shape[1]
    me = lax.axis_index("ctx")
    sources = chan_sources()
    for k in range(n_out):
        cols = rows_at((me + k) % n_out, width)
        key = value = None
        for j, piece in enumerate(pieces):
            x = piece[starts[j] : starts[j] + tokens, :]
            rows = rows_at(sources[j], depth)
            a = jnp.dot(x, w_ref[0, rows, cols], preferred_element_type=F32)
            b = jnp.dot(x, w_ref[1, rows, cols], preferred_element_type=F32)
            key = a if key is None else key + a
            value = b if value is None else value + b
        outs[k][...] = (key * value).astype(BF16)


def mixed_inputs(pieces, starts, tokens, w, n_ctx):
    total, width = w.shape[1], w.shape[2] // n_ctx
    return call(
        functools.partial(kv_kernel, len(pieces), n_ctx, starts),
        [jax.ShapeDtypeStruct((tokens, width), BF16)] * n_ctx,
        [w, *pieces],
        6,
        4 * tokens * total * width * n_ctx,
        4 * total * width * n_ctx + 2 * tokens * total,
    )


def query_kernel(n_pieces, n_ctx, starts, w_ref, *refs):
    pieces, out_ref = refs[:n_pieces], refs[-1]
    depth = pieces[0].shape[1]
    tokens = out_ref.shape[0]
    width = out_ref.shape[1] // n_ctx
    me = lax.axis_index("ctx")
    sources = chan_sources()
    for k in range(n_ctx):
        cols = rows_at((me + k) % n_ctx, width)
        acc = None
        for j, piece in enumerate(pieces):
            x = piece[starts[j] : starts[j] + tokens, :]
            a = jnp.dot(x, w_ref[rows_at(sources[j], depth), cols], preferred_element_type=F32)
            acc = a if acc is None else acc + a
        out_ref[:, k * width : (k + 1) * width] = acc.astype(BF16)


def queries(pieces, starts, tokens, w, n_ctx):
    total, channels = w.shape
    return call(
        functools.partial(query_kernel, len(pieces), n_ctx, starts),
        jax.ShapeDtypeStruct((tokens, channels), BF16),
        [w, *pieces],
        6,
        2 * tokens * total * channels,
        2 * total * channels + 2 * tokens * total,
    )


def block_products(g_ref, x_ref, y_ref, wanted, width, block):
    def tile(i, first):
        upper = pl.ds(i * 8, 8) if first else rows_at(i, 8)
        lower = pl.ds(block + i * 8, 8) if first else rows_at(block // 8 + i, 8)
        for lane in range(width // LANES):
            cols = pl.ds(lane * LANES, LANES)
            last = max(wanted) + 1
            g_re = [g_ref[b, upper, cols] for b in range(last)]
            g_im = [g_ref[b, lower, cols] for b in range(last)]
            x_re = [x_ref[b, upper, cols] for b in range(last)]
            x_im = [x_ref[b, lower, cols] for b in range(last)]
            g_di = g_re
            if first:
                edge = lax.broadcasted_iota(jnp.int32, (8, LANES), 0) == 0
                g_di = [jnp.where(edge, im, re) for re, im in zip(g_re, g_im)]
                g_im = [jnp.where(edge, 0.0, im) for im in g_im]
            for b in wanted:
                re = g_re[b] * x_re[0] - g_im[b] * x_im[0]
                im = g_di[b] * x_im[0] + g_im[b] * x_re[0]
                for a in range(1, b + 1):
                    re = re + (g_re[b - a] * x_re[a] - g_im[b - a] * x_im[a])
                    im = im + (g_di[b - a] * x_im[a] + g_im[b - a] * x_re[a])
                y_ref[b, upper, cols] = re
                y_ref[b, lower, cols] = im

    tile(0, True)
    pl.loop(1, block // 8)(lambda i: tile(i, False))


def conv_kernel(n_ctx, chunks, fwd_ref, inv_ref, g_ref, *refs):
    n_in = n_ctx * chunks
    ins, outs = refs[:n_in], refs[n_in : 2 * n_in]
    x_ref, y_ref = refs[2 * n_in :]
    me = lax.axis_index("ctx")
    blocks, rows, width = g_ref.shape
    block = rows // 2
    tokens = ins[0].shape[0]
    parts = block // tokens
    per_dev = blocks // n_ctx
    for k in range(n_ctx):
        source = (me - k + n_ctx) % n_ctx
        for b in range(per_dev):
            total = None
            for p in range(parts):
                piece = ins[(b * parts + p) * n_ctx + k][...]
                a = jnp.dot(fwd_ref[:, p * tokens : (p + 1) * tokens], piece, preferred_element_type=F32)
                total = a if total is None else total + a
            x_ref[source * per_dev + b] = total

    block_products(g_ref, x_ref, y_ref, range(blocks), width, block)

    for c in range(chunks):
        for k in range(n_ctx):
            target = (me + k) % n_ctx
            spectrum = y_ref[target * per_dev + c // parts].astype(BF16)
            rows_out = slice(c % parts * tokens, (c % parts + 1) * tokens)
            outs[c * n_ctx + k][...] = jnp.dot(
                inv_ref[rows_out, :], spectrum, preferred_element_type=F32
            ).astype(BF16)


def convolve(forward, inverse, spectra, mixed, n_ctx):
    chunks = len(mixed)
    blocks, rows, width = spectra.shape
    n_in = n_ctx * chunks
    outs = call(
        functools.partial(conv_kernel, n_ctx, chunks),
        [jax.ShapeDtypeStruct(mixed[0][0].shape, BF16)] * n_in,
        [forward, inverse, spectra, *[m for group in mixed for m in group]],
        14,
        2 * blocks * rows * rows * width,
        blocks * rows * width * 8,
        [pltpu.VMEM((blocks, rows, width), F32)] * 2,
    )
    return [outs[c * n_ctx : (c + 1) * n_ctx] for c in range(chunks)]


def gate_kernel(n_ctx, skip_ref, q_ref, *refs):
    mixed, conv, out_ref = refs[:n_ctx], refs[n_ctx : 2 * n_ctx], refs[-1]
    _, width = mixed[0].shape
    me = lax.axis_index("ctx")
    for m in range(n_ctx):
        cols = slice(m * width, (m + 1) * width)
        skip = skip_ref[pl.ds((me + m) % n_ctx, 1), :]
        query = q_ref[:, cols].astype(F32)
        total = conv[(-m) % n_ctx][...].astype(F32) + skip * mixed[m][...].astype(F32)
        out_ref[:, cols] = (query * total).astype(BF16)


def gate(skip, query, mixed, conv, n_ctx):
    shape = (mixed[0].shape[0], query.shape[1])
    return call(
        functools.partial(gate_kernel, n_ctx),
        jax.ShapeDtypeStruct(shape, BF16),
        [skip, query, *mixed, *conv],
        4,
        3 * shape[0] * shape[1],
        8 * shape[0] * shape[1],
    )


def out_kernel(n_pieces, n_ctx, columns, w_ref, *refs):
    pieces, out_ref = refs[:n_pieces], refs[-1]
    width = pieces[0].shape[1] // n_ctx
    cols = rows_at(pl.program_id(0), columns)
    me = lax.axis_index("ctx")
    acc = None
    for j, source in enumerate(chan_sources()):
        for m in range(n_ctx):
            w = w_ref[rows_at(source * n_ctx + (me + m) % n_ctx, width), cols]
            a = jnp.dot(pieces[j][:, m * width : (m + 1) * width], w, preferred_element_type=F32)
            acc = a if acc is None else acc + a
    out_ref[...] = acc.astype(BF16)


def project_out(pieces, w, chunk, rows, before, n_ctx, columns=256):
    tokens = pieces[0].shape[0]
    total, out_width = w.shape
    operands = [w, *pieces]
    specs = [VMEM] * len(operands)
    aliases = {}
    if before is not None:
        specs.append(pl.BlockSpec(memory_space=pl.ANY))
        aliases = {len(operands): 0}
        operands.append(before)
    return pl.pallas_call(
        functools.partial(out_kernel, len(pieces), n_ctx, columns),
        out_shape=jax.ShapeDtypeStruct((rows, out_width), BF16),
        grid=(out_width // columns,),
        in_specs=specs,
        out_specs=pl.BlockSpec((tokens, columns), lambda i: (chunk, i)),
        input_output_aliases=aliases,
        compiler_params=pltpu.CompilerParams(vmem_limit_bytes=6 * MIB),
        cost_estimate=pl.CostEstimate(
            flops=2 * tokens * total * out_width,
            bytes_accessed=2 * total * out_width + 2 * tokens * (total + out_width),
            transcendentals=0,
        ),
        name="out_projection",
    )(*operands)


def shift(x, axis, by):
    n = lax.axis_size(axis)
    return lax.ppermute(x, axis, [(i, (i + by) % n) for i in range(n)])


def swap_cores(x):
    n = lax.axis_size("chan")
    return lax.ppermute(x, "chan", [(i, i ^ 1) for i in range(n)])


def gather_far(x):
    pieces = []
    for hop in range(1, lax.axis_size("chan") // 2):
        far = shift(x, "chan", 2 * hop)
        pieces += [far, swap_cores(far)]
    return pieces


def exchange(parts):
    out = [parts[0]]
    for k in range(1, len(parts)):
        out.append(shift(parts[k], "ctx", k))
    return out


def layer(features, filter_taps, skip_gain, in_weight, out_weight):
    return layer_body(features, filter_taps, skip_gain, in_weight, out_weight)


def layer_body(features, filter_taps, skip_gain, in_weight, out_weight):
    n_ctx = lax.axis_size("ctx")
    rows, channels = features.shape[0], in_weight.shape[2]
    width = channels // n_ctx
    tokens = rows // CHUNKS
    forward, inverse = (jnp.asarray(t) for t in real_dft_tables(BLOCK))
    skip = skip_gain.reshape(n_ctx, width)

    far = [gather_far(features[:tokens])]
    near = swap_cores(features)
    later, skip = lax.optimization_barrier((features, skip))
    for c in range(1, CHUNKS):
        far.append(gather_far(later[c * tokens : (c + 1) * tokens]))
    w_kv, w_q, spectra, skip = prologue(forward, skip, filter_taps, in_weight.transpose(1, 0, 2), width)

    mixed, arrived, query = [], [], []
    for c in range(CHUNKS):
        pieces = [features, near, *far[c]]
        starts = [c * tokens] * 2 + [0] * len(far[c])
        mixed.append(mixed_inputs(pieces, starts, tokens, w_kv, n_ctx))
        arrived.append(exchange(mixed[c]))
        query.append(queries(pieces, starts, tokens, w_q, n_ctx))
    conv = convolve(forward, inverse, spectra, arrived, n_ctx)

    out = None
    for c in range(CHUNKS):
        back = exchange(conv[c])
        gated = gate(skip, query[c], mixed[c], back, n_ctx)
        beside = swap_cores(gated)
        pieces = [gated, beside, *gather_far(gated)]
        out = project_out(pieces, out_weight, c, rows, out, n_ctx)
    return out


P_SIZE = 128


def dft_tables(block_len):
    period = 2 * block_len
    freq_col = jnp.arange(period, dtype=jnp.int32)[:, None]
    place_row = jnp.arange(period, dtype=jnp.int32)[None, :]
    angles = (freq_col * place_row % period).astype(F32) * (2.0 * math.pi / period)
    forward = jnp.concatenate([jnp.cos(angles), -jnp.sin(angles)], axis=0).astype(BF16)
    out_place = jnp.arange(block_len, dtype=jnp.int32)[:, None] + block_len
    angle_out = (out_place * place_row % period).astype(F32) * (2.0 * math.pi / period)
    inverse = (jnp.concatenate([jnp.cos(angle_out), -jnp.sin(angle_out)], axis=1) / period).astype(BF16)
    return (forward, inverse)


def plain_layer(features, filter_taps, skip_gain, in_weight, out_weight):
    forward, inverse = dft_tables(P_SIZE)
    channels = in_weight.shape[2]
    tok_rows = features.shape[0]
    per_dev = tok_rows // P_SIZE
    period = 2 * P_SIZE
    total_blocks = per_dev * lax.axis_size("ctx")
    first_mine = lax.axis_index("ctx") * per_dev
    padded = jnp.concatenate([jnp.zeros((P_SIZE, channels), BF16), filter_taps], axis=0)
    tap_blocks = padded.reshape(total_blocks + 1, P_SIZE, channels)
    segments = jnp.concatenate([tap_blocks[:-1], tap_blocks[1:]], axis=1)
    lag = jnp.einsum("fn,knc->kfc", forward, segments, preferred_element_type=F32).astype(BF16)
    flipped = jnp.concatenate([lag[::-1], jnp.zeros_like(lag)], axis=0)
    gathered = lax.all_gather(features, "chan", axis=1, tiled=True)
    w = in_weight.transpose(1, 0, 2)
    q, k, v = (jnp.dot(gathered, w[s], preferred_element_type=F32) for s in range(3))
    query = q.astype(BF16)
    mixed = (k * v).astype(BF16)
    everyone = lax.all_gather(mixed, "ctx", axis=0, tiled=True).reshape(total_blocks, P_SIZE, channels)
    source = jnp.einsum("fp,bpc->bfc", forward[:, :P_SIZE], everyone, preferred_element_type=F32)
    source = source.astype(BF16).astype(F32)
    source_re, source_im = source[:, :period], source[:, period:]
    outputs = []
    for out_block in range(per_dev):
        start = total_blocks - 1 - (first_mine + out_block)
        window = lax.dynamic_slice_in_dim(flipped, start, total_blocks, 0).astype(F32)
        lag_re, lag_im = window[:, :period], window[:, period:]
        out_re = jnp.sum(lag_re * source_re - lag_im * source_im, axis=0)
        out_im = jnp.sum(lag_re * source_im + lag_im * source_re, axis=0)
        outputs.append(jnp.concatenate([out_re, out_im], axis=0))
    spectra = jnp.stack(outputs).astype(BF16)
    conv = jnp.einsum("tf,bfc->btc", inverse, spectra, preferred_element_type=F32)
    conv = conv.reshape(tok_rows, channels)
    gated = (query.astype(F32) * (conv + skip_gain[None, :] * mixed.astype(F32))).astype(BF16)
    everything = lax.all_gather(gated, "chan", axis=1, tiled=True)
    return jnp.dot(everything, out_weight, preferred_element_type=F32).astype(BF16)


def shards(features, filter_taps, skip_gain, in_weight, out_weight):
    slices = in_weight.shape[2] % (lax.axis_size("ctx") * LANES) == 0
    paired = lax.axis_size("chan") % 2 == 0
    blocks = features.shape[0] % BLOCK == 0 and BLOCK % (features.shape[0] // CHUNKS) == 0
    chosen = layer if slices and paired and blocks else plain_layer
    return chosen(features, filter_taps, skip_gain, in_weight, out_weight)


def solution(mesh):
    return jax.shard_map(
        shards,
        mesh=mesh,
        in_specs=(
            P(("grp", "ctx"), "chan"),
            P(None, "chan"),
            P("chan"),
            P(None, None, "chan"),
            P(None, "chan"),
        ),
        out_specs=P(("grp", "ctx"), "chan"),
        check_vma=False,
    )
```

```python
import functools
import math

import jax
import jax.numpy as jnp
import ml_dtypes
import numpy as np
from jax import lax
from jax.experimental import pallas as pl
from jax.experimental.pallas import tpu as pltpu
from jax.sharding import PartitionSpec as P


BF16 = jnp.bfloat16
F32 = jnp.float32
LANES = 128
MIB = 1 << 20
CHUNKS = 2
VMEM = pl.BlockSpec(memory_space=pltpu.VMEM)
HBM = pl.BlockSpec(memory_space=pltpu.HBM)


def real_dft_tables(block):
    period = 2 * block
    freq = np.arange(block)[:, None]
    place = np.arange(block)[None, :]
    angle = (freq * place % period) * (2.0 * math.pi / period)
    lower = -np.sin(angle)
    lower[0] = 1.0 - 2.0 * (np.arange(block) % 2)
    forward = np.concatenate([np.cos(angle), lower], axis=0)
    out_place = np.arange(block)[:, None] + block
    freq_row = np.arange(block)[None, :]
    angle_out = (out_place * freq_row % period) * (2.0 * math.pi / period)
    weight = np.where(freq_row == 0, 1.0, 2.0)
    lower_out = -np.sin(angle_out) * weight
    lower_out[:, 0] = 1.0 - 2.0 * (np.arange(block) % 2)
    inverse = np.concatenate([np.cos(angle_out) * weight, lower_out], axis=1) / period
    return forward.astype(ml_dtypes.bfloat16), inverse.astype(ml_dtypes.bfloat16)


def call(kernel, out, operands, limit, flops, moved, scratch=()):
    return pl.pallas_call(
        kernel,
        out_shape=out,
        in_specs=[VMEM] * len(operands),
        out_specs=jax.tree.map(lambda _: VMEM, out),
        scratch_shapes=scratch,
        compiler_params=pltpu.CompilerParams(vmem_limit_bytes=limit * MIB),
        cost_estimate=pl.CostEstimate(flops=flops, bytes_accessed=moved, transcendentals=0),
    )(*operands)


def chan_sources():
    n_chan, chan = lax.axis_size("chan"), lax.axis_index("chan")
    sources = [chan, chan ^ 1]
    for hop in range(1, n_chan // 2):
        far = (chan - 2 * hop + n_chan) % n_chan
        sources += [far, far ^ 1]
    return sources


def paired(n):
    return n & (n - 1) == 0


def target(me, k, n):
    return me ^ k if paired(n) else (me + k) % n


def origin(me, k, n):
    return me ^ k if paired(n) else (me - k + n) % n


def mirror(k, n):
    return k if paired(n) else -k % n


def rows_at(first, count):
    return pl.ds(pl.multiple_of(first * count, count), count)


def prologue_kernel(
    width, skip_hbm, fwd_hbm, inv_hbm, taps_ref, w_ref, fwd_ref, inv_ref, kv_ref, query_ref, out_ref, skip_out, skip_ref, taps_in, prev_ref, sems
):
    block = inv_ref.shape[0]
    cols = rows_at(lax.axis_index("ctx"), width)
    copies = [
        pltpu.make_async_copy(skip_hbm, skip_ref, sems.at[5]),
        pltpu.make_async_copy(fwd_hbm, fwd_ref, sems.at[0]),
        pltpu.make_async_copy(taps_ref.at[:, cols], taps_in, sems.at[1]),
        pltpu.make_async_copy(inv_hbm, inv_ref, sems.at[2]),
        pltpu.make_async_copy(w_ref.at[1:3], kv_ref, sems.at[3]),
        pltpu.make_async_copy(w_ref.at[0], query_ref, sems.at[4]),
    ]
    for copy in copies:
        copy.start()
    prev_ref[...] = jnp.zeros_like(prev_ref)
    for copy in copies[:3]:
        copy.wait()
    for k in range(skip_out.shape[0]):
        skip_out[k, :] = skip_ref[k * width : (k + 1) * width]

    @pl.loop(0, out_ref.shape[0])
    def _(k):
        now = jnp.dot(fwd_ref[...], taps_in[rows_at(k, block), :], preferred_element_type=F32)
        parity = lax.broadcasted_iota(jnp.int32, now.shape, 0) % 2
        out_ref[k] = prev_ref[...] + jnp.where(parity == 0, now, -now)
        prev_ref[...] = now

    for copy in copies[3:]:
        copy.wait()


def prologue(tables, skip, taps, w, n_ctx):
    rows, block = tables[0].shape
    width = w.shape[2] // n_ctx
    count = taps.shape[0] // block
    out = [
        *(jax.ShapeDtypeStruct(t.shape, BF16) for t in tables),
        jax.ShapeDtypeStruct((2, *w.shape[1:]), BF16),
        jax.ShapeDtypeStruct(w.shape[1:], BF16),
        jax.ShapeDtypeStruct((count, rows, width), F32),
        jax.ShapeDtypeStruct((n_ctx, width), F32),
    ]
    return pl.pallas_call(
        functools.partial(prologue_kernel, width),
        out_shape=out,
        in_specs=[HBM] * 5,
        out_specs=[VMEM] * len(out),
        scratch_shapes=[
            pltpu.VMEM(skip.shape, F32),
            pltpu.VMEM((taps.shape[0], width), BF16),
            pltpu.VMEM((rows, width), F32),
            pltpu.SemaphoreType.DMA((6,)),
        ],
        compiler_params=pltpu.CompilerParams(vmem_limit_bytes=6 * MIB),
        cost_estimate=pl.CostEstimate(
            flops=2 * count * rows * block * width,
            bytes_accessed=2 * w.size + count * width * (rows * 4 + block * 2),
            transcendentals=0,
        ),
        name="prologue",
    )(*(pltpu.with_memory_space_constraint(x, pltpu.HBM) for x in (skip, *tables, taps, w)))


def kv_kernel(n_pieces, n_out, starts, w_ref, *refs):
    pieces, outs = refs[:n_pieces], refs[n_pieces:]
    tokens, width = outs[0].shape
    depth = pieces[0].shape[1]
    me = lax.axis_index("ctx")
    sources = chan_sources()
    for k in range(n_out):
        cols = rows_at(target(me, k, n_out), width)
        key = value = None
        for j, piece in enumerate(pieces):
            x = piece[starts[j] : starts[j] + tokens, :]
            rows = rows_at(sources[j], depth)
            a = jnp.dot(x, w_ref[0, rows, cols], preferred_element_type=F32)
            b = jnp.dot(x, w_ref[1, rows, cols], preferred_element_type=F32)
            key = a if key is None else key + a
            value = b if value is None else value + b
        outs[k][...] = (key * value).astype(BF16)


def mixed_inputs(pieces, starts, tokens, w, n_ctx):
    total, width = w.shape[1], w.shape[2] // n_ctx
    return call(
        functools.partial(kv_kernel, len(pieces), n_ctx, starts),
        [jax.ShapeDtypeStruct((tokens, width), BF16)] * n_ctx,
        [w, *pieces],
        6,
        4 * tokens * total * width * n_ctx,
        4 * total * width * n_ctx + 2 * tokens * total,
    )


def query_kernel(n_pieces, n_ctx, starts, w_ref, *refs):
    pieces, out_ref = refs[:n_pieces], refs[-1]
    depth = pieces[0].shape[1]
    tokens = out_ref.shape[0]
    width = out_ref.shape[1] // n_ctx
    me = lax.axis_index("ctx")
    sources = chan_sources()
    for k in range(n_ctx):
        cols = rows_at(target(me, k, n_ctx), width)
        acc = None
        for j, piece in enumerate(pieces):
            x = piece[starts[j] : starts[j] + tokens, :]
            a = jnp.dot(x, w_ref[rows_at(sources[j], depth), cols], preferred_element_type=F32)
            acc = a if acc is None else acc + a
        out_ref[:, k * width : (k + 1) * width] = acc.astype(BF16)


def queries(pieces, starts, tokens, w, n_ctx):
    total, channels = w.shape
    return call(
        functools.partial(query_kernel, len(pieces), n_ctx, starts),
        jax.ShapeDtypeStruct((tokens, channels), BF16),
        [w, *pieces],
        6,
        2 * tokens * total * channels,
        2 * total * channels + 2 * tokens * total,
    )


def block_products(g_ref, x_ref, before_ref, after_ref, plan, width, block):
    lags = sorted({lag for _, _, terms in plan for lag, _ in terms})
    slots = sorted({slot for _, _, terms in plan for _, slot in terms})

    def tile(i, first):
        upper = pl.ds(i * 8, 8) if first else rows_at(i, 8)
        lower = pl.ds(block + i * 8, 8) if first else rows_at(block // 8 + i, 8)
        for lane in range(width // LANES):
            cols = pl.ds(lane * LANES, LANES)
            g_re = {b: g_ref[b, upper, cols] for b in lags}
            g_im = {b: g_ref[b, lower, cols] for b in lags}
            x_re = {b: x_ref[b, upper, cols] for b in slots}
            x_im = {b: x_ref[b, lower, cols] for b in slots}
            g_di = g_re
            if first:
                edge = lax.broadcasted_iota(jnp.int32, (8, LANES), 0) == 0
                g_di = {b: jnp.where(edge, g_im[b], g_re[b]) for b in lags}
                g_im = {b: jnp.where(edge, 0.0, g_im[b]) for b in lags}
            for start, end, terms in plan:
                re = im = None
                if start is not None:
                    re, im = before_ref[start, upper, cols], before_ref[start, lower, cols]
                for lag, slot in terms:
                    up = g_re[lag] * x_re[slot] - g_im[lag] * x_im[slot]
                    down = g_di[lag] * x_im[slot] + g_im[lag] * x_re[slot]
                    re = up if re is None else re + up
                    im = down if im is None else im + down
                after_ref[end, upper, cols] = re
                after_ref[end, lower, cols] = im

    tile(0, True)
    pl.loop(1, block // 8)(lambda i: tile(i, False))


def forward_dft(n_ctx, fwd_ref, ins, x_ref):
    me = lax.axis_index("ctx")
    for k in range(n_ctx):
        x_ref[origin(me, k, n_ctx)] = jnp.dot(fwd_ref[...], ins[k][...], preferred_element_type=F32)


def inverse_dft(n_ctx, inv_ref, y_ref, outs):
    me = lax.axis_index("ctx")
    for k in range(n_ctx):
        spectrum = y_ref[target(me, k, n_ctx)].astype(BF16)
        outs[k][...] = jnp.dot(inv_ref[...], spectrum, preferred_element_type=F32).astype(BF16)


def early_kernel(n_ctx, fwd_ref, g_ref, *refs):
    ins, sum_ref, x_ref = refs[:n_ctx], refs[n_ctx], refs[n_ctx + 1]
    blocks, rows, width = g_ref.shape
    forward_dft(n_ctx, fwd_ref, ins, x_ref)
    plan = [(None, b, [(b - a, a // 2) for a in range(0, b + 1, 2)]) for b in range(blocks)]
    block_products(g_ref, x_ref, None, sum_ref, plan, width, rows // 2)


def middle_kernel(n_ctx, fwd_ref, inv_ref, g_ref, sum_ref, *refs):
    ins, x_ref, outs, y_ref = refs[:n_ctx], refs[n_ctx], refs[n_ctx + 1 : 2 * n_ctx + 1], refs[-1]
    blocks, rows, width = g_ref.shape
    forward_dft(n_ctx, fwd_ref, ins, x_ref)
    plan = [(b, b // 2, [(b - a, a // 2) for a in range(1, b, 2)]) for b in range(0, blocks, 2)]
    block_products(g_ref, x_ref, sum_ref, y_ref, plan, width, rows // 2)
    inverse_dft(n_ctx, inv_ref, y_ref, outs)


def late_kernel(n_ctx, inv_ref, g_ref, sum_ref, x_ref, *refs):
    outs, y_ref = refs[:n_ctx], refs[-1]
    blocks, rows, width = g_ref.shape
    plan = [(b, b // 2, [(b - a, a // 2) for a in range(1, b + 1, 2)]) for b in range(1, blocks, 2)]
    block_products(g_ref, x_ref, sum_ref, y_ref, plan, width, rows // 2)
    inverse_dft(n_ctx, inv_ref, y_ref, outs)


def convolve(forward, inverse, spectra, arrived, n_ctx):
    blocks, rows, width = spectra.shape
    half = (n_ctx, rows, width)
    piece = jax.ShapeDtypeStruct((rows // 2, width), BF16)
    flops, moved = blocks * rows * rows * width // 2, blocks * rows * width * 8
    sums = call(
        functools.partial(early_kernel, n_ctx),
        jax.ShapeDtypeStruct(spectra.shape, F32),
        [forward, spectra, *arrived[0]],
        6,
        flops,
        moved,
        [pltpu.VMEM(half, F32)],
    )
    x, *even = call(
        functools.partial(middle_kernel, n_ctx),
        [jax.ShapeDtypeStruct(half, F32)] + [piece] * n_ctx,
        [forward, inverse, spectra, sums, *arrived[1]],
        6,
        flops,
        moved,
        [pltpu.VMEM(half, F32)],
    )
    odd = call(
        functools.partial(late_kernel, n_ctx),
        [piece] * n_ctx,
        [inverse, spectra, sums, x],
        6,
        flops,
        moved,
        [pltpu.VMEM(half, F32)],
    )
    return even, odd


def gate_kernel(n_ctx, skip_ref, q_ref, *refs):
    mixed, conv, out_ref = refs[:n_ctx], refs[n_ctx : 2 * n_ctx], refs[-1]
    _, width = mixed[0].shape
    me = lax.axis_index("ctx")
    for m in range(n_ctx):
        cols = slice(m * width, (m + 1) * width)
        skip = skip_ref[pl.ds(target(me, m, n_ctx), 1), :]
        query = q_ref[:, cols].astype(F32)
        total = conv[mirror(m, n_ctx)][...].astype(F32) + skip * mixed[m][...].astype(F32)
        out_ref[:, cols] = (query * total).astype(BF16)


def gate(skip, query, mixed, conv, n_ctx):
    shape = (mixed[0].shape[0], query.shape[1])
    return call(
        functools.partial(gate_kernel, n_ctx),
        jax.ShapeDtypeStruct(shape, BF16),
        [skip, query, *mixed, *conv],
        4,
        3 * shape[0] * shape[1],
        8 * shape[0] * shape[1],
    )


def out_kernel(which, has_before, n_ctx, w_ref, *refs):
    pieces, out_ref = refs[: len(which)], refs[-1]
    columns = out_ref.shape[1]
    width = pieces[0].shape[1] // n_ctx
    cols = rows_at(pl.program_id(0), columns)
    me = lax.axis_index("ctx")
    sources = chan_sources()
    acc = refs[len(which)][:, cols] if has_before else None
    for piece, j in zip(pieces, which):
        for m in range(n_ctx):
            w = w_ref[rows_at(sources[j] * n_ctx + target(me, m, n_ctx), width), cols]
            a = jnp.dot(piece[:, m * width : (m + 1) * width], w, preferred_element_type=F32)
            acc = a if acc is None else acc + a
    out_ref[...] = acc.astype(out_ref.dtype)


def project_out(pieces, which, w, before, n_ctx, final=None, columns=256):
    tokens = pieces[0].shape[0]
    _, out_width = w.shape
    operands = [w, *(pieces[j] for j in which)] + ([] if before is None else [before])
    specs = [VMEM] * len(operands)
    aliases = {}
    out_spec, shape = pl.BlockSpec((tokens, columns), lambda i: (0, i)), (tokens, out_width)
    if final is not None:
        chunk, rows, so_far = final
        out_spec, shape = pl.BlockSpec((tokens, columns), lambda i: (chunk, i)), (rows, out_width)
        if so_far is not None:
            specs.append(pl.BlockSpec(memory_space=pl.ANY))
            aliases = {len(operands): 0}
            operands.append(so_far)
    share = len(which) * pieces[0].shape[1]
    return pl.pallas_call(
        functools.partial(out_kernel, tuple(which), before is not None, n_ctx),
        out_shape=jax.ShapeDtypeStruct(shape, F32 if final is None else BF16),
        grid=(out_width // columns,),
        in_specs=specs,
        out_specs=out_spec,
        input_output_aliases=aliases,
        compiler_params=pltpu.CompilerParams(vmem_limit_bytes=6 * MIB),
        cost_estimate=pl.CostEstimate(
            flops=2 * tokens * share * out_width,
            bytes_accessed=2 * share * out_width + 2 * tokens * (share + out_width),
            transcendentals=0,
        ),
        name="out_projection",
    )(*operands)


def shift(x, axis, by):
    n = lax.axis_size(axis)
    return lax.ppermute(x, axis, [(i, (i + by) % n) for i in range(n)])


def swap_cores(x):
    n = lax.axis_size("chan")
    return lax.ppermute(x, "chan", [(i, i ^ 1) for i in range(n)])


def gather_far(x):
    pieces = []
    for hop in range(1, lax.axis_size("chan") // 2):
        far = shift(x, "chan", 2 * hop)
        pieces += [far, swap_cores(far)]
    return pieces


def exchange(parts):
    out, n = [parts[0]], len(parts)
    for k in range(1, n):
        out.append(lax.ppermute(parts[k], "ctx", [(i, target(i, k, n)) for i in range(n)]))
    return out


def layer(features, filter_taps, skip_gain, in_weight, out_weight):
    return layer_body(features, filter_taps, skip_gain, in_weight, out_weight)


def layer_body(features, filter_taps, skip_gain, in_weight, out_weight):
    n_ctx = lax.axis_size("ctx")
    rows = features.shape[0]
    tokens = rows // CHUNKS
    tables = [jnp.asarray(t) for t in real_dft_tables(tokens)]

    far = [gather_far(features[:tokens])]
    near = swap_cores(features)
    later, skip = lax.optimization_barrier((features, skip_gain))
    far.append(gather_far(later[tokens:]))
    forward, inverse, w_kv, w_q, spectra, skip = prologue(
        tables, skip, filter_taps, in_weight.transpose(1, 0, 2), n_ctx
    )

    mixed, arrived, query = [], [], []
    for c in range(CHUNKS):
        pieces = [features, near, *far[c]]
        starts = [c * tokens] * 2 + [0] * len(far[c])
        mixed.append(mixed_inputs(pieces, starts, tokens, w_kv, n_ctx))
        arrived.append(exchange(mixed[c]))
        query.append(queries(pieces, starts, tokens, w_q, n_ctx))
    conv = convolve(forward, inverse, spectra, arrived, n_ctx)

    gathered = []
    for c in range(CHUNKS):
        back = exchange(conv[c])
        gated = gate(skip, query[c], mixed[c], back, n_ctx)
        beside = swap_cores(gated)
        gathered.append([gated, beside, *gather_far(gated)])
    every = range(len(gathered[0]))
    out = project_out(gathered[0], every, out_weight, None, n_ctx, (0, rows, None))
    part = project_out(gathered[1], every[:2], out_weight, None, n_ctx)
    part = project_out(gathered[1], every[2:-1], out_weight, part, n_ctx)
    return project_out(gathered[1], every[-1:], out_weight, part, n_ctx, (1, rows, out))


P_SIZE = 128


def dft_tables(block_len):
    period = 2 * block_len
    freq_col = jnp.arange(period, dtype=jnp.int32)[:, None]
    place_row = jnp.arange(period, dtype=jnp.int32)[None, :]
    angles = (freq_col * place_row % period).astype(F32) * (2.0 * math.pi / period)
    forward = jnp.concatenate([jnp.cos(angles), -jnp.sin(angles)], axis=0).astype(BF16)
    out_place = jnp.arange(block_len, dtype=jnp.int32)[:, None] + block_len
    angle_out = (out_place * place_row % period).astype(F32) * (2.0 * math.pi / period)
    inverse = (jnp.concatenate([jnp.cos(angle_out), -jnp.sin(angle_out)], axis=1) / period).astype(BF16)
    return (forward, inverse)


def plain_layer(features, filter_taps, skip_gain, in_weight, out_weight):
    forward, inverse = dft_tables(P_SIZE)
    channels = in_weight.shape[2]
    tok_rows = features.shape[0]
    per_dev = tok_rows // P_SIZE
    period = 2 * P_SIZE
    total_blocks = per_dev * lax.axis_size("ctx")
    first_mine = lax.axis_index("ctx") * per_dev
    padded = jnp.concatenate([jnp.zeros((P_SIZE, channels), BF16), filter_taps], axis=0)
    tap_blocks = padded.reshape(total_blocks + 1, P_SIZE, channels)
    segments = jnp.concatenate([tap_blocks[:-1], tap_blocks[1:]], axis=1)
    lag = jnp.einsum("fn,knc->kfc", forward, segments, preferred_element_type=F32).astype(BF16)
    flipped = jnp.concatenate([lag[::-1], jnp.zeros_like(lag)], axis=0)
    gathered = lax.all_gather(features, "chan", axis=1, tiled=True)
    w = in_weight.transpose(1, 0, 2)
    q, k, v = (jnp.dot(gathered, w[s], preferred_element_type=F32) for s in range(3))
    query = q.astype(BF16)
    mixed = (k * v).astype(BF16)
    everyone = lax.all_gather(mixed, "ctx", axis=0, tiled=True).reshape(total_blocks, P_SIZE, channels)
    source = jnp.einsum("fp,bpc->bfc", forward[:, :P_SIZE], everyone, preferred_element_type=F32)
    source = source.astype(BF16).astype(F32)
    source_re, source_im = source[:, :period], source[:, period:]
    outputs = []
    for out_block in range(per_dev):
        start = total_blocks - 1 - (first_mine + out_block)
        window = lax.dynamic_slice_in_dim(flipped, start, total_blocks, 0).astype(F32)
        lag_re, lag_im = window[:, :period], window[:, period:]
        out_re = jnp.sum(lag_re * source_re - lag_im * source_im, axis=0)
        out_im = jnp.sum(lag_re * source_im + lag_im * source_re, axis=0)
        outputs.append(jnp.concatenate([out_re, out_im], axis=0))
    spectra = jnp.stack(outputs).astype(BF16)
    conv = jnp.einsum("tf,bfc->btc", inverse, spectra, preferred_element_type=F32)
    conv = conv.reshape(tok_rows, channels)
    gated = (query.astype(F32) * (conv + skip_gain[None, :] * mixed.astype(F32))).astype(BF16)
    everything = lax.all_gather(gated, "chan", axis=1, tiled=True)
    return jnp.dot(everything, out_weight, preferred_element_type=F32).astype(BF16)


def shards(features, filter_taps, skip_gain, in_weight, out_weight):
    slices = in_weight.shape[2] % (lax.axis_size("ctx") * LANES) == 0
    cores = lax.axis_size("chan") % 2 == 0 and lax.axis_size("chan") > 2
    blocks = features.shape[0] % (CHUNKS * LANES) == 0
    chosen = layer if slices and cores and blocks else plain_layer
    return chosen(features, filter_taps, skip_gain, in_weight, out_weight)


def solution(mesh):
    return jax.shard_map(
        shards,
        mesh=mesh,
        in_specs=(
            P(("grp", "ctx"), "chan"),
            P(None, "chan"),
            P("chan"),
            P(None, None, "chan"),
            P(None, "chan"),
        ),
        out_specs=P(("grp", "ctx"), "chan"),
        check_vma=False,
    )
```

```python
import functools
import math

import jax
import jax.numpy as jnp
import ml_dtypes
import numpy as np
from jax import lax
from jax.experimental import pallas as pl
from jax.experimental.pallas import tpu as pltpu
from jax.sharding import PartitionSpec as P


BF16 = jnp.bfloat16
F32 = jnp.float32
LANES = 128
MIB = 1 << 20
CHUNKS = 2
VMEM = pl.BlockSpec(memory_space=pltpu.VMEM)
HBM = pl.BlockSpec(memory_space=pltpu.HBM)


def real_dft_tables(block):
    period = 2 * block
    freq = np.arange(block)[:, None]
    place = np.arange(block)[None, :]
    angle = (freq * place % period) * (2.0 * math.pi / period)
    lower = -np.sin(angle)
    lower[0] = 1.0 - 2.0 * (np.arange(block) % 2)
    forward = np.concatenate([np.cos(angle), lower], axis=0)
    out_place = np.arange(block)[:, None] + block
    freq_row = np.arange(block)[None, :]
    angle_out = (out_place * freq_row % period) * (2.0 * math.pi / period)
    weight = np.where(freq_row == 0, 1.0, 2.0)
    lower_out = -np.sin(angle_out) * weight
    lower_out[:, 0] = 1.0 - 2.0 * (np.arange(block) % 2)
    inverse = np.concatenate([np.cos(angle_out) * weight, lower_out], axis=1) / period
    return forward.astype(ml_dtypes.bfloat16), inverse.astype(ml_dtypes.bfloat16)


def call(kernel, out, operands, limit, flops, moved, scratch=()):
    return pl.pallas_call(
        kernel,
        out_shape=out,
        in_specs=[VMEM] * len(operands),
        out_specs=jax.tree.map(lambda _: VMEM, out),
        scratch_shapes=scratch,
        compiler_params=pltpu.CompilerParams(vmem_limit_bytes=limit * MIB),
        cost_estimate=pl.CostEstimate(flops=flops, bytes_accessed=moved, transcendentals=0),
    )(*operands)


def chan_sources():
    n_chan, chan = lax.axis_size("chan"), lax.axis_index("chan")
    sources = [chan, chan ^ 1]
    for hop in range(1, n_chan // 2):
        far = (chan - 2 * hop + n_chan) % n_chan
        sources += [far, far ^ 1]
    return sources


def paired(n):
    return n & (n - 1) == 0


def target(me, k, n):
    return me ^ k if paired(n) else (me + k) % n


def origin(me, k, n):
    return me ^ k if paired(n) else (me - k + n) % n


def mirror(k, n):
    return k if paired(n) else -k % n


def rows_at(first, count):
    return pl.ds(pl.multiple_of(first * count, count), count)


def prologue_kernel(
    width, skip_hbm, fwd_hbm, inv_hbm, taps_ref, w_ref, fwd_ref, inv_ref, kv_ref, query_ref, out_ref, skip_out, skip_ref, taps_in, prev_ref, sems
):
    block = inv_ref.shape[0]
    cols = rows_at(lax.axis_index("ctx"), width)
    copies = [
        pltpu.make_async_copy(skip_hbm, skip_ref, sems.at[5]),
        pltpu.make_async_copy(fwd_hbm, fwd_ref, sems.at[0]),
        pltpu.make_async_copy(taps_ref.at[:, cols], taps_in, sems.at[1]),
        pltpu.make_async_copy(inv_hbm, inv_ref, sems.at[2]),
        pltpu.make_async_copy(w_ref.at[1:3], kv_ref, sems.at[3]),
        pltpu.make_async_copy(w_ref.at[0], query_ref, sems.at[4]),
    ]
    for copy in copies:
        copy.start()
    prev_ref[...] = jnp.zeros_like(prev_ref)
    for copy in copies[:3]:
        copy.wait()
    for k in range(skip_out.shape[0]):
        skip_out[k, :] = skip_ref[k * width : (k + 1) * width]

    @pl.loop(0, out_ref.shape[0])
    def _(k):
        now = jnp.dot(fwd_ref[...], taps_in[rows_at(k, block), :], preferred_element_type=F32)
        parity = lax.broadcasted_iota(jnp.int32, now.shape, 0) % 2
        out_ref[k] = prev_ref[...] + jnp.where(parity == 0, now, -now)
        prev_ref[...] = now

    for copy in copies[3:]:
        copy.wait()


def prologue(tables, skip, taps, w, n_ctx):
    rows, block = tables[0].shape
    width = w.shape[2] // n_ctx
    count = taps.shape[0] // block
    out = [
        *(jax.ShapeDtypeStruct(t.shape, BF16) for t in tables),
        jax.ShapeDtypeStruct((2, *w.shape[1:]), BF16),
        jax.ShapeDtypeStruct(w.shape[1:], BF16),
        jax.ShapeDtypeStruct((count, rows, width), F32),
        jax.ShapeDtypeStruct((n_ctx, width), F32),
    ]
    return pl.pallas_call(
        functools.partial(prologue_kernel, width),
        out_shape=out,
        in_specs=[HBM] * 5,
        out_specs=[VMEM] * len(out),
        scratch_shapes=[
            pltpu.VMEM(skip.shape, F32),
            pltpu.VMEM((taps.shape[0], width), BF16),
            pltpu.VMEM((rows, width), F32),
            pltpu.SemaphoreType.DMA((6,)),
        ],
        compiler_params=pltpu.CompilerParams(vmem_limit_bytes=6 * MIB),
        cost_estimate=pl.CostEstimate(
            flops=2 * count * rows * block * width,
            bytes_accessed=2 * w.size + count * width * (rows * 4 + block * 2),
            transcendentals=0,
        ),
        name="prologue",
    )(*(pltpu.with_memory_space_constraint(x, pltpu.HBM) for x in (skip, *tables, taps, w)))


def kv_kernel(which, starts, n_ctx, has_before, last, w_ref, *refs):
    pieces, refs = refs[: len(which)], refs[len(which) :]
    before, outs = (refs[:2], refs[2:]) if has_before else ((), refs)
    tokens = outs[0].shape[0]
    width = w_ref.shape[2] // n_ctx
    depth = pieces[0].shape[1]
    me = lax.axis_index("ctx")
    sources = chan_sources()
    for k in range(n_ctx):
        cols = rows_at(target(me, k, n_ctx), width)
        mine = slice(k * width, (k + 1) * width)
        key, value = (ref[:, mine] for ref in before) if has_before else (None, None)
        for piece, j, start in zip(pieces, which, starts):
            x = piece[start : start + tokens, :]
            rows = rows_at(sources[j], depth)
            a = jnp.dot(x, w_ref[0, rows, cols], preferred_element_type=F32)
            b = jnp.dot(x, w_ref[1, rows, cols], preferred_element_type=F32)
            key = a if key is None else key + a
            value = b if value is None else value + b
        if last:
            outs[k][...] = (key * value).astype(BF16)
        else:
            outs[0][:, mine] = key
            outs[1][:, mine] = value


def keys_values(pieces, which, starts, tokens, w, before, n_ctx, last):
    channels = w.shape[2]
    share = len(which) * pieces[0].shape[1]
    if last:
        out = [jax.ShapeDtypeStruct((tokens, channels // n_ctx), BF16)] * n_ctx
    else:
        out = [jax.ShapeDtypeStruct((tokens, channels), F32)] * 2
    return call(
        functools.partial(kv_kernel, tuple(which), tuple(starts), n_ctx, bool(before), last),
        out,
        [w, *(pieces[j] for j in which), *before],
        6,
        4 * tokens * share * channels,
        4 * share * channels + 2 * tokens * share,
    )


def query_kernel(n_pieces, n_ctx, starts, w_ref, *refs):
    pieces, out_ref = refs[:n_pieces], refs[-1]
    depth = pieces[0].shape[1]
    tokens = out_ref.shape[0]
    width = out_ref.shape[1] // n_ctx
    me = lax.axis_index("ctx")
    sources = chan_sources()
    for k in range(n_ctx):
        cols = rows_at(target(me, k, n_ctx), width)
        acc = None
        for j, piece in enumerate(pieces):
            x = piece[starts[j] : starts[j] + tokens, :]
            a = jnp.dot(x, w_ref[rows_at(sources[j], depth), cols], preferred_element_type=F32)
            acc = a if acc is None else acc + a
        out_ref[:, k * width : (k + 1) * width] = acc.astype(BF16)


def queries(pieces, starts, tokens, w, n_ctx):
    total, channels = w.shape
    return call(
        functools.partial(query_kernel, len(pieces), n_ctx, starts),
        jax.ShapeDtypeStruct((tokens, channels), BF16),
        [w, *pieces],
        6,
        2 * tokens * total * channels,
        2 * total * channels + 2 * tokens * total,
    )


def block_products(g_ref, x_ref, before_ref, after_ref, plan, width, block):
    lags = sorted({lag for _, _, terms in plan for lag, _ in terms})
    slots = sorted({slot for _, _, terms in plan for _, slot in terms})

    def tile(i, first):
        upper = pl.ds(i * 8, 8) if first else rows_at(i, 8)
        lower = pl.ds(block + i * 8, 8) if first else rows_at(block // 8 + i, 8)
        for lane in range(width // LANES):
            cols = pl.ds(lane * LANES, LANES)
            g_re = {b: g_ref[b, upper, cols] for b in lags}
            g_im = {b: g_ref[b, lower, cols] for b in lags}
            x_re = {b: x_ref[b, upper, cols] for b in slots}
            x_im = {b: x_ref[b, lower, cols] for b in slots}
            g_di = g_re
            if first:
                edge = lax.broadcasted_iota(jnp.int32, (8, LANES), 0) == 0
                g_di = {b: jnp.where(edge, g_im[b], g_re[b]) for b in lags}
                g_im = {b: jnp.where(edge, 0.0, g_im[b]) for b in lags}
            for start, end, terms in plan:
                re = im = None
                if start is not None:
                    re, im = before_ref[start, upper, cols], before_ref[start, lower, cols]
                for lag, slot in terms:
                    up = g_re[lag] * x_re[slot] - g_im[lag] * x_im[slot]
                    down = g_di[lag] * x_im[slot] + g_im[lag] * x_re[slot]
                    re = up if re is None else re + up
                    im = down if im is None else im + down
                after_ref[end, upper, cols] = re
                after_ref[end, lower, cols] = im

    tile(0, True)
    pl.loop(1, block // 8)(lambda i: tile(i, False))


def forward_dft(n_ctx, fwd_ref, ins, x_ref):
    me = lax.axis_index("ctx")
    for k in range(n_ctx):
        x_ref[origin(me, k, n_ctx)] = jnp.dot(fwd_ref[...], ins[k][...], preferred_element_type=F32)


def inverse_dft(n_ctx, inv_ref, y_ref, outs):
    me = lax.axis_index("ctx")
    for k in range(n_ctx):
        spectrum = y_ref[target(me, k, n_ctx)].astype(BF16)
        outs[k][...] = jnp.dot(inv_ref[...], spectrum, preferred_element_type=F32).astype(BF16)


def early_kernel(n_ctx, fwd_ref, g_ref, *refs):
    ins, sum_ref, x_ref = refs[:n_ctx], refs[n_ctx], refs[n_ctx + 1]
    blocks, rows, width = g_ref.shape
    forward_dft(n_ctx, fwd_ref, ins, x_ref)
    plan = [(None, b, [(b - a, a // 2) for a in range(0, b + 1, 2)]) for b in range(blocks)]
    block_products(g_ref, x_ref, None, sum_ref, plan, width, rows // 2)


def middle_kernel(n_ctx, fwd_ref, inv_ref, g_ref, sum_ref, *refs):
    ins, x_ref, outs, y_ref = refs[:n_ctx], refs[n_ctx], refs[n_ctx + 1 : 2 * n_ctx + 1], refs[-1]
    blocks, rows, width = g_ref.shape
    forward_dft(n_ctx, fwd_ref, ins, x_ref)
    plan = [(b, b // 2, [(b - a, a // 2) for a in range(1, b, 2)]) for b in range(0, blocks, 2)]
    block_products(g_ref, x_ref, sum_ref, y_ref, plan, width, rows // 2)
    inverse_dft(n_ctx, inv_ref, y_ref, outs)


def late_kernel(n_ctx, inv_ref, g_ref, sum_ref, x_ref, *refs):
    outs, y_ref = refs[:n_ctx], refs[-1]
    blocks, rows, width = g_ref.shape
    plan = [(b, b // 2, [(b - a, a // 2) for a in range(1, b + 1, 2)]) for b in range(1, blocks, 2)]
    block_products(g_ref, x_ref, sum_ref, y_ref, plan, width, rows // 2)
    inverse_dft(n_ctx, inv_ref, y_ref, outs)


def convolve(forward, inverse, spectra, arrived, n_ctx):
    blocks, rows, width = spectra.shape
    half = (n_ctx, rows, width)
    piece = jax.ShapeDtypeStruct((rows // 2, width), BF16)
    flops, moved = blocks * rows * rows * width // 2, blocks * rows * width * 8
    sums = call(
        functools.partial(early_kernel, n_ctx),
        jax.ShapeDtypeStruct(spectra.shape, F32),
        [forward, spectra, *arrived[0]],
        6,
        flops,
        moved,
        [pltpu.VMEM(half, F32)],
    )
    x, *even = call(
        functools.partial(middle_kernel, n_ctx),
        [jax.ShapeDtypeStruct(half, F32)] + [piece] * n_ctx,
        [forward, inverse, spectra, sums, *arrived[1]],
        6,
        flops,
        moved,
        [pltpu.VMEM(half, F32)],
    )
    odd = call(
        functools.partial(late_kernel, n_ctx),
        [piece] * n_ctx,
        [inverse, spectra, sums, x],
        6,
        flops,
        moved,
        [pltpu.VMEM(half, F32)],
    )
    return even, odd


def gate_kernel(n_ctx, skip_ref, q_ref, *refs):
    mixed, conv, out_ref = refs[:n_ctx], refs[n_ctx : 2 * n_ctx], refs[-1]
    _, width = mixed[0].shape
    me = lax.axis_index("ctx")
    for m in range(n_ctx):
        cols = slice(m * width, (m + 1) * width)
        skip = skip_ref[pl.ds(target(me, m, n_ctx), 1), :]
        query = q_ref[:, cols].astype(F32)
        total = conv[mirror(m, n_ctx)][...].astype(F32) + skip * mixed[m][...].astype(F32)
        out_ref[:, cols] = (query * total).astype(BF16)


def gate(skip, query, mixed, conv, n_ctx):
    shape = (mixed[0].shape[0], query.shape[1])
    return call(
        functools.partial(gate_kernel, n_ctx),
        jax.ShapeDtypeStruct(shape, BF16),
        [skip, query, *mixed, *conv],
        4,
        3 * shape[0] * shape[1],
        8 * shape[0] * shape[1],
    )


def out_kernel(which, has_before, n_ctx, w_ref, *refs):
    pieces, out_ref = refs[: len(which)], refs[-1]
    columns = out_ref.shape[1]
    width = pieces[0].shape[1] // n_ctx
    cols = rows_at(pl.program_id(0), columns)
    me = lax.axis_index("ctx")
    sources = chan_sources()
    acc = refs[len(which)][:, cols] if has_before else None
    for piece, j in zip(pieces, which):
        for m in range(n_ctx):
            w = w_ref[rows_at(sources[j] * n_ctx + target(me, m, n_ctx), width), cols]
            a = jnp.dot(piece[:, m * width : (m + 1) * width], w, preferred_element_type=F32)
            acc = a if acc is None else acc + a
    out_ref[...] = acc.astype(out_ref.dtype)


def project_out(pieces, which, w, before, n_ctx, final=None, columns=256):
    tokens = pieces[0].shape[0]
    _, out_width = w.shape
    operands = [w, *(pieces[j] for j in which)] + ([] if before is None else [before])
    specs = [VMEM] * len(operands)
    aliases = {}
    out_spec, shape = pl.BlockSpec((tokens, columns), lambda i: (0, i)), (tokens, out_width)
    if final is not None:
        chunk, rows, so_far = final
        out_spec, shape = pl.BlockSpec((tokens, columns), lambda i: (chunk, i)), (rows, out_width)
        if so_far is not None:
            specs.append(pl.BlockSpec(memory_space=pl.ANY))
            aliases = {len(operands): 0}
            operands.append(so_far)
    share = len(which) * pieces[0].shape[1]
    return pl.pallas_call(
        functools.partial(out_kernel, tuple(which), before is not None, n_ctx),
        out_shape=jax.ShapeDtypeStruct(shape, F32 if final is None else BF16),
        grid=(out_width // columns,),
        in_specs=specs,
        out_specs=out_spec,
        input_output_aliases=aliases,
        compiler_params=pltpu.CompilerParams(vmem_limit_bytes=6 * MIB),
        cost_estimate=pl.CostEstimate(
            flops=2 * tokens * share * out_width,
            bytes_accessed=2 * share * out_width + 2 * tokens * (share + out_width),
            transcendentals=0,
        ),
        name="out_projection",
    )(*operands)


def shift(x, axis, by):
    n = lax.axis_size(axis)
    return lax.ppermute(x, axis, [(i, (i + by) % n) for i in range(n)])


def swap_cores(x):
    n = lax.axis_size("chan")
    return lax.ppermute(x, "chan", [(i, i ^ 1) for i in range(n)])


def gather_far(x):
    pieces = []
    for hop in range(1, lax.axis_size("chan") // 2):
        far = shift(x, "chan", 2 * hop)
        pieces += [far, swap_cores(far)]
    return pieces


def exchange(parts):
    out, n = [parts[0]], len(parts)
    for k in range(1, n):
        out.append(lax.ppermute(parts[k], "ctx", [(i, target(i, k, n)) for i in range(n)]))
    return out


def layer(features, filter_taps, skip_gain, in_weight, out_weight):
    return layer_body(features, filter_taps, skip_gain, in_weight, out_weight)


def layer_body(features, filter_taps, skip_gain, in_weight, out_weight):
    n_ctx = lax.axis_size("ctx")
    rows = features.shape[0]
    tokens = rows // CHUNKS
    tables = [jnp.asarray(t) for t in real_dft_tables(tokens)]

    far = [gather_far(features[:tokens])]
    near = swap_cores(features)
    later, skip = lax.optimization_barrier((features, skip_gain))
    far.append(gather_far(later[tokens:]))
    forward, inverse, w_kv, w_q, spectra, skip = prologue(
        tables, skip, filter_taps, in_weight.transpose(1, 0, 2), n_ctx
    )

    mixed, arrived, query = [], [], []
    for c in range(CHUNKS):
        pieces = [features, near, *far[c]]
        starts = [c * tokens] * 2 + [0] * len(far[c])
        total = ()
        for part, which in ("a", (0, 1)), ("b", range(2, len(pieces) - 1)), ("c", (len(pieces) - 1,)):
            chosen = [starts[j] for j in which]
            total = keys_values(pieces, which, chosen, tokens, w_kv, total, n_ctx, part == "c")
        mixed.append(total)
        arrived.append(exchange(mixed[c]))
        query.append(queries(pieces, starts, tokens, w_q, n_ctx))
    conv = convolve(forward, inverse, spectra, arrived, n_ctx)

    gathered = []
    for c in range(CHUNKS):
        back = exchange(conv[c])
        gated = gate(skip, query[c], mixed[c], back, n_ctx)
        beside = swap_cores(gated)
        gathered.append([gated, beside, *gather_far(gated)])
    every = range(len(gathered[0]))
    out = project_out(gathered[0], every, out_weight, None, n_ctx, (0, rows, None))
    part = project_out(gathered[1], every[:2], out_weight, None, n_ctx)
    part = project_out(gathered[1], every[2:-1], out_weight, part, n_ctx)
    return project_out(gathered[1], every[-1:], out_weight, part, n_ctx, (1, rows, out))


P_SIZE = 128


def dft_tables(block_len):
    period = 2 * block_len
    freq_col = jnp.arange(period, dtype=jnp.int32)[:, None]
    place_row = jnp.arange(period, dtype=jnp.int32)[None, :]
    angles = (freq_col * place_row % period).astype(F32) * (2.0 * math.pi / period)
    forward = jnp.concatenate([jnp.cos(angles), -jnp.sin(angles)], axis=0).astype(BF16)
    out_place = jnp.arange(block_len, dtype=jnp.int32)[:, None] + block_len
    angle_out = (out_place * place_row % period).astype(F32) * (2.0 * math.pi / period)
    inverse = (jnp.concatenate([jnp.cos(angle_out), -jnp.sin(angle_out)], axis=1) / period).astype(BF16)
    return (forward, inverse)


def plain_layer(features, filter_taps, skip_gain, in_weight, out_weight):
    forward, inverse = dft_tables(P_SIZE)
    channels = in_weight.shape[2]
    tok_rows = features.shape[0]
    per_dev = tok_rows // P_SIZE
    period = 2 * P_SIZE
    total_blocks = per_dev * lax.axis_size("ctx")
    first_mine = lax.axis_index("ctx") * per_dev
    padded = jnp.concatenate([jnp.zeros((P_SIZE, channels), BF16), filter_taps], axis=0)
    tap_blocks = padded.reshape(total_blocks + 1, P_SIZE, channels)
    segments = jnp.concatenate([tap_blocks[:-1], tap_blocks[1:]], axis=1)
    lag = jnp.einsum("fn,knc->kfc", forward, segments, preferred_element_type=F32).astype(BF16)
    flipped = jnp.concatenate([lag[::-1], jnp.zeros_like(lag)], axis=0)
    gathered = lax.all_gather(features, "chan", axis=1, tiled=True)
    w = in_weight.transpose(1, 0, 2)
    q, k, v = (jnp.dot(gathered, w[s], preferred_element_type=F32) for s in range(3))
    query = q.astype(BF16)
    mixed = (k * v).astype(BF16)
    everyone = lax.all_gather(mixed, "ctx", axis=0, tiled=True).reshape(total_blocks, P_SIZE, channels)
    source = jnp.einsum("fp,bpc->bfc", forward[:, :P_SIZE], everyone, preferred_element_type=F32)
    source = source.astype(BF16).astype(F32)
    source_re, source_im = source[:, :period], source[:, period:]
    outputs = []
    for out_block in range(per_dev):
        start = total_blocks - 1 - (first_mine + out_block)
        window = lax.dynamic_slice_in_dim(flipped, start, total_blocks, 0).astype(F32)
        lag_re, lag_im = window[:, :period], window[:, period:]
        out_re = jnp.sum(lag_re * source_re - lag_im * source_im, axis=0)
        out_im = jnp.sum(lag_re * source_im + lag_im * source_re, axis=0)
        outputs.append(jnp.concatenate([out_re, out_im], axis=0))
    spectra = jnp.stack(outputs).astype(BF16)
    conv = jnp.einsum("tf,bfc->btc", inverse, spectra, preferred_element_type=F32)
    conv = conv.reshape(tok_rows, channels)
    gated = (query.astype(F32) * (conv + skip_gain[None, :] * mixed.astype(F32))).astype(BF16)
    everything = lax.all_gather(gated, "chan", axis=1, tiled=True)
    return jnp.dot(everything, out_weight, preferred_element_type=F32).astype(BF16)


def shards(features, filter_taps, skip_gain, in_weight, out_weight):
    slices = in_weight.shape[2] % (lax.axis_size("ctx") * LANES) == 0
    cores = lax.axis_size("chan") % 2 == 0 and lax.axis_size("chan") > 2
    blocks = features.shape[0] % (CHUNKS * LANES) == 0
    chosen = layer if slices and cores and blocks else plain_layer
    return chosen(features, filter_taps, skip_gain, in_weight, out_weight)


def solution(mesh):
    return jax.shard_map(
        shards,
        mesh=mesh,
        in_specs=(
            P(("grp", "ctx"), "chan"),
            P(None, "chan"),
            P("chan"),
            P(None, None, "chan"),
            P(None, "chan"),
        ),
        out_specs=P(("grp", "ctx"), "chan"),
        check_vma=False,
    )
```

```python
import functools
import math

import jax
import jax.numpy as jnp
import ml_dtypes
import numpy as np
from jax import lax
from jax.experimental import pallas as pl
from jax.experimental.pallas import tpu as pltpu
from jax.sharding import PartitionSpec as P


BF16 = jnp.bfloat16
F32 = jnp.float32
LANES = 128
MIB = 1 << 20
CHUNKS = 2
VMEM = pl.BlockSpec(memory_space=pltpu.VMEM)
HBM = pl.BlockSpec(memory_space=pltpu.HBM)


def real_dft_tables(block):
    period = 2 * block
    freq = np.arange(block)[:, None]
    place = np.arange(block)[None, :]
    angle = (freq * place % period) * (2.0 * math.pi / period)
    lower = -np.sin(angle)
    lower[0] = 1.0 - 2.0 * (np.arange(block) % 2)
    forward = np.concatenate([np.cos(angle), lower], axis=0)
    out_place = np.arange(block)[:, None] + block
    freq_row = np.arange(block)[None, :]
    angle_out = (out_place * freq_row % period) * (2.0 * math.pi / period)
    weight = np.where(freq_row == 0, 1.0, 2.0)
    lower_out = -np.sin(angle_out) * weight
    lower_out[:, 0] = 1.0 - 2.0 * (np.arange(block) % 2)
    inverse = np.concatenate([np.cos(angle_out) * weight, lower_out], axis=1) / period
    return forward.astype(ml_dtypes.bfloat16), inverse.astype(ml_dtypes.bfloat16)


def call(kernel, out, operands, limit, flops, moved, scratch=()):
    return pl.pallas_call(
        kernel,
        out_shape=out,
        in_specs=[VMEM] * len(operands),
        out_specs=jax.tree.map(lambda _: VMEM, out),
        scratch_shapes=scratch,
        compiler_params=pltpu.CompilerParams(vmem_limit_bytes=limit * MIB),
        cost_estimate=pl.CostEstimate(flops=flops, bytes_accessed=moved, transcendentals=0),
    )(*operands)


def chan_sources():
    n_chan, chan = lax.axis_size("chan"), lax.axis_index("chan")
    sources = [chan, chan ^ 1]
    for hop in range(1, n_chan // 2):
        far = (chan - 2 * hop + n_chan) % n_chan
        sources += [far, far ^ 1]
    return sources


def paired(n):
    return n & (n - 1) == 0


def target(me, k, n):
    return me ^ k if paired(n) else (me + k) % n


def origin(me, k, n):
    return me ^ k if paired(n) else (me - k + n) % n


def mirror(k, n):
    return k if paired(n) else -k % n


def rows_at(first, count):
    return pl.ds(pl.multiple_of(first * count, count), count)


def prologue_kernel(
    width, skip_hbm, fwd_hbm, inv_hbm, taps_ref, w_ref, fwd_ref, inv_ref, kv_ref, out_ref, skip_out, skip_ref, taps_in, prev_ref, sems
):
    block = inv_ref.shape[0]
    cols = rows_at(lax.axis_index("ctx"), width)
    copies = [
        pltpu.make_async_copy(skip_hbm, skip_ref, sems.at[4]),
        pltpu.make_async_copy(fwd_hbm, fwd_ref, sems.at[0]),
        pltpu.make_async_copy(taps_ref.at[:, cols], taps_in, sems.at[1]),
        pltpu.make_async_copy(inv_hbm, inv_ref, sems.at[2]),
        pltpu.make_async_copy(w_ref.at[1:3], kv_ref, sems.at[3]),
    ]
    for copy in copies:
        copy.start()
    prev_ref[...] = jnp.zeros_like(prev_ref)
    for copy in copies[:3]:
        copy.wait()
    for k in range(skip_out.shape[0]):
        skip_out[k, :] = skip_ref[k * width : (k + 1) * width]

    @pl.loop(0, out_ref.shape[0])
    def _(k):
        now = jnp.dot(fwd_ref[...], taps_in[rows_at(k, block), :], preferred_element_type=F32)
        parity = lax.broadcasted_iota(jnp.int32, now.shape, 0) % 2
        out_ref[k] = prev_ref[...] + jnp.where(parity == 0, now, -now)
        prev_ref[...] = now

    for copy in copies[3:]:
        copy.wait()


def prologue(tables, skip, taps, w, n_ctx):
    rows, block = tables[0].shape
    width = w.shape[2] // n_ctx
    count = taps.shape[0] // block
    out = [
        *(jax.ShapeDtypeStruct(t.shape, BF16) for t in tables),
        jax.ShapeDtypeStruct((2, *w.shape[1:]), BF16),
        jax.ShapeDtypeStruct((count, rows, width), F32),
        jax.ShapeDtypeStruct((n_ctx, width), F32),
    ]
    return pl.pallas_call(
        functools.partial(prologue_kernel, width),
        out_shape=out,
        in_specs=[HBM] * 5,
        out_specs=[VMEM] * len(out),
        scratch_shapes=[
            pltpu.VMEM(skip.shape, F32),
            pltpu.VMEM((taps.shape[0], width), BF16),
            pltpu.VMEM((rows, width), F32),
            pltpu.SemaphoreType.DMA((5,)),
        ],
        compiler_params=pltpu.CompilerParams(vmem_limit_bytes=6 * MIB),
        cost_estimate=pl.CostEstimate(
            flops=2 * count * rows * block * width,
            bytes_accessed=2 * w.size + count * width * (rows * 4 + block * 2),
            transcendentals=0,
        ),
        name="prologue",
    )(*(pltpu.with_memory_space_constraint(x, pltpu.HBM) for x in (skip, *tables, taps, w)))


def kv_kernel(which, starts, n_ctx, has_before, last, w_ref, *refs):
    pieces, refs = refs[: len(which)], refs[len(which) :]
    before, outs = (refs[:2], refs[2:]) if has_before else ((), refs)
    tokens = outs[0].shape[0]
    width = w_ref.shape[2] // n_ctx
    depth = pieces[0].shape[1]
    me = lax.axis_index("ctx")
    sources = chan_sources()
    for k in range(n_ctx):
        cols = rows_at(target(me, k, n_ctx), width)
        mine = slice(k * width, (k + 1) * width)
        key, value = (ref[:, mine] for ref in before) if has_before else (None, None)
        for piece, j, start in zip(pieces, which, starts):
            x = piece[start : start + tokens, :]
            rows = rows_at(sources[j], depth)
            a = jnp.dot(x, w_ref[0, rows, cols], preferred_element_type=F32)
            b = jnp.dot(x, w_ref[1, rows, cols], preferred_element_type=F32)
            key = a if key is None else key + a
            value = b if value is None else value + b
        if last:
            outs[k][...] = (key * value).astype(BF16)
        else:
            outs[0][:, mine] = key
            outs[1][:, mine] = value


def keys_values(pieces, which, starts, tokens, w, before, n_ctx, last):
    channels = w.shape[2]
    share = len(which) * pieces[0].shape[1]
    if last:
        out = [jax.ShapeDtypeStruct((tokens, channels // n_ctx), BF16)] * n_ctx
    else:
        out = [jax.ShapeDtypeStruct((tokens, channels), F32)] * 2
    return call(
        functools.partial(kv_kernel, tuple(which), tuple(starts), n_ctx, bool(before), last),
        out,
        [w, *(pieces[j] for j in which), *before],
        6,
        4 * tokens * share * channels,
        4 * share * channels + 2 * tokens * share,
    )


def query_kernel(starts, n_ctx, load, w_ref, *refs):
    pieces, refs = refs[: len(starts)], refs[len(starts) :]
    out_ref, acc_ref = refs[0], refs[-1]
    tokens = out_ref.shape[0]
    depth = pieces[0].shape[1]
    width = out_ref.shape[1] // n_ctx
    me = lax.axis_index("ctx")
    rows = [rows_at(source, depth) for source in chan_sources()]
    copies = []
    if load:
        kept_ref, sems = refs[1:3]
        copies = [
            pltpu.make_async_copy(w_ref.at[0, r], kept_ref.at[r], sems.at[j]) for j, r in enumerate(rows)
        ]
        w_ref = kept_ref
    for copy in copies:
        copy.start()
    for j, piece in enumerate(pieces):
        if load:
            copies[j].wait()
        for k in range(n_ctx):
            mine = slice(k * width, (k + 1) * width)
            x = piece[starts[j] : starts[j] + tokens, :]
            cols = rows_at(target(me, k, n_ctx), width)
            a = jnp.dot(x, w_ref[rows[j], cols], preferred_element_type=F32)
            if j > 0:
                a = acc_ref[:, mine] + a
            if j < len(pieces) - 1:
                acc_ref[:, mine] = a
            else:
                out_ref[:, mine] = a.astype(BF16)


def queries(pieces, starts, tokens, w, n_ctx, load):
    total, channels = w.shape[-2:]
    out = [jax.ShapeDtypeStruct((tokens, channels), BF16)]
    scratch = [pltpu.VMEM((tokens, channels), F32)]
    if load:
        w = pltpu.with_memory_space_constraint(w, pltpu.HBM)
        out.append(jax.ShapeDtypeStruct((total, channels), BF16))
        scratch.insert(0, pltpu.SemaphoreType.DMA((len(pieces),)))
    return pl.pallas_call(
        functools.partial(query_kernel, tuple(starts), n_ctx, load),
        out_shape=out,
        in_specs=[HBM if load else VMEM] + [VMEM] * len(pieces),
        out_specs=[VMEM] * len(out),
        scratch_shapes=scratch,
        compiler_params=pltpu.CompilerParams(vmem_limit_bytes=6 * MIB),
        cost_estimate=pl.CostEstimate(
            flops=2 * tokens * total * channels,
            bytes_accessed=2 * total * channels + 2 * tokens * total,
            transcendentals=0,
        ),
        name="q_projection",
    )(w, *pieces)


def block_products(g_ref, x_ref, before_ref, after_ref, plan, width, block):
    lags = sorted({lag for _, _, terms in plan for lag, _ in terms})
    slots = sorted({slot for _, _, terms in plan for _, slot in terms})

    def tile(i, first):
        upper = pl.ds(i * 8, 8) if first else rows_at(i, 8)
        lower = pl.ds(block + i * 8, 8) if first else rows_at(block // 8 + i, 8)
        for lane in range(width // LANES):
            cols = pl.ds(lane * LANES, LANES)
            g_re = {b: g_ref[b, upper, cols] for b in lags}
            g_im = {b: g_ref[b, lower, cols] for b in lags}
            x_re = {b: x_ref[b, upper, cols] for b in slots}
            x_im = {b: x_ref[b, lower, cols] for b in slots}
            g_di = g_re
            if first:
                edge = lax.broadcasted_iota(jnp.int32, (8, LANES), 0) == 0
                g_di = {b: jnp.where(edge, g_im[b], g_re[b]) for b in lags}
                g_im = {b: jnp.where(edge, 0.0, g_im[b]) for b in lags}
            for start, end, terms in plan:
                re = im = None
                if start is not None:
                    re, im = before_ref[start, upper, cols], before_ref[start, lower, cols]
                for lag, slot in terms:
                    up = g_re[lag] * x_re[slot] - g_im[lag] * x_im[slot]
                    down = g_di[lag] * x_im[slot] + g_im[lag] * x_re[slot]
                    re = up if re is None else re + up
                    im = down if im is None else im + down
                after_ref[end, upper, cols] = re
                after_ref[end, lower, cols] = im

    tile(0, True)
    pl.loop(1, block // 8)(lambda i: tile(i, False))


def forward_dft(n_ctx, fwd_ref, ins, x_ref):
    me = lax.axis_index("ctx")
    for k in range(n_ctx):
        x_ref[origin(me, k, n_ctx)] = jnp.dot(fwd_ref[...], ins[k][...], preferred_element_type=F32)


def inverse_dft(n_ctx, inv_ref, y_ref, outs):
    me = lax.axis_index("ctx")
    tokens = outs[0].shape[0]
    for p in range(len(outs) // n_ctx):
        for k in range(n_ctx):
            spectrum = y_ref[target(me, k, n_ctx)].astype(BF16)
            part = inv_ref[p * tokens : (p + 1) * tokens, :]
            outs[p * n_ctx + k][...] = jnp.dot(part, spectrum, preferred_element_type=F32).astype(BF16)


def early_kernel(n_ctx, fwd_ref, g_ref, *refs):
    ins, sum_ref, x_ref = refs[:n_ctx], refs[n_ctx], refs[n_ctx + 1]
    blocks, rows, width = g_ref.shape
    forward_dft(n_ctx, fwd_ref, ins, x_ref)
    plan = [(None, b, [(b - a, a // 2) for a in range(0, b + 1, 2)]) for b in range(blocks)]
    block_products(g_ref, x_ref, None, sum_ref, plan, width, rows // 2)


def middle_kernel(n_ctx, fwd_ref, inv_ref, g_ref, sum_ref, *refs):
    ins, x_ref, outs, y_ref = refs[:n_ctx], refs[n_ctx], refs[n_ctx + 1 : 2 * n_ctx + 1], refs[-1]
    blocks, rows, width = g_ref.shape
    forward_dft(n_ctx, fwd_ref, ins, x_ref)
    plan = [(b, b // 2, [(b - a, a // 2) for a in range(1, b, 2)]) for b in range(0, blocks, 2)]
    block_products(g_ref, x_ref, sum_ref, y_ref, plan, width, rows // 2)
    inverse_dft(n_ctx, inv_ref, y_ref, outs)


def late_kernel(n_ctx, inv_ref, g_ref, sum_ref, x_ref, *refs):
    outs, y_ref = refs[:-1], refs[-1]
    blocks, rows, width = g_ref.shape
    plan = [(b, b // 2, [(b - a, a // 2) for a in range(1, b + 1, 2)]) for b in range(1, blocks, 2)]
    block_products(g_ref, x_ref, sum_ref, y_ref, plan, width, rows // 2)
    inverse_dft(n_ctx, inv_ref, y_ref, outs)


def convolve(forward, inverse, spectra, arrived, n_ctx):
    blocks, rows, width = spectra.shape
    half = (n_ctx, rows, width)
    piece = jax.ShapeDtypeStruct((rows // 2, width), BF16)
    flops, moved = blocks * rows * rows * width // 2, blocks * rows * width * 8
    sums = call(
        functools.partial(early_kernel, n_ctx),
        jax.ShapeDtypeStruct(spectra.shape, F32),
        [forward, spectra, *arrived[0]],
        6,
        flops,
        moved,
        [pltpu.VMEM(half, F32)],
    )
    x, *even = call(
        functools.partial(middle_kernel, n_ctx),
        [jax.ShapeDtypeStruct(half, F32)] + [piece] * n_ctx,
        [forward, inverse, spectra, sums, *arrived[1]],
        6,
        flops,
        moved,
        [pltpu.VMEM(half, F32)],
    )
    odd = call(
        functools.partial(late_kernel, n_ctx),
        [jax.ShapeDtypeStruct((rows // 4, width), BF16)] * (2 * n_ctx),
        [inverse, spectra, sums, x],
        6,
        flops,
        moved,
        [pltpu.VMEM(half, F32)],
    )
    return even, odd[:n_ctx], odd[n_ctx:]


def gate_kernel(n_ctx, start, skip_ref, q_ref, *refs):
    mixed, conv, out_ref = refs[:n_ctx], refs[n_ctx : 2 * n_ctx], refs[-1]
    tokens, width = conv[0].shape
    rows = slice(start, start + tokens)
    me = lax.axis_index("ctx")
    for m in range(n_ctx):
        cols = slice(m * width, (m + 1) * width)
        skip = skip_ref[pl.ds(target(me, m, n_ctx), 1), :]
        query = q_ref[rows, cols].astype(F32)
        total = conv[mirror(m, n_ctx)][...].astype(F32) + skip * mixed[m][rows, :].astype(F32)
        out_ref[:, cols] = (query * total).astype(BF16)


def gate(skip, query, mixed, conv, start, n_ctx):
    shape = (conv[0].shape[0], query.shape[1])
    return call(
        functools.partial(gate_kernel, n_ctx, start),
        jax.ShapeDtypeStruct(shape, BF16),
        [skip, query, *mixed, *conv],
        4,
        3 * shape[0] * shape[1],
        8 * shape[0] * shape[1],
    )


def out_kernel(which, has_before, n_ctx, w_ref, *refs):
    pieces, out_ref = refs[: len(which)], refs[-1]
    columns = out_ref.shape[1]
    width = pieces[0].shape[1] // n_ctx
    cols = rows_at(pl.program_id(0), columns)
    me = lax.axis_index("ctx")
    sources = chan_sources()
    acc = refs[len(which)][:, cols] if has_before else None
    for piece, j in zip(pieces, which):
        for m in range(n_ctx):
            w = w_ref[rows_at(sources[j] * n_ctx + target(me, m, n_ctx), width), cols]
            a = jnp.dot(piece[:, m * width : (m + 1) * width], w, preferred_element_type=F32)
            acc = a if acc is None else acc + a
    out_ref[...] = acc.astype(out_ref.dtype)


def project_out(pieces, which, w, before, n_ctx, final=None, columns=256):
    tokens = pieces[0].shape[0]
    _, out_width = w.shape
    operands = [w, *(pieces[j] for j in which)] + ([] if before is None else [before])
    specs = [VMEM] * len(operands)
    aliases = {}
    out_spec, shape = pl.BlockSpec((tokens, columns), lambda i: (0, i)), (tokens, out_width)
    if final is not None:
        chunk, rows, so_far = final
        out_spec, shape = pl.BlockSpec((tokens, columns), lambda i: (chunk, i)), (rows, out_width)
        if so_far is not None:
            specs.append(pl.BlockSpec(memory_space=pl.ANY))
            aliases = {len(operands): 0}
            operands.append(so_far)
    share = len(which) * pieces[0].shape[1]
    return pl.pallas_call(
        functools.partial(out_kernel, tuple(which), before is not None, n_ctx),
        out_shape=jax.ShapeDtypeStruct(shape, F32 if final is None else BF16),
        grid=(out_width // columns,),
        in_specs=specs,
        out_specs=out_spec,
        input_output_aliases=aliases,
        compiler_params=pltpu.CompilerParams(vmem_limit_bytes=6 * MIB),
        cost_estimate=pl.CostEstimate(
            flops=2 * tokens * share * out_width,
            bytes_accessed=2 * share * out_width + 2 * tokens * (share + out_width),
            transcendentals=0,
        ),
        name="out_projection",
    )(*operands)


def shift(x, axis, by):
    n = lax.axis_size(axis)
    return lax.ppermute(x, axis, [(i, (i + by) % n) for i in range(n)])


def swap_cores(x):
    n = lax.axis_size("chan")
    return lax.ppermute(x, "chan", [(i, i ^ 1) for i in range(n)])


def gather_far(x):
    pieces = []
    for hop in range(1, lax.axis_size("chan") // 2):
        far = shift(x, "chan", 2 * hop)
        pieces += [far, swap_cores(far)]
    return pieces


def exchange(parts):
    out, n = [parts[0]], len(parts)
    for k in range(1, n):
        out.append(lax.ppermute(parts[k], "ctx", [(i, target(i, k, n)) for i in range(n)]))
    return out


def layer(features, filter_taps, skip_gain, in_weight, out_weight):
    return layer_body(features, filter_taps, skip_gain, in_weight, out_weight)


def layer_body(features, filter_taps, skip_gain, in_weight, out_weight):
    n_ctx = lax.axis_size("ctx")
    rows = features.shape[0]
    tokens = rows // CHUNKS
    tables = [jnp.asarray(t) for t in real_dft_tables(tokens)]
    w = in_weight.transpose(1, 0, 2)

    far = [gather_far(features[:tokens])]
    near = swap_cores(features)
    later, skip = lax.optimization_barrier((features, skip_gain))
    far.append(gather_far(later[tokens:]))
    forward, inverse, w_kv, spectra, skip = prologue(tables, skip, filter_taps, w, n_ctx)

    mixed, arrived, query, w_q = [], [], [], None
    for c in range(CHUNKS):
        pieces = [features, near, *far[c]]
        starts = [c * tokens] * 2 + [0] * len(far[c])
        total = ()
        for part, which in ("a", (0, 1)), ("b", range(2, len(pieces) - 1)), ("c", (len(pieces) - 1,)):
            chosen = [starts[j] for j in which]
            total = keys_values(pieces, which, chosen, tokens, w_kv, total, n_ctx, part == "c")
        mixed.append(total)
        arrived.append(exchange(mixed[c]))
        made, *kept = queries(pieces, starts, tokens, w if c == 0 else w_q, n_ctx, c == 0)
        query.append(made)
        w_q = kept[0] if kept else w_q
    conv = convolve(forward, inverse, spectra, arrived, n_ctx)

    gathered = []
    for r, (c, start) in enumerate(((0, 0), (1, 0), (1, tokens // 2))):
        back = exchange(conv[r])
        gated = gate(skip, query[c], mixed[c], back, start, n_ctx)
        beside = swap_cores(gated)
        gathered.append([gated, beside, *gather_far(gated)])
    every = range(len(gathered[0]))
    out = project_out(gathered[0], every, out_weight, None, n_ctx, (0, rows, None))
    out = project_out(gathered[1], every, out_weight, None, n_ctx, (2, rows, out))
    part = project_out(gathered[2], every[:2], out_weight, None, n_ctx)
    part = project_out(gathered[2], every[2:-1], out_weight, part, n_ctx)
    return project_out(gathered[2], every[-1:], out_weight, part, n_ctx, (3, rows, out))


P_SIZE = 128


def dft_tables(block_len):
    period = 2 * block_len
    freq_col = jnp.arange(period, dtype=jnp.int32)[:, None]
    place_row = jnp.arange(period, dtype=jnp.int32)[None, :]
    angles = (freq_col * place_row % period).astype(F32) * (2.0 * math.pi / period)
    forward = jnp.concatenate([jnp.cos(angles), -jnp.sin(angles)], axis=0).astype(BF16)
    out_place = jnp.arange(block_len, dtype=jnp.int32)[:, None] + block_len
    angle_out = (out_place * place_row % period).astype(F32) * (2.0 * math.pi / period)
    inverse = (jnp.concatenate([jnp.cos(angle_out), -jnp.sin(angle_out)], axis=1) / period).astype(BF16)
    return (forward, inverse)


def plain_layer(features, filter_taps, skip_gain, in_weight, out_weight):
    forward, inverse = dft_tables(P_SIZE)
    channels = in_weight.shape[2]
    tok_rows = features.shape[0]
    per_dev = tok_rows // P_SIZE
    period = 2 * P_SIZE
    total_blocks = per_dev * lax.axis_size("ctx")
    first_mine = lax.axis_index("ctx") * per_dev
    padded = jnp.concatenate([jnp.zeros((P_SIZE, channels), BF16), filter_taps], axis=0)
    tap_blocks = padded.reshape(total_blocks + 1, P_SIZE, channels)
    segments = jnp.concatenate([tap_blocks[:-1], tap_blocks[1:]], axis=1)
    lag = jnp.einsum("fn,knc->kfc", forward, segments, preferred_element_type=F32).astype(BF16)
    flipped = jnp.concatenate([lag[::-1], jnp.zeros_like(lag)], axis=0)
    gathered = lax.all_gather(features, "chan", axis=1, tiled=True)
    w = in_weight.transpose(1, 0, 2)
    q, k, v = (jnp.dot(gathered, w[s], preferred_element_type=F32) for s in range(3))
    query = q.astype(BF16)
    mixed = (k * v).astype(BF16)
    everyone = lax.all_gather(mixed, "ctx", axis=0, tiled=True).reshape(total_blocks, P_SIZE, channels)
    source = jnp.einsum("fp,bpc->bfc", forward[:, :P_SIZE], everyone, preferred_element_type=F32)
    source = source.astype(BF16).astype(F32)
    source_re, source_im = source[:, :period], source[:, period:]
    outputs = []
    for out_block in range(per_dev):
        start = total_blocks - 1 - (first_mine + out_block)
        window = lax.dynamic_slice_in_dim(flipped, start, total_blocks, 0).astype(F32)
        lag_re, lag_im = window[:, :period], window[:, period:]
        out_re = jnp.sum(lag_re * source_re - lag_im * source_im, axis=0)
        out_im = jnp.sum(lag_re * source_im + lag_im * source_re, axis=0)
        outputs.append(jnp.concatenate([out_re, out_im], axis=0))
    spectra = jnp.stack(outputs).astype(BF16)
    conv = jnp.einsum("tf,bfc->btc", inverse, spectra, preferred_element_type=F32)
    conv = conv.reshape(tok_rows, channels)
    gated = (query.astype(F32) * (conv + skip_gain[None, :] * mixed.astype(F32))).astype(BF16)
    everything = lax.all_gather(gated, "chan", axis=1, tiled=True)
    return jnp.dot(everything, out_weight, preferred_element_type=F32).astype(BF16)


def shards(features, filter_taps, skip_gain, in_weight, out_weight):
    slices = in_weight.shape[2] % (lax.axis_size("ctx") * LANES) == 0
    cores = lax.axis_size("chan") % 2 == 0 and lax.axis_size("chan") > 2
    blocks = features.shape[0] % (CHUNKS * LANES) == 0
    chosen = layer if slices and cores and blocks else plain_layer
    return chosen(features, filter_taps, skip_gain, in_weight, out_weight)


def solution(mesh):
    return jax.shard_map(
        shards,
        mesh=mesh,
        in_specs=(
            P(("grp", "ctx"), "chan"),
            P(None, "chan"),
            P("chan"),
            P(None, None, "chan"),
            P(None, "chan"),
        ),
        out_specs=P(("grp", "ctx"), "chan"),
        check_vma=False,
    )
```

```python
import functools
import math

import jax
import jax.numpy as jnp
import ml_dtypes
import numpy as np
from jax import lax
from jax.experimental import pallas as pl
from jax.experimental.pallas import tpu as pltpu
from jax.sharding import PartitionSpec as P


BF16 = jnp.bfloat16
F32 = jnp.float32
LANES = 128
MIB = 1 << 20
CHUNKS = 2
VMEM = pl.BlockSpec(memory_space=pltpu.VMEM)
HBM = pl.BlockSpec(memory_space=pltpu.HBM)


def real_dft_tables(block):
    period = 2 * block
    freq = np.arange(block)[:, None]
    place = np.arange(block)[None, :]
    angle = (freq * place % period) * (2.0 * math.pi / period)
    lower = -np.sin(angle)
    lower[0] = 1.0 - 2.0 * (np.arange(block) % 2)
    forward = np.concatenate([np.cos(angle), lower], axis=0)
    out_place = np.arange(block)[:, None] + block
    freq_row = np.arange(block)[None, :]
    angle_out = (out_place * freq_row % period) * (2.0 * math.pi / period)
    weight = np.where(freq_row == 0, 1.0, 2.0)
    lower_out = -np.sin(angle_out) * weight
    lower_out[:, 0] = 1.0 - 2.0 * (np.arange(block) % 2)
    inverse = np.concatenate([np.cos(angle_out) * weight, lower_out], axis=1) / period
    return forward.astype(ml_dtypes.bfloat16), inverse.astype(ml_dtypes.bfloat16)


def call(kernel, out, operands, limit, flops, moved, scratch=()):
    return pl.pallas_call(
        kernel,
        out_shape=out,
        in_specs=[VMEM] * len(operands),
        out_specs=jax.tree.map(lambda _: VMEM, out),
        scratch_shapes=scratch,
        compiler_params=pltpu.CompilerParams(vmem_limit_bytes=limit * MIB),
        cost_estimate=pl.CostEstimate(flops=flops, bytes_accessed=moved, transcendentals=0),
    )(*operands)


def chan_sources():
    n_chan, chan = lax.axis_size("chan"), lax.axis_index("chan")
    sources = [chan, chan ^ 1]
    for hop in range(1, n_chan // 2):
        far = (chan - 2 * hop + n_chan) % n_chan
        sources += [far, far ^ 1]
    return sources


def paired(n):
    return n & (n - 1) == 0


def target(me, k, n):
    return me ^ k if paired(n) else (me + k) % n


def origin(me, k, n):
    return me ^ k if paired(n) else (me - k + n) % n


def mirror(k, n):
    return k if paired(n) else -k % n


def rows_at(first, count):
    return pl.ds(pl.multiple_of(first * count, count), count)


def prologue_kernel(
    width, skip_hbm, fwd_hbm, inv_hbm, taps_ref, w_ref, fwd_ref, inv_ref, kv_ref, out_ref, skip_out, skip_ref, taps_in, prev_ref, sems
):
    block = inv_ref.shape[0]
    cols = rows_at(lax.axis_index("ctx"), width)
    copies = [
        pltpu.make_async_copy(skip_hbm, skip_ref, sems.at[4]),
        pltpu.make_async_copy(fwd_hbm, fwd_ref, sems.at[0]),
        pltpu.make_async_copy(taps_ref.at[:, cols], taps_in, sems.at[1]),
        pltpu.make_async_copy(inv_hbm, inv_ref, sems.at[2]),
        pltpu.make_async_copy(w_ref.at[1:3], kv_ref, sems.at[3]),
    ]
    for copy in copies:
        copy.start()
    prev_ref[...] = jnp.zeros_like(prev_ref)
    for copy in copies[:3]:
        copy.wait()
    for k in range(skip_out.shape[0]):
        skip_out[k, :] = skip_ref[k * width : (k + 1) * width]

    @pl.loop(0, out_ref.shape[0])
    def _(k):
        now = jnp.dot(fwd_ref[...], taps_in[rows_at(k, block), :], preferred_element_type=F32)
        parity = lax.broadcasted_iota(jnp.int32, now.shape, 0) % 2
        out_ref[k] = prev_ref[...] + jnp.where(parity == 0, now, -now)
        prev_ref[...] = now

    for copy in copies[3:]:
        copy.wait()


def prologue(tables, skip, taps, w, n_ctx):
    rows, block = tables[0].shape
    width = w.shape[2] // n_ctx
    count = taps.shape[0] // block
    out = [
        *(jax.ShapeDtypeStruct(t.shape, BF16) for t in tables),
        jax.ShapeDtypeStruct((2, *w.shape[1:]), BF16),
        jax.ShapeDtypeStruct((count, rows, width), F32),
        jax.ShapeDtypeStruct((n_ctx, width), F32),
    ]
    return pl.pallas_call(
        functools.partial(prologue_kernel, width),
        out_shape=out,
        in_specs=[HBM] * 5,
        out_specs=[VMEM] * len(out),
        scratch_shapes=[
            pltpu.VMEM(skip.shape, F32),
            pltpu.VMEM((taps.shape[0], width), BF16),
            pltpu.VMEM((rows, width), F32),
            pltpu.SemaphoreType.DMA((5,)),
        ],
        compiler_params=pltpu.CompilerParams(vmem_limit_bytes=6 * MIB),
        cost_estimate=pl.CostEstimate(
            flops=2 * count * rows * block * width,
            bytes_accessed=2 * w.size + count * width * (rows * 4 + block * 2),
            transcendentals=0,
        ),
        name="prologue",
    )(*(pltpu.with_memory_space_constraint(x, pltpu.HBM) for x in (skip, *tables, taps, w)))


def kv_kernel(which, starts, n_ctx, has_before, last, w_ref, *refs):
    pieces, refs = refs[: len(which)], refs[len(which) :]
    before, outs = (refs[:2], refs[2:]) if has_before else ((), refs)
    tokens = outs[0].shape[0]
    width = w_ref.shape[2] // n_ctx
    depth = pieces[0].shape[1]
    me = lax.axis_index("ctx")
    sources = chan_sources()
    for k in range(n_ctx):
        cols = rows_at(target(me, k, n_ctx), width)
        mine = slice(k * width, (k + 1) * width)
        key, value = (ref[:, mine] for ref in before) if has_before else (None, None)
        for piece, j, start in zip(pieces, which, starts):
            x = piece[start : start + tokens, :]
            rows = rows_at(sources[j], depth)
            a = jnp.dot(x, w_ref[0, rows, cols], preferred_element_type=F32)
            b = jnp.dot(x, w_ref[1, rows, cols], preferred_element_type=F32)
            key = a if key is None else key + a
            value = b if value is None else value + b
        if last:
            outs[k][...] = (key * value).astype(BF16)
        else:
            outs[0][:, mine] = key
            outs[1][:, mine] = value


def keys_values(pieces, which, starts, tokens, w, before, n_ctx, last):
    channels = w.shape[2]
    share = len(which) * pieces[0].shape[1]
    if last:
        out = [jax.ShapeDtypeStruct((tokens, channels // n_ctx), BF16)] * n_ctx
    else:
        out = [jax.ShapeDtypeStruct((tokens, channels), F32)] * 2
    return call(
        functools.partial(kv_kernel, tuple(which), tuple(starts), n_ctx, bool(before), last),
        out,
        [w, *(pieces[j] for j in which), *before],
        6,
        4 * tokens * share * channels,
        4 * share * channels + 2 * tokens * share,
    )


def query_kernel(starts, n_ctx, load, w_ref, *refs):
    pieces, refs = refs[: len(starts)], refs[len(starts) :]
    out_ref, acc_ref = refs[0], refs[-1]
    tokens = out_ref.shape[0]
    depth = pieces[0].shape[1]
    width = out_ref.shape[1] // n_ctx
    me = lax.axis_index("ctx")
    rows = [rows_at(source, depth) for source in chan_sources()]
    copies = []
    if load:
        kept_ref, sems = refs[1:3]
        copies = [
            pltpu.make_async_copy(w_ref.at[0, r], kept_ref.at[r], sems.at[j]) for j, r in enumerate(rows)
        ]
        w_ref = kept_ref
    for copy in copies:
        copy.start()
    for j, piece in enumerate(pieces):
        if load:
            copies[j].wait()
        for k in range(n_ctx):
            mine = slice(k * width, (k + 1) * width)
            x = piece[starts[j] : starts[j] + tokens, :]
            cols = rows_at(target(me, k, n_ctx), width)
            a = jnp.dot(x, w_ref[rows[j], cols], preferred_element_type=F32)
            if j > 0:
                a = acc_ref[:, mine] + a
            if j < len(pieces) - 1:
                acc_ref[:, mine] = a
            else:
                out_ref[:, mine] = a.astype(BF16)


def queries(pieces, starts, tokens, w, n_ctx, load):
    total, channels = w.shape[-2:]
    out = [jax.ShapeDtypeStruct((tokens, channels), BF16)]
    scratch = [pltpu.VMEM((tokens, channels), F32)]
    if load:
        w = pltpu.with_memory_space_constraint(w, pltpu.HBM)
        out.append(jax.ShapeDtypeStruct((total, channels), BF16))
        scratch.insert(0, pltpu.SemaphoreType.DMA((len(pieces),)))
    return pl.pallas_call(
        functools.partial(query_kernel, tuple(starts), n_ctx, load),
        out_shape=out,
        in_specs=[HBM if load else VMEM] + [VMEM] * len(pieces),
        out_specs=[VMEM] * len(out),
        scratch_shapes=scratch,
        compiler_params=pltpu.CompilerParams(vmem_limit_bytes=6 * MIB),
        cost_estimate=pl.CostEstimate(
            flops=2 * tokens * total * channels,
            bytes_accessed=2 * total * channels + 2 * tokens * total,
            transcendentals=0,
        ),
        name="q_projection",
    )(w, *pieces)


def block_products(g_ref, x_ref, before_ref, after_ref, plan, width, block):
    lags = sorted({lag for _, _, terms in plan for lag, _ in terms})
    slots = sorted({slot for _, _, terms in plan for _, slot in terms})

    def tile(i, first):
        upper = pl.ds(i * 8, 8) if first else rows_at(i, 8)
        lower = pl.ds(block + i * 8, 8) if first else rows_at(block // 8 + i, 8)
        for lane in range(width // LANES):
            cols = pl.ds(lane * LANES, LANES)
            g_re = {b: g_ref[b, upper, cols] for b in lags}
            g_im = {b: g_ref[b, lower, cols] for b in lags}
            x_re = {b: x_ref[b, upper, cols] for b in slots}
            x_im = {b: x_ref[b, lower, cols] for b in slots}
            g_di = g_re
            if first:
                edge = lax.broadcasted_iota(jnp.int32, (8, LANES), 0) == 0
                g_di = {b: jnp.where(edge, g_im[b], g_re[b]) for b in lags}
                g_im = {b: jnp.where(edge, 0.0, g_im[b]) for b in lags}
            for start, end, terms in plan:
                re = im = None
                if start is not None:
                    re, im = before_ref[start, upper, cols], before_ref[start, lower, cols]
                for lag, slot in terms:
                    up = g_re[lag] * x_re[slot] - g_im[lag] * x_im[slot]
                    down = g_di[lag] * x_im[slot] + g_im[lag] * x_re[slot]
                    re = up if re is None else re + up
                    im = down if im is None else im + down
                after_ref[end, upper, cols] = re
                after_ref[end, lower, cols] = im

    tile(0, True)
    pl.loop(1, block // 8)(lambda i: tile(i, False))


def forward_dft(n_ctx, fwd_ref, ins, x_ref):
    me = lax.axis_index("ctx")
    for k in range(n_ctx):
        x_ref[origin(me, k, n_ctx)] = jnp.dot(fwd_ref[...], ins[k][...], preferred_element_type=F32)


def inverse_dft(n_ctx, inv_ref, y_ref, outs):
    me = lax.axis_index("ctx")
    tokens = outs[0].shape[0]
    for p in range(len(outs) // n_ctx):
        for k in range(n_ctx):
            spectrum = y_ref[target(me, k, n_ctx)].astype(BF16)
            part = inv_ref[p * tokens : (p + 1) * tokens, :]
            outs[p * n_ctx + k][...] = jnp.dot(part, spectrum, preferred_element_type=F32).astype(BF16)


def early_kernel(n_ctx, fwd_ref, g_ref, *refs):
    ins, sum_ref, x_ref = refs[:n_ctx], refs[n_ctx], refs[n_ctx + 1]
    blocks, rows, width = g_ref.shape
    forward_dft(n_ctx, fwd_ref, ins, x_ref)
    plan = [(None, b, [(b - a, a // 2) for a in range(0, b + 1, 2)]) for b in range(blocks)]
    block_products(g_ref, x_ref, None, sum_ref, plan, width, rows // 2)


def middle_kernel(n_ctx, fwd_ref, inv_ref, g_ref, sum_ref, *refs):
    ins, x_ref, outs, y_ref = refs[:n_ctx], refs[n_ctx], refs[n_ctx + 1 : 2 * n_ctx + 1], refs[-1]
    blocks, rows, width = g_ref.shape
    forward_dft(n_ctx, fwd_ref, ins, x_ref)
    plan = [(b, b // 2, [(b - a, a // 2) for a in range(1, b, 2)]) for b in range(0, blocks, 2)]
    block_products(g_ref, x_ref, sum_ref, y_ref, plan, width, rows // 2)
    inverse_dft(n_ctx, inv_ref, y_ref, outs)


def late_kernel(n_ctx, inv_ref, g_ref, sum_ref, x_ref, *refs):
    outs, y_ref = refs[:-1], refs[-1]
    blocks, rows, width = g_ref.shape
    plan = [(b, b // 2, [(b - a, a // 2) for a in range(1, b + 1, 2)]) for b in range(1, blocks, 2)]
    block_products(g_ref, x_ref, sum_ref, y_ref, plan, width, rows // 2)
    inverse_dft(n_ctx, inv_ref, y_ref, outs)


def convolve(forward, inverse, spectra, arrived, n_ctx):
    blocks, rows, width = spectra.shape
    half = (n_ctx, rows, width)
    piece = jax.ShapeDtypeStruct((rows // 2, width), BF16)
    flops, moved = blocks * rows * rows * width // 2, blocks * rows * width * 8
    sums = call(
        functools.partial(early_kernel, n_ctx),
        jax.ShapeDtypeStruct(spectra.shape, F32),
        [forward, spectra, *arrived[0]],
        6,
        flops,
        moved,
        [pltpu.VMEM(half, F32)],
    )
    x, *even = call(
        functools.partial(middle_kernel, n_ctx),
        [jax.ShapeDtypeStruct(half, F32)] + [piece] * n_ctx,
        [forward, inverse, spectra, sums, *arrived[1]],
        6,
        flops,
        moved,
        [pltpu.VMEM(half, F32)],
    )
    odd = call(
        functools.partial(late_kernel, n_ctx),
        [jax.ShapeDtypeStruct((rows // 4, width), BF16)] * (2 * n_ctx),
        [inverse, spectra, sums, x],
        6,
        flops,
        moved,
        [pltpu.VMEM(half, F32)],
    )
    return even, odd[:n_ctx], odd[n_ctx:]


def gate_kernel(n_ctx, start, skip_ref, q_ref, *refs):
    mixed, conv, out_ref = refs[:n_ctx], refs[n_ctx : 2 * n_ctx], refs[-1]
    tokens, width = conv[0].shape
    rows = slice(start, start + tokens)
    me = lax.axis_index("ctx")
    for m in range(n_ctx):
        cols = slice(m * width, (m + 1) * width)
        skip = skip_ref[pl.ds(target(me, m, n_ctx), 1), :]
        query = q_ref[rows, cols].astype(F32)
        total = conv[mirror(m, n_ctx)][...].astype(F32) + skip * mixed[m][rows, :].astype(F32)
        out_ref[:, cols] = (query * total).astype(BF16)


def gate(skip, query, mixed, conv, start, n_ctx):
    shape = (conv[0].shape[0], query.shape[1])
    return call(
        functools.partial(gate_kernel, n_ctx, start),
        jax.ShapeDtypeStruct(shape, BF16),
        [skip, query, *mixed, *conv],
        4,
        3 * shape[0] * shape[1],
        8 * shape[0] * shape[1],
    )


def out_kernel(which, parts, has_before, n_ctx, w_ref, *refs):
    pieces, out_ref = refs[: len(which) * parts], refs[-1]
    columns = out_ref.shape[1]
    width = pieces[0].shape[1] // n_ctx
    cols = rows_at(pl.program_id(0), columns)
    me = lax.axis_index("ctx")
    sources = chan_sources()
    acc = refs[len(pieces)][:, cols] if has_before else None
    for i, j in enumerate(which):
        for m in range(n_ctx):
            w = w_ref[rows_at(sources[j] * n_ctx + target(me, m, n_ctx), width), cols]
            mine = slice(m * width, (m + 1) * width)
            x = jnp.concatenate([p[:, mine] for p in pieces[i * parts : (i + 1) * parts]], axis=0)
            a = jnp.dot(x, w, preferred_element_type=F32)
            acc = a if acc is None else acc + a
    out_ref[...] = acc.astype(out_ref.dtype)


def project_out(gathered, which, w, before, n_ctx, final=None, columns=256):
    parts = len(gathered)
    tokens = sum(pieces[0].shape[0] for pieces in gathered)
    _, out_width = w.shape
    operands = [w, *(pieces[j] for j in which for pieces in gathered)] + ([] if before is None else [before])
    specs = [VMEM] * len(operands)
    aliases = {}
    out_spec, shape = pl.BlockSpec((tokens, columns), lambda i: (0, i)), (tokens, out_width)
    if final is not None:
        chunk, rows, so_far = final
        out_spec, shape = pl.BlockSpec((tokens, columns), lambda i: (chunk, i)), (rows, out_width)
        if so_far is not None:
            specs.append(pl.BlockSpec(memory_space=pl.ANY))
            aliases = {len(operands): 0}
            operands.append(so_far)
    share = len(which) * gathered[0][0].shape[1]
    return pl.pallas_call(
        functools.partial(out_kernel, tuple(which), parts, before is not None, n_ctx),
        out_shape=jax.ShapeDtypeStruct(shape, F32 if final is None else BF16),
        grid=(out_width // columns,),
        in_specs=specs,
        out_specs=out_spec,
        input_output_aliases=aliases,
        compiler_params=pltpu.CompilerParams(vmem_limit_bytes=6 * MIB),
        cost_estimate=pl.CostEstimate(
            flops=2 * tokens * share * out_width,
            bytes_accessed=2 * share * out_width + 2 * tokens * (share + out_width),
            transcendentals=0,
        ),
        name="out_projection",
    )(*operands)


def shift(x, axis, by):
    n = lax.axis_size(axis)
    return lax.ppermute(x, axis, [(i, (i + by) % n) for i in range(n)])


def swap_cores(x):
    n = lax.axis_size("chan")
    return lax.ppermute(x, "chan", [(i, i ^ 1) for i in range(n)])


def gather_far(x):
    pieces = []
    for hop in range(1, lax.axis_size("chan") // 2):
        far = shift(x, "chan", 2 * hop)
        pieces += [far, swap_cores(far)]
    return pieces


def exchange(parts):
    out, n = [parts[0]], len(parts)
    for k in range(1, n):
        out.append(lax.ppermute(parts[k], "ctx", [(i, target(i, k, n)) for i in range(n)]))
    return out


def layer(features, filter_taps, skip_gain, in_weight, out_weight):
    return layer_body(features, filter_taps, skip_gain, in_weight, out_weight)


def layer_body(features, filter_taps, skip_gain, in_weight, out_weight):
    n_ctx = lax.axis_size("ctx")
    rows = features.shape[0]
    tokens = rows // CHUNKS
    tables = [jnp.asarray(t) for t in real_dft_tables(tokens)]
    w = in_weight.transpose(1, 0, 2)

    far = [gather_far(features[:tokens])]
    near = swap_cores(features)
    later, skip = lax.optimization_barrier((features, skip_gain))
    far.append(gather_far(later[tokens:]))
    forward, inverse, w_kv, spectra, skip = prologue(tables, skip, filter_taps, w, n_ctx)

    mixed, arrived, query, w_q = [], [], [], None
    for c in range(CHUNKS):
        pieces = [features, near, *far[c]]
        starts = [c * tokens] * 2 + [0] * len(far[c])
        total = ()
        for part, which in ("a", (0, 1)), ("b", range(2, len(pieces) - 1)), ("c", (len(pieces) - 1,)):
            chosen = [starts[j] for j in which]
            total = keys_values(pieces, which, chosen, tokens, w_kv, total, n_ctx, part == "c")
        mixed.append(total)
        arrived.append(exchange(mixed[c]))
        made, *kept = queries(pieces, starts, tokens, w if c == 0 else w_q, n_ctx, c == 0)
        query.append(made)
        w_q = kept[0] if kept else w_q
    conv = convolve(forward, inverse, spectra, arrived, n_ctx)

    gathered = []
    for r, (c, start) in enumerate(((0, 0), (1, 0), (1, tokens // 2))):
        back = exchange(conv[r])
        gated = gate(skip, query[c], mixed[c], back, start, n_ctx)
        beside = swap_cores(gated)
        gathered.append([gated, beside, *gather_far(gated)])
    every = range(len(gathered[0]))
    out = project_out(gathered[:1], every, out_weight, None, n_ctx, (0, rows, None))
    part = project_out(gathered[1:], every[:2], out_weight, None, n_ctx)
    part = project_out(gathered[1:], every[2:-1], out_weight, part, n_ctx)
    return project_out(gathered[1:], every[-1:], out_weight, part, n_ctx, (1, rows, out))


P_SIZE = 128


def dft_tables(block_len):
    period = 2 * block_len
    freq_col = jnp.arange(period, dtype=jnp.int32)[:, None]
    place_row = jnp.arange(period, dtype=jnp.int32)[None, :]
    angles = (freq_col * place_row % period).astype(F32) * (2.0 * math.pi / period)
    forward = jnp.concatenate([jnp.cos(angles), -jnp.sin(angles)], axis=0).astype(BF16)
    out_place = jnp.arange(block_len, dtype=jnp.int32)[:, None] + block_len
    angle_out = (out_place * place_row % period).astype(F32) * (2.0 * math.pi / period)
    inverse = (jnp.concatenate([jnp.cos(angle_out), -jnp.sin(angle_out)], axis=1) / period).astype(BF16)
    return (forward, inverse)


def plain_layer(features, filter_taps, skip_gain, in_weight, out_weight):
    forward, inverse = dft_tables(P_SIZE)
    channels = in_weight.shape[2]
    tok_rows = features.shape[0]
    per_dev = tok_rows // P_SIZE
    period = 2 * P_SIZE
    total_blocks = per_dev * lax.axis_size("ctx")
    first_mine = lax.axis_index("ctx") * per_dev
    padded = jnp.concatenate([jnp.zeros((P_SIZE, channels), BF16), filter_taps], axis=0)
    tap_blocks = padded.reshape(total_blocks + 1, P_SIZE, channels)
    segments = jnp.concatenate([tap_blocks[:-1], tap_blocks[1:]], axis=1)
    lag = jnp.einsum("fn,knc->kfc", forward, segments, preferred_element_type=F32).astype(BF16)
    flipped = jnp.concatenate([lag[::-1], jnp.zeros_like(lag)], axis=0)
    gathered = lax.all_gather(features, "chan", axis=1, tiled=True)
    w = in_weight.transpose(1, 0, 2)
    q, k, v = (jnp.dot(gathered, w[s], preferred_element_type=F32) for s in range(3))
    query = q.astype(BF16)
    mixed = (k * v).astype(BF16)
    everyone = lax.all_gather(mixed, "ctx", axis=0, tiled=True).reshape(total_blocks, P_SIZE, channels)
    source = jnp.einsum("fp,bpc->bfc", forward[:, :P_SIZE], everyone, preferred_element_type=F32)
    source = source.astype(BF16).astype(F32)
    source_re, source_im = source[:, :period], source[:, period:]
    outputs = []
    for out_block in range(per_dev):
        start = total_blocks - 1 - (first_mine + out_block)
        window = lax.dynamic_slice_in_dim(flipped, start, total_blocks, 0).astype(F32)
        lag_re, lag_im = window[:, :period], window[:, period:]
        out_re = jnp.sum(lag_re * source_re - lag_im * source_im, axis=0)
        out_im = jnp.sum(lag_re * source_im + lag_im * source_re, axis=0)
        outputs.append(jnp.concatenate([out_re, out_im], axis=0))
    spectra = jnp.stack(outputs).astype(BF16)
    conv = jnp.einsum("tf,bfc->btc", inverse, spectra, preferred_element_type=F32)
    conv = conv.reshape(tok_rows, channels)
    gated = (query.astype(F32) * (conv + skip_gain[None, :] * mixed.astype(F32))).astype(BF16)
    everything = lax.all_gather(gated, "chan", axis=1, tiled=True)
    return jnp.dot(everything, out_weight, preferred_element_type=F32).astype(BF16)


def shards(features, filter_taps, skip_gain, in_weight, out_weight):
    slices = in_weight.shape[2] % (lax.axis_size("ctx") * LANES) == 0
    cores = lax.axis_size("chan") % 2 == 0 and lax.axis_size("chan") > 2
    blocks = features.shape[0] % (CHUNKS * LANES) == 0
    chosen = layer if slices and cores and blocks else plain_layer
    return chosen(features, filter_taps, skip_gain, in_weight, out_weight)


def solution(mesh):
    return jax.shard_map(
        shards,
        mesh=mesh,
        in_specs=(
            P(("grp", "ctx"), "chan"),
            P(None, "chan"),
            P("chan"),
            P(None, None, "chan"),
            P(None, "chan"),
        ),
        out_specs=P(("grp", "ctx"), "chan"),
        check_vma=False,
    )
```

```python
import functools
import math

import jax
import jax.numpy as jnp
import ml_dtypes
import numpy as np
from jax import lax
from jax.experimental import pallas as pl
from jax.experimental.pallas import tpu as pltpu
from jax.sharding import PartitionSpec as P


BF16 = jnp.bfloat16
F32 = jnp.float32
LANES = 128
MIB = 1 << 20
CHUNKS = 2
VMEM = pl.BlockSpec(memory_space=pltpu.VMEM)
HBM = pl.BlockSpec(memory_space=pltpu.HBM)


def real_dft_tables(block):
    period = 2 * block
    freq = np.arange(block)[:, None]
    place = np.arange(block)[None, :]
    angle = (freq * place % period) * (2.0 * math.pi / period)
    lower = -np.sin(angle)
    lower[0] = 1.0 - 2.0 * (np.arange(block) % 2)
    forward = np.concatenate([np.cos(angle), lower], axis=0)
    out_place = np.arange(block)[:, None] + block
    freq_row = np.arange(block)[None, :]
    angle_out = (out_place * freq_row % period) * (2.0 * math.pi / period)
    weight = np.where(freq_row == 0, 1.0, 2.0)
    lower_out = -np.sin(angle_out) * weight
    lower_out[:, 0] = 1.0 - 2.0 * (np.arange(block) % 2)
    inverse = np.concatenate([np.cos(angle_out) * weight, lower_out], axis=1) / period
    return forward.astype(ml_dtypes.bfloat16), inverse.astype(ml_dtypes.bfloat16)


def call(kernel, out, operands, limit, flops, moved, scratch=()):
    return pl.pallas_call(
        kernel,
        out_shape=out,
        in_specs=[VMEM] * len(operands),
        out_specs=jax.tree.map(lambda _: VMEM, out),
        scratch_shapes=scratch,
        compiler_params=pltpu.CompilerParams(vmem_limit_bytes=limit * MIB),
        cost_estimate=pl.CostEstimate(flops=flops, bytes_accessed=moved, transcendentals=0),
    )(*operands)


def chan_sources():
    n_chan, chan = lax.axis_size("chan"), lax.axis_index("chan")
    sources = [chan, chan ^ 1]
    for hop in range(1, n_chan // 2):
        far = (chan - 2 * hop + n_chan) % n_chan
        sources += [far, far ^ 1]
    return sources


def paired(n):
    return n & (n - 1) == 0


def target(me, k, n):
    return me ^ k if paired(n) else (me + k) % n


def origin(me, k, n):
    return me ^ k if paired(n) else (me - k + n) % n


def mirror(k, n):
    return k if paired(n) else -k % n


def rows_at(first, count):
    return pl.ds(pl.multiple_of(first * count, count), count)


def prologue_kernel(
    width, skip_hbm, fwd_hbm, inv_hbm, taps_ref, w_ref, fwd_ref, inv_ref, kv_ref, out_ref, skip_out, skip_ref, taps_in, prev_ref, sems
):
    block = inv_ref.shape[0]
    cols = rows_at(lax.axis_index("ctx"), width)
    copies = [
        pltpu.make_async_copy(skip_hbm, skip_ref, sems.at[4]),
        pltpu.make_async_copy(fwd_hbm, fwd_ref, sems.at[0]),
        pltpu.make_async_copy(taps_ref.at[:, cols], taps_in, sems.at[1]),
        pltpu.make_async_copy(inv_hbm, inv_ref, sems.at[2]),
        pltpu.make_async_copy(w_ref.at[1:3], kv_ref, sems.at[3]),
    ]
    for copy in copies:
        copy.start()
    prev_ref[...] = jnp.zeros_like(prev_ref)
    for copy in copies[:3]:
        copy.wait()
    for k in range(skip_out.shape[0]):
        skip_out[k, :] = skip_ref[k * width : (k + 1) * width]

    @pl.loop(0, out_ref.shape[0])
    def _(k):
        now = jnp.dot(fwd_ref[...], taps_in[rows_at(k, block), :], preferred_element_type=F32)
        parity = lax.broadcasted_iota(jnp.int32, now.shape, 0) % 2
        out_ref[k] = prev_ref[...] + jnp.where(parity == 0, now, -now)
        prev_ref[...] = now

    for copy in copies[3:]:
        copy.wait()


def prologue(tables, skip, taps, w, n_ctx):
    rows, block = tables[0].shape
    width = w.shape[2] // n_ctx
    count = taps.shape[0] // block
    out = [
        *(jax.ShapeDtypeStruct(t.shape, BF16) for t in tables),
        jax.ShapeDtypeStruct((2, *w.shape[1:]), BF16),
        jax.ShapeDtypeStruct((count, rows, width), F32),
        jax.ShapeDtypeStruct((n_ctx, width), F32),
    ]
    return pl.pallas_call(
        functools.partial(prologue_kernel, width),
        out_shape=out,
        in_specs=[HBM] * 5,
        out_specs=[VMEM] * len(out),
        scratch_shapes=[
            pltpu.VMEM(skip.shape, F32),
            pltpu.VMEM((taps.shape[0], width), BF16),
            pltpu.VMEM((rows, width), F32),
            pltpu.SemaphoreType.DMA((5,)),
        ],
        compiler_params=pltpu.CompilerParams(vmem_limit_bytes=6 * MIB),
        cost_estimate=pl.CostEstimate(
            flops=2 * count * rows * block * width,
            bytes_accessed=2 * w.size + count * width * (rows * 4 + block * 2),
            transcendentals=0,
        ),
        name="prologue",
    )(*(pltpu.with_memory_space_constraint(x, pltpu.HBM) for x in (skip, *tables, taps, w)))


def kv_kernel(which, starts, n_ctx, has_before, last, w_ref, *refs):
    pieces, refs = refs[: len(which)], refs[len(which) :]
    before, outs = (refs[:2], refs[2:]) if has_before else ((), refs)
    tokens = outs[0].shape[0]
    width = w_ref.shape[2] // n_ctx
    depth = pieces[0].shape[1]
    me = lax.axis_index("ctx")
    sources = chan_sources()
    for k in range(n_ctx):
        cols = rows_at(target(me, k, n_ctx), width)
        mine = slice(k * width, (k + 1) * width)
        key, value = (ref[:, mine] for ref in before) if has_before else (None, None)
        for piece, j, start in zip(pieces, which, starts):
            x = piece[start : start + tokens, :]
            rows = rows_at(sources[j], depth)
            a = jnp.dot(x, w_ref[0, rows, cols], preferred_element_type=F32)
            b = jnp.dot(x, w_ref[1, rows, cols], preferred_element_type=F32)
            key = a if key is None else key + a
            value = b if value is None else value + b
        if last:
            outs[k][...] = (key * value).astype(BF16)
        else:
            outs[0][:, mine] = key
            outs[1][:, mine] = value


def keys_values(pieces, which, starts, tokens, w, before, n_ctx, last):
    channels = w.shape[2]
    share = len(which) * pieces[0].shape[1]
    if last:
        out = [jax.ShapeDtypeStruct((tokens, channels // n_ctx), BF16)] * n_ctx
    else:
        out = [jax.ShapeDtypeStruct((tokens, channels), F32)] * 2
    return call(
        functools.partial(kv_kernel, tuple(which), tuple(starts), n_ctx, bool(before), last),
        out,
        [w, *(pieces[j] for j in which), *before],
        6,
        4 * tokens * share * channels,
        4 * share * channels + 2 * tokens * share,
    )


def query_kernel(starts, n_ctx, load, w_ref, *refs):
    pieces, refs = refs[: len(starts)], refs[len(starts) :]
    out_ref, acc_ref = refs[0], refs[-1]
    tokens = out_ref.shape[0]
    depth = pieces[0].shape[1]
    width = out_ref.shape[1] // n_ctx
    me = lax.axis_index("ctx")
    rows = [rows_at(source, depth) for source in chan_sources()]
    copies = []
    if load:
        kept_ref, sems = refs[1:3]
        copies = [
            pltpu.make_async_copy(w_ref.at[0, r], kept_ref.at[r], sems.at[j]) for j, r in enumerate(rows)
        ]
        w_ref = kept_ref
    for copy in copies:
        copy.start()
    for j, piece in enumerate(pieces):
        if load:
            copies[j].wait()
        for k in range(n_ctx):
            mine = slice(k * width, (k + 1) * width)
            x = piece[starts[j] : starts[j] + tokens, :]
            cols = rows_at(target(me, k, n_ctx), width)
            a = jnp.dot(x, w_ref[rows[j], cols], preferred_element_type=F32)
            if j > 0:
                a = acc_ref[:, mine] + a
            if j < len(pieces) - 1:
                acc_ref[:, mine] = a
            else:
                out_ref[:, mine] = a.astype(BF16)


def queries(pieces, starts, tokens, w, n_ctx, load):
    total, channels = w.shape[-2:]
    out = [jax.ShapeDtypeStruct((tokens, channels), BF16)]
    scratch = [pltpu.VMEM((tokens, channels), F32)]
    if load:
        w = pltpu.with_memory_space_constraint(w, pltpu.HBM)
        out.append(jax.ShapeDtypeStruct((total, channels), BF16))
        scratch.insert(0, pltpu.SemaphoreType.DMA((len(pieces),)))
    return pl.pallas_call(
        functools.partial(query_kernel, tuple(starts), n_ctx, load),
        out_shape=out,
        in_specs=[HBM if load else VMEM] + [VMEM] * len(pieces),
        out_specs=[VMEM] * len(out),
        scratch_shapes=scratch,
        compiler_params=pltpu.CompilerParams(vmem_limit_bytes=6 * MIB),
        cost_estimate=pl.CostEstimate(
            flops=2 * tokens * total * channels,
            bytes_accessed=2 * total * channels + 2 * tokens * total,
            transcendentals=0,
        ),
        name="q_projection",
    )(w, *pieces)


def block_products(g_ref, x_ref, before_ref, after_ref, plan, width, block):
    lags = sorted({lag for _, _, terms in plan for lag, _ in terms})
    slots = sorted({slot for _, _, terms in plan for _, slot in terms})

    def tile(i, first):
        upper = pl.ds(i * 8, 8) if first else rows_at(i, 8)
        lower = pl.ds(block + i * 8, 8) if first else rows_at(block // 8 + i, 8)
        for lane in range(width // LANES):
            cols = pl.ds(lane * LANES, LANES)
            g_re = {b: g_ref[b, upper, cols] for b in lags}
            g_im = {b: g_ref[b, lower, cols] for b in lags}
            x_re = {b: x_ref[b, upper, cols] for b in slots}
            x_im = {b: x_ref[b, lower, cols] for b in slots}
            g_di = g_re
            if first:
                edge = lax.broadcasted_iota(jnp.int32, (8, LANES), 0) == 0
                g_di = {b: jnp.where(edge, g_im[b], g_re[b]) for b in lags}
                g_im = {b: jnp.where(edge, 0.0, g_im[b]) for b in lags}
            for start, end, terms in plan:
                re = im = None
                if start is not None:
                    re, im = before_ref[start, upper, cols], before_ref[start, lower, cols]
                for lag, slot in terms:
                    up = g_re[lag] * x_re[slot] - g_im[lag] * x_im[slot]
                    down = g_di[lag] * x_im[slot] + g_im[lag] * x_re[slot]
                    re = up if re is None else re + up
                    im = down if im is None else im + down
                after_ref[end, upper, cols] = re
                after_ref[end, lower, cols] = im

    tile(0, True)
    pl.loop(1, block // 8)(lambda i: tile(i, False))


def forward_dft(n_ctx, fwd_ref, ins, x_ref):
    me = lax.axis_index("ctx")
    for k in range(n_ctx):
        x_ref[origin(me, k, n_ctx)] = jnp.dot(fwd_ref[...], ins[k][...], preferred_element_type=F32)


def inverse_dft(n_ctx, inv_ref, y_ref, outs):
    me = lax.axis_index("ctx")
    tokens = outs[0].shape[0]
    for p in range(len(outs) // n_ctx):
        for k in range(n_ctx):
            spectrum = y_ref[target(me, k, n_ctx)].astype(BF16)
            part = inv_ref[p * tokens : (p + 1) * tokens, :]
            outs[p * n_ctx + k][...] = jnp.dot(part, spectrum, preferred_element_type=F32).astype(BF16)


def early_kernel(n_ctx, fwd_ref, g_ref, *refs):
    ins, sum_ref, x_ref = refs[:n_ctx], refs[n_ctx], refs[n_ctx + 1]
    blocks, rows, width = g_ref.shape
    forward_dft(n_ctx, fwd_ref, ins, x_ref)
    plan = [(None, b, [(b - a, a // 2) for a in range(0, b + 1, 2)]) for b in range(blocks)]
    block_products(g_ref, x_ref, None, sum_ref, plan, width, rows // 2)


def middle_kernel(n_ctx, fwd_ref, inv_ref, g_ref, sum_ref, *refs):
    ins, x_ref, outs, y_ref = refs[:n_ctx], refs[n_ctx], refs[n_ctx + 1 : -1], refs[-1]
    blocks, rows, width = g_ref.shape
    forward_dft(n_ctx, fwd_ref, ins, x_ref)
    plan = [(b, b // 2, [(b - a, a // 2) for a in range(1, b, 2)]) for b in range(0, blocks, 2)]
    block_products(g_ref, x_ref, sum_ref, y_ref, plan, width, rows // 2)
    inverse_dft(n_ctx, inv_ref, y_ref, outs)


def late_kernel(n_ctx, inv_ref, g_ref, sum_ref, x_ref, *refs):
    outs, y_ref = refs[:-1], refs[-1]
    blocks, rows, width = g_ref.shape
    plan = [(b, b // 2, [(b - a, a // 2) for a in range(1, b + 1, 2)]) for b in range(1, blocks, 2)]
    block_products(g_ref, x_ref, sum_ref, y_ref, plan, width, rows // 2)
    inverse_dft(n_ctx, inv_ref, y_ref, outs)


def convolve(forward, inverse, spectra, arrived, n_ctx):
    blocks, rows, width = spectra.shape
    half = (n_ctx, rows, width)
    piece = jax.ShapeDtypeStruct((rows // 4, width), BF16)
    flops, moved = blocks * rows * rows * width // 2, blocks * rows * width * 8
    sums = call(
        functools.partial(early_kernel, n_ctx),
        jax.ShapeDtypeStruct(spectra.shape, F32),
        [forward, spectra, *arrived[0]],
        6,
        flops,
        moved,
        [pltpu.VMEM(half, F32)],
    )
    x, *even = call(
        functools.partial(middle_kernel, n_ctx),
        [jax.ShapeDtypeStruct(half, F32)] + [piece] * (2 * n_ctx),
        [forward, inverse, spectra, sums, *arrived[1]],
        6,
        flops,
        moved,
        [pltpu.VMEM(half, F32)],
    )
    odd = call(
        functools.partial(late_kernel, n_ctx),
        [piece] * (2 * n_ctx),
        [inverse, spectra, sums, x],
        6,
        flops,
        moved,
        [pltpu.VMEM(half, F32)],
    )
    return even[:n_ctx], even[n_ctx:], odd[:n_ctx], odd[n_ctx:]


def gate_kernel(n_ctx, start, skip_ref, q_ref, *refs):
    mixed, conv, out_ref = refs[:n_ctx], refs[n_ctx : 2 * n_ctx], refs[-1]
    tokens, width = conv[0].shape
    rows = slice(start, start + tokens)
    me = lax.axis_index("ctx")
    for m in range(n_ctx):
        cols = slice(m * width, (m + 1) * width)
        skip = skip_ref[pl.ds(target(me, m, n_ctx), 1), :]
        query = q_ref[rows, cols].astype(F32)
        total = conv[mirror(m, n_ctx)][...].astype(F32) + skip * mixed[m][rows, :].astype(F32)
        out_ref[:, cols] = (query * total).astype(BF16)


def gate(skip, query, mixed, conv, start, n_ctx):
    shape = (conv[0].shape[0], query.shape[1])
    return call(
        functools.partial(gate_kernel, n_ctx, start),
        jax.ShapeDtypeStruct(shape, BF16),
        [skip, query, *mixed, *conv],
        4,
        3 * shape[0] * shape[1],
        8 * shape[0] * shape[1],
    )


def out_kernel(which, parts, has_before, n_ctx, w_ref, *refs):
    pieces, out_ref = refs[: len(which) * parts], refs[-1]
    columns = out_ref.shape[1]
    width = pieces[0].shape[1] // n_ctx
    cols = rows_at(pl.program_id(0), columns)
    me = lax.axis_index("ctx")
    sources = chan_sources()
    acc = refs[len(pieces)][:, cols] if has_before else None
    for i, j in enumerate(which):
        for m in range(n_ctx):
            w = w_ref[rows_at(sources[j] * n_ctx + target(me, m, n_ctx), width), cols]
            mine = slice(m * width, (m + 1) * width)
            x = jnp.concatenate([p[:, mine] for p in pieces[i * parts : (i + 1) * parts]], axis=0)
            a = jnp.dot(x, w, preferred_element_type=F32)
            acc = a if acc is None else acc + a
    out_ref[...] = acc.astype(out_ref.dtype)


def project_out(gathered, which, w, before, n_ctx, final=None, columns=256):
    parts = len(gathered)
    tokens = sum(pieces[0].shape[0] for pieces in gathered)
    _, out_width = w.shape
    operands = [w, *(pieces[j] for j in which for pieces in gathered)] + ([] if before is None else [before])
    specs = [VMEM] * len(operands)
    aliases = {}
    out_spec, shape = pl.BlockSpec((tokens, columns), lambda i: (0, i)), (tokens, out_width)
    if final is not None:
        chunk, rows, so_far = final
        out_spec, shape = pl.BlockSpec((tokens, columns), lambda i: (chunk, i)), (rows, out_width)
        if so_far is not None:
            specs.append(pl.BlockSpec(memory_space=pl.ANY))
            aliases = {len(operands): 0}
            operands.append(so_far)
    share = len(which) * gathered[0][0].shape[1]
    return pl.pallas_call(
        functools.partial(out_kernel, tuple(which), parts, before is not None, n_ctx),
        out_shape=jax.ShapeDtypeStruct(shape, F32 if final is None else BF16),
        grid=(out_width // columns,),
        in_specs=specs,
        out_specs=out_spec,
        input_output_aliases=aliases,
        compiler_params=pltpu.CompilerParams(vmem_limit_bytes=6 * MIB),
        cost_estimate=pl.CostEstimate(
            flops=2 * tokens * share * out_width,
            bytes_accessed=2 * share * out_width + 2 * tokens * (share + out_width),
            transcendentals=0,
        ),
        name="out_projection",
    )(*operands)


def shift(x, axis, by):
    n = lax.axis_size(axis)
    return lax.ppermute(x, axis, [(i, (i + by) % n) for i in range(n)])


def swap_cores(x):
    n = lax.axis_size("chan")
    return lax.ppermute(x, "chan", [(i, i ^ 1) for i in range(n)])


def gather_far(x):
    pieces = []
    for hop in range(1, lax.axis_size("chan") // 2):
        far = shift(x, "chan", 2 * hop)
        pieces += [far, swap_cores(far)]
    return pieces


def exchange(parts):
    out, n = [parts[0]], len(parts)
    for k in range(1, n):
        out.append(lax.ppermute(parts[k], "ctx", [(i, target(i, k, n)) for i in range(n)]))
    return out


def layer(features, filter_taps, skip_gain, in_weight, out_weight):
    return layer_body(features, filter_taps, skip_gain, in_weight, out_weight)


def layer_body(features, filter_taps, skip_gain, in_weight, out_weight):
    n_ctx = lax.axis_size("ctx")
    rows = features.shape[0]
    tokens = rows // CHUNKS
    tables = [jnp.asarray(t) for t in real_dft_tables(tokens)]
    w = in_weight.transpose(1, 0, 2)

    far = [gather_far(features[:tokens])]
    near = swap_cores(features)
    later, skip = lax.optimization_barrier((features, skip_gain))
    far.append(gather_far(later[tokens:]))
    forward, inverse, w_kv, spectra, skip = prologue(tables, skip, filter_taps, w, n_ctx)

    mixed, arrived, query, w_q = [], [], [], None
    for c in range(CHUNKS):
        pieces = [features, near, *far[c]]
        starts = [c * tokens] * 2 + [0] * len(far[c])
        total = ()
        for part, which in ("a", (0, 1)), ("b", range(2, len(pieces) - 1)), ("c", (len(pieces) - 1,)):
            chosen = [starts[j] for j in which]
            total = keys_values(pieces, which, chosen, tokens, w_kv, total, n_ctx, part == "c")
        mixed.append(total)
        arrived.append(exchange(mixed[c]))
        made, *kept = queries(pieces, starts, tokens, w if c == 0 else w_q, n_ctx, c == 0)
        query.append(made)
        w_q = kept[0] if kept else w_q
    conv = convolve(forward, inverse, spectra, arrived, n_ctx)

    gathered = []
    for r in range(2 * CHUNKS):
        c, start = r // 2, r % 2 * (tokens // 2)
        back = exchange(conv[r])
        gated = gate(skip, query[c], mixed[c], back, start, n_ctx)
        beside = swap_cores(gated)
        gathered.append([gated, beside, *gather_far(gated)])
    every = range(len(gathered[0]))
    out = project_out(gathered[:2], every, out_weight, None, n_ctx, (0, rows, None))
    part = project_out(gathered[2:], every[:2], out_weight, None, n_ctx)
    part = project_out(gathered[2:], every[2:-1], out_weight, part, n_ctx)
    return project_out(gathered[2:], every[-1:], out_weight, part, n_ctx, (1, rows, out))


P_SIZE = 128


def dft_tables(block_len):
    period = 2 * block_len
    freq_col = jnp.arange(period, dtype=jnp.int32)[:, None]
    place_row = jnp.arange(period, dtype=jnp.int32)[None, :]
    angles = (freq_col * place_row % period).astype(F32) * (2.0 * math.pi / period)
    forward = jnp.concatenate([jnp.cos(angles), -jnp.sin(angles)], axis=0).astype(BF16)
    out_place = jnp.arange(block_len, dtype=jnp.int32)[:, None] + block_len
    angle_out = (out_place * place_row % period).astype(F32) * (2.0 * math.pi / period)
    inverse = (jnp.concatenate([jnp.cos(angle_out), -jnp.sin(angle_out)], axis=1) / period).astype(BF16)
    return (forward, inverse)


def plain_layer(features, filter_taps, skip_gain, in_weight, out_weight):
    forward, inverse = dft_tables(P_SIZE)
    channels = in_weight.shape[2]
    tok_rows = features.shape[0]
    per_dev = tok_rows // P_SIZE
    period = 2 * P_SIZE
    total_blocks = per_dev * lax.axis_size("ctx")
    first_mine = lax.axis_index("ctx") * per_dev
    padded = jnp.concatenate([jnp.zeros((P_SIZE, channels), BF16), filter_taps], axis=0)
    tap_blocks = padded.reshape(total_blocks + 1, P_SIZE, channels)
    segments = jnp.concatenate([tap_blocks[:-1], tap_blocks[1:]], axis=1)
    lag = jnp.einsum("fn,knc->kfc", forward, segments, preferred_element_type=F32).astype(BF16)
    flipped = jnp.concatenate([lag[::-1], jnp.zeros_like(lag)], axis=0)
    gathered = lax.all_gather(features, "chan", axis=1, tiled=True)
    w = in_weight.transpose(1, 0, 2)
    q, k, v = (jnp.dot(gathered, w[s], preferred_element_type=F32) for s in range(3))
    query = q.astype(BF16)
    mixed = (k * v).astype(BF16)
    everyone = lax.all_gather(mixed, "ctx", axis=0, tiled=True).reshape(total_blocks, P_SIZE, channels)
    source = jnp.einsum("fp,bpc->bfc", forward[:, :P_SIZE], everyone, preferred_element_type=F32)
    source = source.astype(BF16).astype(F32)
    source_re, source_im = source[:, :period], source[:, period:]
    outputs = []
    for out_block in range(per_dev):
        start = total_blocks - 1 - (first_mine + out_block)
        window = lax.dynamic_slice_in_dim(flipped, start, total_blocks, 0).astype(F32)
        lag_re, lag_im = window[:, :period], window[:, period:]
        out_re = jnp.sum(lag_re * source_re - lag_im * source_im, axis=0)
        out_im = jnp.sum(lag_re * source_im + lag_im * source_re, axis=0)
        outputs.append(jnp.concatenate([out_re, out_im], axis=0))
    spectra = jnp.stack(outputs).astype(BF16)
    conv = jnp.einsum("tf,bfc->btc", inverse, spectra, preferred_element_type=F32)
    conv = conv.reshape(tok_rows, channels)
    gated = (query.astype(F32) * (conv + skip_gain[None, :] * mixed.astype(F32))).astype(BF16)
    everything = lax.all_gather(gated, "chan", axis=1, tiled=True)
    return jnp.dot(everything, out_weight, preferred_element_type=F32).astype(BF16)


def shards(features, filter_taps, skip_gain, in_weight, out_weight):
    slices = in_weight.shape[2] % (lax.axis_size("ctx") * LANES) == 0
    cores = lax.axis_size("chan") % 2 == 0 and lax.axis_size("chan") > 2
    blocks = features.shape[0] % (CHUNKS * LANES) == 0
    chosen = layer if slices and cores and blocks else plain_layer
    return chosen(features, filter_taps, skip_gain, in_weight, out_weight)


def solution(mesh):
    return jax.shard_map(
        shards,
        mesh=mesh,
        in_specs=(
            P(("grp", "ctx"), "chan"),
            P(None, "chan"),
            P("chan"),
            P(None, None, "chan"),
            P(None, "chan"),
        ),
        out_specs=P(("grp", "ctx"), "chan"),
        check_vma=False,
    )
```

```python
import functools
import math

import jax
import jax.numpy as jnp
import ml_dtypes
import numpy as np
from jax import lax
from jax.experimental import pallas as pl
from jax.experimental.pallas import tpu as pltpu
from jax.sharding import PartitionSpec as P


BF16 = jnp.bfloat16
F32 = jnp.float32
LANES = 128
MIB = 1 << 20
CHUNKS = 2
VMEM = pl.BlockSpec(memory_space=pltpu.VMEM)
HBM = pl.BlockSpec(memory_space=pltpu.HBM)


def real_dft_tables(block):
    period = 2 * block
    freq = np.arange(block)[:, None]
    place = np.arange(block)[None, :]
    angle = (freq * place % period) * (2.0 * math.pi / period)
    lower = -np.sin(angle)
    lower[0] = 1.0 - 2.0 * (np.arange(block) % 2)
    forward = np.concatenate([np.cos(angle), lower], axis=0)
    out_place = np.arange(block)[:, None] + block
    freq_row = np.arange(block)[None, :]
    angle_out = (out_place * freq_row % period) * (2.0 * math.pi / period)
    weight = np.where(freq_row == 0, 1.0, 2.0)
    lower_out = -np.sin(angle_out) * weight
    lower_out[:, 0] = 1.0 - 2.0 * (np.arange(block) % 2)
    inverse = np.concatenate([np.cos(angle_out) * weight, lower_out], axis=1) / period
    return forward.astype(ml_dtypes.bfloat16), inverse.astype(ml_dtypes.bfloat16)


def call(kernel, out, operands, limit, flops, moved, scratch=()):
    return pl.pallas_call(
        kernel,
        out_shape=out,
        in_specs=[VMEM] * len(operands),
        out_specs=jax.tree.map(lambda _: VMEM, out),
        scratch_shapes=scratch,
        compiler_params=pltpu.CompilerParams(vmem_limit_bytes=limit * MIB),
        cost_estimate=pl.CostEstimate(flops=flops, bytes_accessed=moved, transcendentals=0),
    )(*operands)


def chan_sources():
    n_chan, chan = lax.axis_size("chan"), lax.axis_index("chan")
    sources = [chan, chan ^ 1]
    for hop in range(1, n_chan // 2):
        far = (chan - 2 * hop + n_chan) % n_chan
        sources += [far, far ^ 1]
    return sources


def paired(n):
    return n & (n - 1) == 0


def target(me, k, n):
    return me ^ k if paired(n) else (me + k) % n


def origin(me, k, n):
    return me ^ k if paired(n) else (me - k + n) % n


def mirror(k, n):
    return k if paired(n) else -k % n


def rows_at(first, count):
    return pl.ds(pl.multiple_of(first * count, count), count)


def halves_kernel(x_ref, *refs):
    outs, sems = refs[:-1], refs[-1]
    rows = outs[0].shape[0]
    copies = [
        pltpu.make_async_copy(x_ref.at[c * rows : (c + 1) * rows], out, sems.at[c]) for c, out in enumerate(outs)
    ]
    for copy in copies:
        copy.start()
    for copy in copies:
        copy.wait()


def halves(x):
    out = [jax.ShapeDtypeStruct((x.shape[0] // CHUNKS, x.shape[1]), x.dtype)] * CHUNKS
    return pl.pallas_call(
        halves_kernel,
        out_shape=out,
        in_specs=[HBM],
        out_specs=[VMEM] * CHUNKS,
        scratch_shapes=[pltpu.SemaphoreType.DMA((CHUNKS,))],
        compiler_params=pltpu.CompilerParams(vmem_limit_bytes=2 * MIB),
        cost_estimate=pl.CostEstimate(flops=0, bytes_accessed=4 * x.size, transcendentals=0),
        name="halves",
    )(pltpu.with_memory_space_constraint(x, pltpu.HBM))


def prologue_kernel(
    width, skip_hbm, fwd_hbm, inv_hbm, taps_ref, w_ref, fwd_ref, inv_ref, kv_ref, out_ref, skip_out, skip_ref, taps_in, prev_ref, sems
):
    block = inv_ref.shape[0]
    cols = rows_at(lax.axis_index("ctx"), width)
    copies = [
        pltpu.make_async_copy(skip_hbm, skip_ref, sems.at[4]),
        pltpu.make_async_copy(fwd_hbm, fwd_ref, sems.at[0]),
        pltpu.make_async_copy(taps_ref.at[:, cols], taps_in, sems.at[1]),
        pltpu.make_async_copy(inv_hbm, inv_ref, sems.at[2]),
        pltpu.make_async_copy(w_ref.at[1:3], kv_ref, sems.at[3]),
    ]
    for copy in copies:
        copy.start()
    prev_ref[...] = jnp.zeros_like(prev_ref)
    for copy in copies[:3]:
        copy.wait()
    for k in range(skip_out.shape[0]):
        skip_out[k, :] = skip_ref[k * width : (k + 1) * width]

    @pl.loop(0, out_ref.shape[0])
    def _(k):
        now = jnp.dot(fwd_ref[...], taps_in[rows_at(k, block), :], preferred_element_type=F32)
        parity = lax.broadcasted_iota(jnp.int32, now.shape, 0) % 2
        out_ref[k] = prev_ref[...] + jnp.where(parity == 0, now, -now)
        prev_ref[...] = now

    for copy in copies[3:]:
        copy.wait()


def prologue(tables, skip, taps, w, n_ctx):
    rows, block = tables[0].shape
    width = w.shape[2] // n_ctx
    count = taps.shape[0] // block
    out = [
        *(jax.ShapeDtypeStruct(t.shape, BF16) for t in tables),
        jax.ShapeDtypeStruct((2, *w.shape[1:]), BF16),
        jax.ShapeDtypeStruct((count, rows, width), F32),
        jax.ShapeDtypeStruct((n_ctx, width), F32),
    ]
    return pl.pallas_call(
        functools.partial(prologue_kernel, width),
        out_shape=out,
        in_specs=[HBM] * 5,
        out_specs=[VMEM] * len(out),
        scratch_shapes=[
            pltpu.VMEM(skip.shape, F32),
            pltpu.VMEM((taps.shape[0], width), BF16),
            pltpu.VMEM((rows, width), F32),
            pltpu.SemaphoreType.DMA((5,)),
        ],
        compiler_params=pltpu.CompilerParams(vmem_limit_bytes=6 * MIB),
        cost_estimate=pl.CostEstimate(
            flops=2 * count * rows * block * width,
            bytes_accessed=2 * w.size + count * width * (rows * 4 + block * 2),
            transcendentals=0,
        ),
        name="prologue",
    )(*(pltpu.with_memory_space_constraint(x, pltpu.HBM) for x in (skip, *tables, taps, w)))


def kv_kernel(which, starts, n_ctx, has_before, slices, w_ref, *refs):
    pieces, refs = refs[: len(which)], refs[len(which) :]
    before, outs = (refs[:2], refs[2:]) if has_before else ((), refs)
    tokens = outs[0].shape[0]
    width = w_ref.shape[2] // n_ctx
    depth = pieces[0].shape[1]
    me = lax.axis_index("ctx")
    sources = chan_sources()
    for k in slices or range(n_ctx):
        cols = rows_at(target(me, k, n_ctx), width)
        mine = slice(k * width, (k + 1) * width)
        key, value = (ref[:, mine] for ref in before) if has_before else (None, None)
        for piece, j, start in zip(pieces, which, starts):
            x = piece[start : start + tokens, :]
            rows = rows_at(sources[j], depth)
            a = jnp.dot(x, w_ref[0, rows, cols], preferred_element_type=F32)
            b = jnp.dot(x, w_ref[1, rows, cols], preferred_element_type=F32)
            key = a if key is None else key + a
            value = b if value is None else value + b
        if slices:
            outs[slices.index(k)][...] = (key * value).astype(BF16)
        else:
            outs[0][:, mine] = key
            outs[1][:, mine] = value


def keys_values(pieces, which, starts, tokens, w, before, n_ctx, slices=()):
    channels = w.shape[2]
    share = len(which) * pieces[0].shape[1]
    if slices:
        out = [jax.ShapeDtypeStruct((tokens, channels // n_ctx), BF16)] * len(slices)
    else:
        out = [jax.ShapeDtypeStruct((tokens, channels), F32)] * 2
    return call(
        functools.partial(kv_kernel, tuple(which), tuple(starts), n_ctx, bool(before), slices),
        out,
        [w, *(pieces[j] for j in which), *before],
        6,
        4 * tokens * share * channels * (len(slices) or n_ctx) // n_ctx,
        4 * share * channels + 2 * tokens * share,
    )


def query_kernel(starts, n_ctx, load, w_ref, *refs):
    pieces, refs = refs[: len(starts)], refs[len(starts) :]
    out_ref, acc_ref = refs[0], refs[-1]
    tokens = out_ref.shape[0]
    depth = pieces[0].shape[1]
    width = out_ref.shape[1] // n_ctx
    me = lax.axis_index("ctx")
    rows = [rows_at(source, depth) for source in chan_sources()]
    copies = []
    if load:
        kept_ref, sems = refs[1:3]
        copies = [
            pltpu.make_async_copy(w_ref.at[0, r], kept_ref.at[r], sems.at[j]) for j, r in enumerate(rows)
        ]
        w_ref = kept_ref
    for copy in copies:
        copy.start()
    for j, piece in enumerate(pieces):
        if load:
            copies[j].wait()
        for k in range(n_ctx):
            mine = slice(k * width, (k + 1) * width)
            x = piece[starts[j] : starts[j] + tokens, :]
            cols = rows_at(target(me, k, n_ctx), width)
            a = jnp.dot(x, w_ref[rows[j], cols], preferred_element_type=F32)
            if j > 0:
                a = acc_ref[:, mine] + a
            if j < len(pieces) - 1:
                acc_ref[:, mine] = a
            else:
                out_ref[:, mine] = a.astype(BF16)


def queries(pieces, starts, tokens, w, n_ctx, load):
    total, channels = w.shape[-2:]
    out = [jax.ShapeDtypeStruct((tokens, channels), BF16)]
    scratch = [pltpu.VMEM((tokens, channels), F32)]
    if load:
        w = pltpu.with_memory_space_constraint(w, pltpu.HBM)
        out.append(jax.ShapeDtypeStruct((total, channels), BF16))
        scratch.insert(0, pltpu.SemaphoreType.DMA((len(pieces),)))
    return pl.pallas_call(
        functools.partial(query_kernel, tuple(starts), n_ctx, load),
        out_shape=out,
        in_specs=[HBM if load else VMEM] + [VMEM] * len(pieces),
        out_specs=[VMEM] * len(out),
        scratch_shapes=scratch,
        compiler_params=pltpu.CompilerParams(vmem_limit_bytes=6 * MIB),
        cost_estimate=pl.CostEstimate(
            flops=2 * tokens * total * channels,
            bytes_accessed=2 * total * channels + 2 * tokens * total,
            transcendentals=0,
        ),
        name="q_projection",
    )(w, *pieces)


def block_products(g_ref, x_ref, before_ref, after_ref, plan, width, block):
    lags = sorted({lag for _, _, terms in plan for lag, _ in terms})
    slots = sorted({slot for _, _, terms in plan for _, slot in terms})

    def tile(i, first):
        upper = pl.ds(i * 8, 8) if first else rows_at(i, 8)
        lower = pl.ds(block + i * 8, 8) if first else rows_at(block // 8 + i, 8)
        for lane in range(width // LANES):
            cols = pl.ds(lane * LANES, LANES)
            g_re = {b: g_ref[b, upper, cols] for b in lags}
            g_im = {b: g_ref[b, lower, cols] for b in lags}
            x_re = {b: x_ref[b, upper, cols] for b in slots}
            x_im = {b: x_ref[b, lower, cols] for b in slots}
            g_di = g_re
            if first:
                edge = lax.broadcasted_iota(jnp.int32, (8, LANES), 0) == 0
                g_di = {b: jnp.where(edge, g_im[b], g_re[b]) for b in lags}
                g_im = {b: jnp.where(edge, 0.0, g_im[b]) for b in lags}
            for start, end, terms in plan:
                re = im = None
                if start is not None:
                    re, im = before_ref[start, upper, cols], before_ref[start, lower, cols]
                for lag, slot in terms:
                    up = g_re[lag] * x_re[slot] - g_im[lag] * x_im[slot]
                    down = g_di[lag] * x_im[slot] + g_im[lag] * x_re[slot]
                    re = up if re is None else re + up
                    im = down if im is None else im + down
                after_ref[end, upper, cols] = re
                after_ref[end, lower, cols] = im

    tile(0, True)
    pl.loop(1, block // 8)(lambda i: tile(i, False))


def forward_dft(n_ctx, fwd_ref, ins, x_ref):
    me = lax.axis_index("ctx")
    for k in range(n_ctx):
        x_ref[origin(me, k, n_ctx)] = jnp.dot(fwd_ref[...], ins[k][...], preferred_element_type=F32)


def inverse_dft(n_ctx, inv_ref, y_ref, outs):
    me = lax.axis_index("ctx")
    tokens = outs[0].shape[0]
    for p in range(len(outs) // n_ctx):
        for k in range(n_ctx):
            spectrum = y_ref[target(me, k, n_ctx)].astype(BF16)
            part = inv_ref[p * tokens : (p + 1) * tokens, :]
            outs[p * n_ctx + k][...] = jnp.dot(part, spectrum, preferred_element_type=F32).astype(BF16)


def early_kernel(n_ctx, fwd_ref, g_ref, *refs):
    ins, sum_ref, x_ref = refs[:n_ctx], refs[n_ctx], refs[n_ctx + 1]
    blocks, rows, width = g_ref.shape
    forward_dft(n_ctx, fwd_ref, ins, x_ref)
    plan = [(None, b, [(b - a, a // 2) for a in range(0, b + 1, 2)]) for b in range(blocks)]
    block_products(g_ref, x_ref, None, sum_ref, plan, width, rows // 2)


def middle_kernel(n_ctx, fwd_ref, inv_ref, g_ref, sum_ref, *refs):
    ins, x_ref, outs, y_ref = refs[:n_ctx], refs[n_ctx], refs[n_ctx + 1 : -1], refs[-1]
    blocks, rows, width = g_ref.shape
    forward_dft(n_ctx, fwd_ref, ins, x_ref)
    plan = [(b, b // 2, [(b - a, a // 2) for a in range(1, b, 2)]) for b in range(0, blocks, 2)]
    block_products(g_ref, x_ref, sum_ref, y_ref, plan, width, rows // 2)
    inverse_dft(n_ctx, inv_ref, y_ref, outs)


def late_kernel(n_ctx, inv_ref, g_ref, sum_ref, x_ref, *refs):
    outs, y_ref = refs[:-1], refs[-1]
    blocks, rows, width = g_ref.shape
    plan = [(b, b // 2, [(b - a, a // 2) for a in range(1, b + 1, 2)]) for b in range(1, blocks, 2)]
    block_products(g_ref, x_ref, sum_ref, y_ref, plan, width, rows // 2)
    inverse_dft(n_ctx, inv_ref, y_ref, outs)


def convolve(forward, inverse, spectra, arrived, n_ctx):
    blocks, rows, width = spectra.shape
    half = (n_ctx, rows, width)
    piece = jax.ShapeDtypeStruct((rows // 4, width), BF16)
    flops, moved = blocks * rows * rows * width // 2, blocks * rows * width * 8
    sums = call(
        functools.partial(early_kernel, n_ctx),
        jax.ShapeDtypeStruct(spectra.shape, F32),
        [forward, spectra, *arrived[0]],
        6,
        flops,
        moved,
        [pltpu.VMEM(half, F32)],
    )
    x, *even = call(
        functools.partial(middle_kernel, n_ctx),
        [jax.ShapeDtypeStruct(half, F32)] + [piece] * (2 * n_ctx),
        [forward, inverse, spectra, sums, *arrived[1]],
        6,
        flops,
        moved,
        [pltpu.VMEM(half, F32)],
    )
    odd = call(
        functools.partial(late_kernel, n_ctx),
        [piece] * (2 * n_ctx),
        [inverse, spectra, sums, x],
        6,
        flops,
        moved,
        [pltpu.VMEM(half, F32)],
    )
    return even[:n_ctx], even[n_ctx:], odd[:n_ctx], odd[n_ctx:]


def gate_kernel(n_ctx, start, skip_ref, q_ref, *refs):
    mixed, conv, out_ref = refs[:n_ctx], refs[n_ctx : 2 * n_ctx], refs[-1]
    tokens, width = conv[0].shape
    rows = slice(start, start + tokens)
    me = lax.axis_index("ctx")
    for m in range(n_ctx):
        cols = slice(m * width, (m + 1) * width)
        skip = skip_ref[pl.ds(target(me, m, n_ctx), 1), :]
        query = q_ref[rows, cols].astype(F32)
        total = conv[mirror(m, n_ctx)][...].astype(F32) + skip * mixed[m][rows, :].astype(F32)
        out_ref[:, cols] = (query * total).astype(BF16)


def gate(skip, query, mixed, conv, start, n_ctx):
    shape = (conv[0].shape[0], query.shape[1])
    return call(
        functools.partial(gate_kernel, n_ctx, start),
        jax.ShapeDtypeStruct(shape, BF16),
        [skip, query, *mixed, *conv],
        4,
        3 * shape[0] * shape[1],
        8 * shape[0] * shape[1],
    )


def out_kernel(which, parts, has_before, n_ctx, columns, row, w_ref, *refs):
    pieces, out_ref = refs[: len(which) * parts], refs[-1 if row is None else -3]
    width = pieces[0].shape[1] // n_ctx
    me = lax.axis_index("ctx")
    sources = chan_sources()
    copies = []
    for i in range(w_ref.shape[1] // columns):
        cols = slice(i * columns, (i + 1) * columns)
        acc = refs[len(pieces)][:, cols] if has_before else None
        for i_piece, j in enumerate(which):
            for m in range(n_ctx):
                w = w_ref[rows_at(sources[j] * n_ctx + target(me, m, n_ctx), width), cols]
                mine = slice(m * width, (m + 1) * width)
                group = pieces[i_piece * parts : (i_piece + 1) * parts]
                x = jnp.concatenate([p[:, mine] for p in group], axis=0)
                a = jnp.dot(x, w, preferred_element_type=F32)
                acc = a if acc is None else acc + a
        if row is None:
            out_ref[:, cols] = acc
            continue
        made_ref, sems = refs[-2:]
        made_ref[:, cols] = acc.astype(BF16)
        there = out_ref.at[row : row + made_ref.shape[0], cols]
        copies.append(pltpu.make_async_copy(made_ref.at[:, cols], there, sems.at[i]))
        copies[-1].start()
    for copy in copies:
        copy.wait()


def project_out(gathered, which, w, before, n_ctx, final=None, columns=256):
    parts = len(gathered)
    tokens = sum(pieces[0].shape[0] for pieces in gathered)
    _, out_width = w.shape
    operands = [w, *(pieces[j] for j in which for pieces in gathered)] + ([] if before is None else [before])
    specs = [VMEM] * len(operands)
    aliases, scratch, row = {}, [], None
    out_spec, shape = VMEM, (tokens, out_width)
    if final is not None:
        row, rows, so_far = final
        out_spec, shape = HBM, (rows, out_width)
        scratch = [pltpu.VMEM((tokens, out_width), BF16), pltpu.SemaphoreType.DMA((out_width // columns,))]
        if so_far is not None:
            specs.append(HBM)
            aliases = {len(operands): 0}
            operands.append(so_far)
    share = len(which) * gathered[0][0].shape[1]
    return pl.pallas_call(
        functools.partial(out_kernel, tuple(which), parts, before is not None, n_ctx, columns, row),
        out_shape=jax.ShapeDtypeStruct(shape, F32 if final is None else BF16),
        in_specs=specs,
        out_specs=out_spec,
        scratch_shapes=scratch,
        input_output_aliases=aliases,
        compiler_params=pltpu.CompilerParams(vmem_limit_bytes=6 * MIB),
        cost_estimate=pl.CostEstimate(
            flops=2 * tokens * share * out_width,
            bytes_accessed=2 * share * out_width + 2 * tokens * (share + out_width),
            transcendentals=0,
        ),
        name="out_projection",
    )(*operands)


def shift(x, axis, by):
    n = lax.axis_size(axis)
    return lax.ppermute(x, axis, [(i, (i + by) % n) for i in range(n)])


def swap_cores(x):
    n = lax.axis_size("chan")
    return lax.ppermute(x, "chan", [(i, i ^ 1) for i in range(n)])


def gather_far(x):
    pieces = []
    for hop in range(1, lax.axis_size("chan") // 2):
        far = shift(x, "chan", 2 * hop)
        pieces += [far, swap_cores(far)]
    return pieces


def exchange(parts):
    out, n = [parts[0]], len(parts)
    for k in range(1, n):
        out.append(lax.ppermute(parts[k], "ctx", [(i, target(i, k, n)) for i in range(n)]))
    return out


def layer(features, filter_taps, skip_gain, in_weight, out_weight):
    return layer_body(features, filter_taps, skip_gain, in_weight, out_weight)


def layer_body(features, filter_taps, skip_gain, in_weight, out_weight):
    n_ctx = lax.axis_size("ctx")
    rows = features.shape[0]
    tokens = rows // CHUNKS
    tables = [jnp.asarray(t) for t in real_dft_tables(tokens)]
    w = in_weight.transpose(1, 0, 2)

    own = halves(features)
    far = [gather_far(own[c]) for c in range(CHUNKS)]
    near = swap_cores(features)
    forward, inverse, w_kv, spectra, skip = prologue(tables, skip_gain, filter_taps, w, n_ctx)

    mixed, arrived, query, w_q = [], [], [], None
    for c in range(CHUNKS):
        pieces = [own[c], near, *far[c]]
        starts = [0, c * tokens] + [0] * len(far[c])
        total = ()
        for part, which in ("a", (0, 1)), ("b", range(2, len(pieces) - 1)):
            total = keys_values(pieces, which, [starts[j] for j in which], tokens, w_kv, total, n_ctx)
        last, made = len(pieces) - 1, {}
        for part, slices in ("c", tuple(range(2, n_ctx))), ("d", (1, 0)):
            some = keys_values(pieces, (last,), (starts[last],), tokens, w_kv, total, n_ctx, slices)
            made.update(zip(slices, some))
        mixed.append([made[k] for k in range(n_ctx)])
        arrived.append(exchange(mixed[c]))
        made, *kept = queries(pieces, starts, tokens, w if c == 0 else w_q, n_ctx, c == 0)
        query.append(made)
        w_q = kept[0] if kept else w_q
    conv = convolve(forward, inverse, spectra, arrived, n_ctx)

    gathered = []
    for r in range(2 * CHUNKS):
        c, start = r // 2, r % 2 * (tokens // 2)
        back = exchange(conv[r])
        gated = gate(skip, query[c], mixed[c], back, start, n_ctx)
        beside = swap_cores(gated)
        gathered.append([gated, beside, *gather_far(gated)])
    every = range(len(gathered[0]))
    out = project_out(gathered[:2], every, out_weight, None, n_ctx, (0, rows, None))
    part = project_out(gathered[2:], every[:2], out_weight, None, n_ctx)
    part = project_out(gathered[2:], every[2:-1], out_weight, part, n_ctx)
    return project_out(gathered[2:], every[-1:], out_weight, part, n_ctx, (tokens, rows, out))


P_SIZE = 128


def dft_tables(block_len):
    period = 2 * block_len
    freq_col = jnp.arange(period, dtype=jnp.int32)[:, None]
    place_row = jnp.arange(period, dtype=jnp.int32)[None, :]
    angles = (freq_col * place_row % period).astype(F32) * (2.0 * math.pi / period)
    forward = jnp.concatenate([jnp.cos(angles), -jnp.sin(angles)], axis=0).astype(BF16)
    out_place = jnp.arange(block_len, dtype=jnp.int32)[:, None] + block_len
    angle_out = (out_place * place_row % period).astype(F32) * (2.0 * math.pi / period)
    inverse = (jnp.concatenate([jnp.cos(angle_out), -jnp.sin(angle_out)], axis=1) / period).astype(BF16)
    return (forward, inverse)


def plain_layer(features, filter_taps, skip_gain, in_weight, out_weight):
    forward, inverse = dft_tables(P_SIZE)
    channels = in_weight.shape[2]
    tok_rows = features.shape[0]
    per_dev = tok_rows // P_SIZE
    period = 2 * P_SIZE
    total_blocks = per_dev * lax.axis_size("ctx")
    first_mine = lax.axis_index("ctx") * per_dev
    padded = jnp.concatenate([jnp.zeros((P_SIZE, channels), BF16), filter_taps], axis=0)
    tap_blocks = padded.reshape(total_blocks + 1, P_SIZE, channels)
    segments = jnp.concatenate([tap_blocks[:-1], tap_blocks[1:]], axis=1)
    lag = jnp.einsum("fn,knc->kfc", forward, segments, preferred_element_type=F32).astype(BF16)
    flipped = jnp.concatenate([lag[::-1], jnp.zeros_like(lag)], axis=0)
    gathered = lax.all_gather(features, "chan", axis=1, tiled=True)
    w = in_weight.transpose(1, 0, 2)
    q, k, v = (jnp.dot(gathered, w[s], preferred_element_type=F32) for s in range(3))
    query = q.astype(BF16)
    mixed = (k * v).astype(BF16)
    everyone = lax.all_gather(mixed, "ctx", axis=0, tiled=True).reshape(total_blocks, P_SIZE, channels)
    source = jnp.einsum("fp,bpc->bfc", forward[:, :P_SIZE], everyone, preferred_element_type=F32)
    source = source.astype(BF16).astype(F32)
    source_re, source_im = source[:, :period], source[:, period:]
    outputs = []
    for out_block in range(per_dev):
        start = total_blocks - 1 - (first_mine + out_block)
        window = lax.dynamic_slice_in_dim(flipped, start, total_blocks, 0).astype(F32)
        lag_re, lag_im = window[:, :period], window[:, period:]
        out_re = jnp.sum(lag_re * source_re - lag_im * source_im, axis=0)
        out_im = jnp.sum(lag_re * source_im + lag_im * source_re, axis=0)
        outputs.append(jnp.concatenate([out_re, out_im], axis=0))
    spectra = jnp.stack(outputs).astype(BF16)
    conv = jnp.einsum("tf,bfc->btc", inverse, spectra, preferred_element_type=F32)
    conv = conv.reshape(tok_rows, channels)
    gated = (query.astype(F32) * (conv + skip_gain[None, :] * mixed.astype(F32))).astype(BF16)
    everything = lax.all_gather(gated, "chan", axis=1, tiled=True)
    return jnp.dot(everything, out_weight, preferred_element_type=F32).astype(BF16)


def shards(features, filter_taps, skip_gain, in_weight, out_weight):
    slices = in_weight.shape[2] % (lax.axis_size("ctx") * LANES) == 0
    cores = lax.axis_size("chan") % 2 == 0 and lax.axis_size("chan") > 2
    blocks = features.shape[0] % (CHUNKS * LANES) == 0
    chosen = layer if slices and cores and blocks else plain_layer
    return chosen(features, filter_taps, skip_gain, in_weight, out_weight)


def solution(mesh):
    return jax.shard_map(
        shards,
        mesh=mesh,
        in_specs=(
            P(("grp", "ctx"), "chan"),
            P(None, "chan"),
            P("chan"),
            P(None, None, "chan"),
            P(None, "chan"),
        ),
        out_specs=P(("grp", "ctx"), "chan"),
        check_vma=False,
    )
```

```python
import functools
import math

import jax
import jax.numpy as jnp
import ml_dtypes
import numpy as np
from jax import lax
from jax.experimental import pallas as pl
from jax.experimental.pallas import tpu as pltpu
from jax.sharding import PartitionSpec as P


BF16 = jnp.bfloat16
F32 = jnp.float32
LANES = 128
MIB = 1 << 20
CHUNKS = 2
PARTS = 2
VMEM = pl.BlockSpec(memory_space=pltpu.VMEM)
HBM = pl.BlockSpec(memory_space=pltpu.HBM)


def real_dft_tables(block):
    period = 2 * block
    freq = np.arange(block)[:, None]
    place = np.arange(block)[None, :]
    angle = (freq * place % period) * (2.0 * math.pi / period)
    lower = -np.sin(angle)
    lower[0] = 1.0 - 2.0 * (np.arange(block) % 2)
    forward = np.concatenate([np.cos(angle), lower], axis=0)
    out_place = np.arange(block)[:, None] + block
    freq_row = np.arange(block)[None, :]
    angle_out = (out_place * freq_row % period) * (2.0 * math.pi / period)
    weight = np.where(freq_row == 0, 1.0, 2.0)
    lower_out = -np.sin(angle_out) * weight
    lower_out[:, 0] = 1.0 - 2.0 * (np.arange(block) % 2)
    inverse = np.concatenate([np.cos(angle_out) * weight, lower_out], axis=1) / period
    return forward.astype(ml_dtypes.bfloat16), inverse.astype(ml_dtypes.bfloat16)


def call(kernel, out, operands, limit, flops, moved, scratch=()):
    return pl.pallas_call(
        kernel,
        out_shape=out,
        in_specs=[VMEM] * len(operands),
        out_specs=jax.tree.map(lambda _: VMEM, out),
        scratch_shapes=scratch,
        compiler_params=pltpu.CompilerParams(vmem_limit_bytes=limit * MIB),
        cost_estimate=pl.CostEstimate(flops=flops, bytes_accessed=moved, transcendentals=0),
    )(*operands)


def chan_sources():
    n_chan, chan = lax.axis_size("chan"), lax.axis_index("chan")
    sources = [chan, chan ^ 1]
    for hop in range(1, n_chan // 2):
        far = (chan - 2 * hop + n_chan) % n_chan
        sources += [far, far ^ 1]
    return sources


def paired(n):
    return n & (n - 1) == 0


def target(me, k, n):
    return me ^ k if paired(n) else (me + k) % n


def origin(me, k, n):
    return me ^ k if paired(n) else (me - k + n) % n


def mirror(k, n):
    return k if paired(n) else -k % n


def rows_at(first, count):
    return pl.ds(pl.multiple_of(first * count, count), count)


def halves_kernel(x_ref, *refs):
    outs, sems = refs[:-1], refs[-1]
    rows = outs[0].shape[0]
    copies = [
        pltpu.make_async_copy(x_ref.at[c * rows : (c + 1) * rows], out, sems.at[c]) for c, out in enumerate(outs)
    ]
    for copy in copies:
        copy.start()
    for copy in copies:
        copy.wait()


def halves(x):
    out = [jax.ShapeDtypeStruct((x.shape[0] // CHUNKS, x.shape[1]), x.dtype)] * CHUNKS
    return pl.pallas_call(
        halves_kernel,
        out_shape=out,
        in_specs=[HBM],
        out_specs=[VMEM] * CHUNKS,
        scratch_shapes=[pltpu.SemaphoreType.DMA((CHUNKS,))],
        compiler_params=pltpu.CompilerParams(vmem_limit_bytes=2 * MIB),
        cost_estimate=pl.CostEstimate(flops=0, bytes_accessed=4 * x.size, transcendentals=0),
        name="halves",
    )(pltpu.with_memory_space_constraint(x, pltpu.HBM))


def prologue_kernel(
    width, skip_hbm, fwd_hbm, inv_hbm, taps_ref, w_ref, fwd_ref, inv_ref, kv_ref, query_ref, out_ref, skip_out, skip_ref, taps_in, prev_ref, sems
):
    block = inv_ref.shape[0]
    cols = rows_at(lax.axis_index("ctx"), width)
    copies = [
        pltpu.make_async_copy(skip_hbm, skip_ref, sems.at[4]),
        pltpu.make_async_copy(fwd_hbm, fwd_ref, sems.at[0]),
        pltpu.make_async_copy(taps_ref.at[:, cols], taps_in, sems.at[1]),
        pltpu.make_async_copy(inv_hbm, inv_ref, sems.at[2]),
        pltpu.make_async_copy(w_ref.at[1:3], kv_ref, sems.at[3]),
        pltpu.make_async_copy(w_ref.at[0], query_ref, sems.at[5]),
    ]
    for copy in copies:
        copy.start()
    prev_ref[...] = jnp.zeros_like(prev_ref)
    for copy in copies[:3]:
        copy.wait()
    for k in range(skip_out.shape[0]):
        skip_out[k, :] = skip_ref[k * width : (k + 1) * width]

    @pl.loop(0, out_ref.shape[0])
    def _(k):
        now = jnp.dot(fwd_ref[...], taps_in[rows_at(k, block), :], preferred_element_type=F32)
        parity = lax.broadcasted_iota(jnp.int32, now.shape, 0) % 2
        out_ref[k] = prev_ref[...] + jnp.where(parity == 0, now, -now)
        prev_ref[...] = now

    for copy in copies[3:]:
        copy.wait()


def prologue(tables, skip, taps, w, n_ctx):
    rows, block = tables[0].shape
    width = w.shape[2] // n_ctx
    count = taps.shape[0] // block
    out = [
        *(jax.ShapeDtypeStruct(t.shape, BF16) for t in tables),
        jax.ShapeDtypeStruct((2, *w.shape[1:]), BF16),
        jax.ShapeDtypeStruct(w.shape[1:], BF16),
        jax.ShapeDtypeStruct((count, rows, width), F32),
        jax.ShapeDtypeStruct((n_ctx, width), F32),
    ]
    return pl.pallas_call(
        functools.partial(prologue_kernel, width),
        out_shape=out,
        in_specs=[HBM] * 5,
        out_specs=[VMEM] * len(out),
        scratch_shapes=[
            pltpu.VMEM(skip.shape, F32),
            pltpu.VMEM((taps.shape[0], width), BF16),
            pltpu.VMEM((rows, width), F32),
            pltpu.SemaphoreType.DMA((6,)),
        ],
        compiler_params=pltpu.CompilerParams(vmem_limit_bytes=6 * MIB),
        cost_estimate=pl.CostEstimate(
            flops=2 * count * rows * block * width,
            bytes_accessed=2 * w.size + count * width * (rows * 4 + block * 2),
            transcendentals=0,
        ),
        name="prologue",
    )(*(pltpu.with_memory_space_constraint(x, pltpu.HBM) for x in (skip, *tables, taps, w)))


def kv_kernel(which, starts, n_ctx, has_before, slices, parts, w_ref, *refs):
    pieces, refs = refs[: len(which)], refs[len(which) :]
    before, outs = (refs[:2], refs[2:]) if has_before else ((), refs)
    tokens = outs[0].shape[0]
    width = w_ref.shape[2] // n_ctx
    depth = pieces[0].shape[1]
    me = lax.axis_index("ctx")
    sources = chan_sources()
    for k in slices or range(n_ctx):
        cols = rows_at(target(me, k, n_ctx), width)
        mine = slice(k * width, (k + 1) * width)
        key, value = (ref[:, mine] for ref in before) if has_before else (None, None)
        for piece, j, start in zip(pieces, which, starts):
            x = piece[start : start + tokens, :]
            rows = rows_at(sources[j], depth)
            a = jnp.dot(x, w_ref[0, rows, cols], preferred_element_type=F32)
            b = jnp.dot(x, w_ref[1, rows, cols], preferred_element_type=F32)
            key = a if key is None else key + a
            value = b if value is None else value + b
        if slices:
            made = (key * value).astype(BF16)
            for p in range(parts):
                cut = slice(p * width // parts, (p + 1) * width // parts)
                outs[slices.index(k) * parts + p][...] = made[:, cut]
        else:
            outs[0][:, mine] = key
            outs[1][:, mine] = value


def keys_values(pieces, which, starts, tokens, w, before, n_ctx, slices=(), parts=1):
    channels = w.shape[2]
    share = len(which) * pieces[0].shape[1]
    if slices:
        out = [jax.ShapeDtypeStruct((tokens, channels // n_ctx // parts), BF16)] * (len(slices) * parts)
    else:
        out = [jax.ShapeDtypeStruct((tokens, channels), F32)] * 2
    return call(
        functools.partial(kv_kernel, tuple(which), tuple(starts), n_ctx, bool(before), slices, parts),
        out,
        [w, *(pieces[j] for j in which), *before],
        6,
        4 * tokens * share * channels * (len(slices) or n_ctx) // n_ctx,
        4 * share * channels + 2 * tokens * share,
    )


def query_kernel(starts, n_ctx, w_ref, *refs):
    pieces, out_ref = refs[:-1], refs[-1]
    tokens = out_ref.shape[0]
    depth = pieces[0].shape[1]
    width = out_ref.shape[1] // n_ctx
    me = lax.axis_index("ctx")
    rows = [rows_at(source, depth) for source in chan_sources()]
    for k in range(n_ctx):
        cols = rows_at(target(me, k, n_ctx), width)
        acc = None
        for j, piece in enumerate(pieces):
            x = piece[starts[j] : starts[j] + tokens, :]
            a = jnp.dot(x, w_ref[rows[j], cols], preferred_element_type=F32)
            acc = a if acc is None else acc + a
        out_ref[:, k * width : (k + 1) * width] = acc.astype(BF16)


def queries(pieces, starts, tokens, w, n_ctx):
    total, channels = w.shape
    return call(
        functools.partial(query_kernel, tuple(starts), n_ctx),
        jax.ShapeDtypeStruct((tokens, channels), BF16),
        [w, *pieces],
        6,
        2 * tokens * total * channels,
        2 * total * channels + 2 * tokens * total,
    )


def block_products(g_ref, x_ref, before_ref, after_ref, plan, start, block):
    lags = sorted({lag for _, _, terms in plan for lag, _ in terms})
    slots = sorted({slot for _, _, terms in plan for _, slot in terms})

    def tile(i, first):
        upper = pl.ds(i * 8, 8) if first else rows_at(i, 8)
        lower = pl.ds(block + i * 8, 8) if first else rows_at(block // 8 + i, 8)
        for lane in range(x_ref.shape[2] // LANES):
            cols, own = pl.ds(start + lane * LANES, LANES), pl.ds(lane * LANES, LANES)
            g_re = {b: g_ref[b, upper, cols] for b in lags}
            g_im = {b: g_ref[b, lower, cols] for b in lags}
            x_re = {b: x_ref[b, upper, own] for b in slots}
            x_im = {b: x_ref[b, lower, own] for b in slots}
            g_di = g_re
            if first:
                edge = lax.broadcasted_iota(jnp.int32, (8, LANES), 0) == 0
                g_di = {b: jnp.where(edge, g_im[b], g_re[b]) for b in lags}
                g_im = {b: jnp.where(edge, 0.0, g_im[b]) for b in lags}
            for here, end, terms in plan:
                re = im = None
                if here is not None:
                    re, im = before_ref[here, upper, cols], before_ref[here, lower, cols]
                for lag, slot in terms:
                    up = g_re[lag] * x_re[slot] - g_im[lag] * x_im[slot]
                    down = g_di[lag] * x_im[slot] + g_im[lag] * x_re[slot]
                    re = up if re is None else re + up
                    im = down if im is None else im + down
                after_ref[end, upper, own] = re
                after_ref[end, lower, own] = im

    tile(0, True)
    pl.loop(1, block // 8)(lambda i: tile(i, False))


def part_of(ref, start, width):
    return ref[...] if ref.shape[1] == width else ref[:, start : start + width]


def forward_dft(n_ctx, fwd_ref, ins, x_ref, start):
    me = lax.axis_index("ctx")
    for k in range(n_ctx):
        piece = part_of(ins[k], start, x_ref.shape[2])
        x_ref[origin(me, k, n_ctx)] = jnp.dot(fwd_ref[...], piece, preferred_element_type=F32)


def inverse_dft(n_ctx, inv_ref, y_ref, outs):
    me = lax.axis_index("ctx")
    for k in range(n_ctx):
        spectrum = y_ref[target(me, k, n_ctx)].astype(BF16)
        outs[k][...] = jnp.dot(inv_ref[...], spectrum, preferred_element_type=F32).astype(BF16)


def early_kernel(n_ctx, fwd_ref, g_ref, *refs):
    ins, sum_ref, x_ref = refs[:n_ctx], refs[n_ctx], refs[n_ctx + 1]
    blocks, rows, _ = g_ref.shape
    forward_dft(n_ctx, fwd_ref, ins, x_ref, 0)
    plan = [(None, b, [(b - a, a // 2) for a in range(0, b + 1, 2)]) for b in range(blocks)]
    block_products(g_ref, x_ref, None, sum_ref, plan, 0, rows // 2)


def middle_kernel(n_ctx, start, fwd_ref, inv_ref, g_ref, sum_ref, *refs):
    ins, x_ref, outs, y_ref = refs[:n_ctx], refs[n_ctx], refs[n_ctx + 1 : -1], refs[-1]
    blocks, rows, _ = g_ref.shape
    forward_dft(n_ctx, fwd_ref, ins, x_ref, start)
    plan = [(b, b // 2, [(b - a, a // 2) for a in range(1, b, 2)]) for b in range(0, blocks, 2)]
    block_products(g_ref, x_ref, sum_ref, y_ref, plan, start, rows // 2)
    inverse_dft(n_ctx, inv_ref, y_ref, outs)


def late_kernel(n_ctx, start, inv_ref, g_ref, sum_ref, x_ref, *refs):
    outs, y_ref = refs[:-1], refs[-1]
    blocks, rows, _ = g_ref.shape
    plan = [(b, b // 2, [(b - a, a // 2) for a in range(1, b + 1, 2)]) for b in range(1, blocks, 2)]
    block_products(g_ref, x_ref, sum_ref, y_ref, plan, start, rows // 2)
    inverse_dft(n_ctx, inv_ref, y_ref, outs)


def convolve(forward, inverse, spectra, even, odd, n_ctx):
    blocks, rows, width = spectra.shape
    parts = len(odd)
    share = width // parts
    some = (n_ctx, rows, share)
    piece = jax.ShapeDtypeStruct((rows // 2, share), BF16)
    flops, moved = blocks * rows * rows * width // 2, blocks * rows * width * 8
    sums = call(
        functools.partial(early_kernel, n_ctx),
        jax.ShapeDtypeStruct(spectra.shape, F32),
        [forward, spectra, *even],
        6,
        flops,
        moved,
        [pltpu.VMEM((n_ctx, rows, width), F32)],
    )
    first, second = [], []
    for h in range(parts):
        x, *made = call(
            functools.partial(middle_kernel, n_ctx, h * share),
            [jax.ShapeDtypeStruct(some, F32)] + [piece] * n_ctx,
            [forward, inverse, spectra, sums, *odd[h]],
            6,
            flops // parts,
            moved // parts,
            [pltpu.VMEM(some, F32)],
        )
        first.append(made)
        second.append(
            call(
                functools.partial(late_kernel, n_ctx, h * share),
                [piece] * n_ctx,
                [inverse, spectra, sums, x],
                6,
                flops // parts,
                moved // parts,
                [pltpu.VMEM(some, F32)],
            )
        )
    return [*first, *second]


def gate_kernel(n_ctx, start, skip_ref, q_ref, *refs):
    mixed, conv, out_ref = refs[:n_ctx], refs[n_ctx : 2 * n_ctx], refs[-1]
    share, width = conv[0].shape[1], q_ref.shape[1] // n_ctx
    me = lax.axis_index("ctx")
    for m in range(n_ctx):
        skip = skip_ref[pl.ds(target(me, m, n_ctx), 1), :][:, start : start + share]
        query = q_ref[:, m * width + start : m * width + start + share].astype(F32)
        source = part_of(mixed[m], start, share).astype(F32)
        total = conv[mirror(m, n_ctx)][...].astype(F32) + skip * source
        out_ref[:, m * share : (m + 1) * share] = (query * total).astype(BF16)


def gate(skip, query, mixed, conv, start, n_ctx):
    tokens, share = conv[0].shape
    return call(
        functools.partial(gate_kernel, n_ctx, start),
        jax.ShapeDtypeStruct((tokens, share * n_ctx), BF16),
        [skip, query, *mixed, *conv],
        4,
        3 * tokens * share * n_ctx,
        8 * tokens * share * n_ctx,
    )


def out_kernel(which, parts, has_before, n_ctx, columns, row, w_ref, *refs):
    pieces, out_ref = refs[: len(which) * parts], refs[-1 if row is None else -3]
    share = pieces[0].shape[1] // n_ctx
    width = share * parts
    me = lax.axis_index("ctx")
    sources = chan_sources()
    copies = []
    for i in range(w_ref.shape[1] // columns):
        cols = slice(i * columns, (i + 1) * columns)
        acc = refs[len(pieces)][:, cols] if has_before else None
        for i_piece, j in enumerate(which):
            for m in range(n_ctx):
                w = w_ref[rows_at(sources[j] * n_ctx + target(me, m, n_ctx), width), cols]
                mine = slice(m * share, (m + 1) * share)
                group = pieces[i_piece * parts : (i_piece + 1) * parts]
                x = jnp.concatenate([p[:, mine] for p in group], axis=1)
                a = jnp.dot(x, w, preferred_element_type=F32)
                acc = a if acc is None else acc + a
        if row is None:
            out_ref[:, cols] = acc
            continue
        made_ref, sems = refs[-2:]
        made_ref[:, cols] = acc.astype(BF16)
        there = out_ref.at[row : row + made_ref.shape[0], cols]
        copies.append(pltpu.make_async_copy(made_ref.at[:, cols], there, sems.at[i]))
        copies[-1].start()
    for copy in copies:
        copy.wait()


def project_out(gathered, which, w, before, n_ctx, final=None, columns=256):
    parts = len(gathered)
    tokens = gathered[0][0].shape[0]
    _, out_width = w.shape
    operands = [w, *(pieces[j] for j in which for pieces in gathered)] + ([] if before is None else [before])
    specs = [VMEM] * len(operands)
    aliases, scratch, row = {}, [], None
    out_spec, shape = VMEM, (tokens, out_width)
    if final is not None:
        row, rows, so_far = final
        out_spec, shape = HBM, (rows, out_width)
        scratch = [pltpu.VMEM((tokens, out_width), BF16), pltpu.SemaphoreType.DMA((out_width // columns,))]
        if so_far is not None:
            specs.append(HBM)
            aliases = {len(operands): 0}
            operands.append(so_far)
    share = len(which) * parts * gathered[0][0].shape[1]
    return pl.pallas_call(
        functools.partial(out_kernel, tuple(which), parts, before is not None, n_ctx, columns, row),
        out_shape=jax.ShapeDtypeStruct(shape, F32 if final is None else BF16),
        in_specs=specs,
        out_specs=out_spec,
        scratch_shapes=scratch,
        input_output_aliases=aliases,
        compiler_params=pltpu.CompilerParams(vmem_limit_bytes=6 * MIB),
        cost_estimate=pl.CostEstimate(
            flops=2 * tokens * share * out_width,
            bytes_accessed=2 * share * out_width + 2 * tokens * (share + out_width),
            transcendentals=0,
        ),
        name="out_projection",
    )(*operands)


def shift(x, axis, by):
    n = lax.axis_size(axis)
    return lax.ppermute(x, axis, [(i, (i + by) % n) for i in range(n)])


def swap_cores(x):
    n = lax.axis_size("chan")
    return lax.ppermute(x, "chan", [(i, i ^ 1) for i in range(n)])


def gather_far(x):
    pieces = []
    for hop in range(1, lax.axis_size("chan") // 2):
        far = shift(x, "chan", 2 * hop)
        pieces += [far, swap_cores(far)]
    return pieces


def exchange(parts, first=1):
    out, n = list(parts[:first]), len(parts)
    for k in range(first, n):
        out.append(lax.ppermute(parts[k], "ctx", [(i, target(i, k, n)) for i in range(n)]))
    return out


def layer(features, filter_taps, skip_gain, in_weight, out_weight):
    return layer_body(features, filter_taps, skip_gain, in_weight, out_weight)


def layer_body(features, filter_taps, skip_gain, in_weight, out_weight):
    n_ctx = lax.axis_size("ctx")
    rows = features.shape[0]
    tokens = rows // CHUNKS
    tables = [jnp.asarray(t) for t in real_dft_tables(tokens)]
    w = in_weight.transpose(1, 0, 2)

    own = halves(features)
    far = [gather_far(own[c]) for c in range(CHUNKS)]
    near = swap_cores(features)
    forward, inverse, w_kv, w_q, spectra, skip = prologue(tables, skip_gain, filter_taps, w, n_ctx)

    mixed, query = [], []
    for c in range(CHUNKS):
        pieces = [own[c], near, *far[c]]
        starts = [0, c * tokens] + [0] * len(far[c])
        total = ()
        for part, which in ("a", (0, 1)), ("b", range(2, len(pieces) - 1)):
            total = keys_values(pieces, which, [starts[j] for j in which], tokens, w_kv, total, n_ctx)
        last, made = len(pieces) - 1, {}
        for part, slices, cuts in ("c", tuple(range(2, n_ctx)), c + 1), ("d", (1, 0), 1):
            some = keys_values(pieces, (last,), (starts[last],), tokens, w_kv, total, n_ctx, slices, cuts)
            made.update({k: some[i * cuts : (i + 1) * cuts] for i, k in enumerate(slices)})
        mixed.append([[made[k][h % len(made[k])] for k in range(n_ctx)] for h in range(PARTS)])
        query.append(queries(pieces, starts, tokens, w_q, n_ctx))
    even = exchange(mixed[0][0])
    odd = [exchange(mixed[1][0])]
    odd += [odd[0][:2] + exchange(mixed[1][h], 2)[2:] for h in range(1, PARTS)]
    conv = convolve(forward, inverse, spectra, even, odd, n_ctx)

    gathered = []
    for r in range(CHUNKS * PARTS):
        c, h = r // PARTS, r % PARTS
        back = exchange(conv[r])
        gated = gate(skip, query[c], mixed[c][h], back, h * back[0].shape[1], n_ctx)
        beside = swap_cores(gated)
        gathered.append([gated, beside, *gather_far(gated)])
    every = range(len(gathered[0]))
    out = project_out(gathered[:2], every, out_weight, None, n_ctx, (0, rows, None))
    part = project_out(gathered[2:], every[:2], out_weight, None, n_ctx)
    part = project_out(gathered[2:], every[2:-1], out_weight, part, n_ctx)
    return project_out(gathered[2:], every[-1:], out_weight, part, n_ctx, (tokens, rows, out))


P_SIZE = 128


def dft_tables(block_len):
    period = 2 * block_len
    freq_col = jnp.arange(period, dtype=jnp.int32)[:, None]
    place_row = jnp.arange(period, dtype=jnp.int32)[None, :]
    angles = (freq_col * place_row % period).astype(F32) * (2.0 * math.pi / period)
    forward = jnp.concatenate([jnp.cos(angles), -jnp.sin(angles)], axis=0).astype(BF16)
    out_place = jnp.arange(block_len, dtype=jnp.int32)[:, None] + block_len
    angle_out = (out_place * place_row % period).astype(F32) * (2.0 * math.pi / period)
    inverse = (jnp.concatenate([jnp.cos(angle_out), -jnp.sin(angle_out)], axis=1) / period).astype(BF16)
    return (forward, inverse)


def plain_layer(features, filter_taps, skip_gain, in_weight, out_weight):
    forward, inverse = dft_tables(P_SIZE)
    channels = in_weight.shape[2]
    tok_rows = features.shape[0]
    per_dev = tok_rows // P_SIZE
    period = 2 * P_SIZE
    total_blocks = per_dev * lax.axis_size("ctx")
    first_mine = lax.axis_index("ctx") * per_dev
    padded = jnp.concatenate([jnp.zeros((P_SIZE, channels), BF16), filter_taps], axis=0)
    tap_blocks = padded.reshape(total_blocks + 1, P_SIZE, channels)
    segments = jnp.concatenate([tap_blocks[:-1], tap_blocks[1:]], axis=1)
    lag = jnp.einsum("fn,knc->kfc", forward, segments, preferred_element_type=F32).astype(BF16)
    flipped = jnp.concatenate([lag[::-1], jnp.zeros_like(lag)], axis=0)
    gathered = lax.all_gather(features, "chan", axis=1, tiled=True)
    w = in_weight.transpose(1, 0, 2)
    q, k, v = (jnp.dot(gathered, w[s], preferred_element_type=F32) for s in range(3))
    query = q.astype(BF16)
    mixed = (k * v).astype(BF16)
    everyone = lax.all_gather(mixed, "ctx", axis=0, tiled=True).reshape(total_blocks, P_SIZE, channels)
    source = jnp.einsum("fp,bpc->bfc", forward[:, :P_SIZE], everyone, preferred_element_type=F32)
    source = source.astype(BF16).astype(F32)
    source_re, source_im = source[:, :period], source[:, period:]
    outputs = []
    for out_block in range(per_dev):
        start = total_blocks - 1 - (first_mine + out_block)
        window = lax.dynamic_slice_in_dim(flipped, start, total_blocks, 0).astype(F32)
        lag_re, lag_im = window[:, :period], window[:, period:]
        out_re = jnp.sum(lag_re * source_re - lag_im * source_im, axis=0)
        out_im = jnp.sum(lag_re * source_im + lag_im * source_re, axis=0)
        outputs.append(jnp.concatenate([out_re, out_im], axis=0))
    spectra = jnp.stack(outputs).astype(BF16)
    conv = jnp.einsum("tf,bfc->btc", inverse, spectra, preferred_element_type=F32)
    conv = conv.reshape(tok_rows, channels)
    gated = (query.astype(F32) * (conv + skip_gain[None, :] * mixed.astype(F32))).astype(BF16)
    everything = lax.all_gather(gated, "chan", axis=1, tiled=True)
    return jnp.dot(everything, out_weight, preferred_element_type=F32).astype(BF16)


def shards(features, filter_taps, skip_gain, in_weight, out_weight):
    slices = lax.axis_size("ctx") > 2 and in_weight.shape[2] % (lax.axis_size("ctx") * PARTS * LANES) == 0
    cores = lax.axis_size("chan") % 2 == 0 and lax.axis_size("chan") > 2
    blocks = features.shape[0] % (CHUNKS * LANES) == 0
    chosen = layer if slices and cores and blocks else plain_layer
    return chosen(features, filter_taps, skip_gain, in_weight, out_weight)


def solution(mesh):
    return jax.shard_map(
        shards,
        mesh=mesh,
        in_specs=(
            P(("grp", "ctx"), "chan"),
            P(None, "chan"),
            P("chan"),
            P(None, None, "chan"),
            P(None, "chan"),
        ),
        out_specs=P(("grp", "ctx"), "chan"),
        check_vma=False,
    )
```

```python
import functools
import math

import jax
import jax.numpy as jnp
import ml_dtypes
import numpy as np
from jax import lax
from jax.experimental import pallas as pl
from jax.experimental.pallas import tpu as pltpu
from jax.sharding import PartitionSpec as P


BF16 = jnp.bfloat16
F32 = jnp.float32
LANES = 128
MIB = 1 << 20
CHUNKS = 2
PARTS = 2
VMEM = pl.BlockSpec(memory_space=pltpu.VMEM)
HBM = pl.BlockSpec(memory_space=pltpu.HBM)


def real_dft_tables(block):
    period = 2 * block
    freq = np.arange(block)[:, None]
    place = np.arange(block)[None, :]
    angle = (freq * place % period) * (2.0 * math.pi / period)
    lower = -np.sin(angle)
    lower[0] = 1.0 - 2.0 * (np.arange(block) % 2)
    forward = np.concatenate([np.cos(angle), lower], axis=0)
    out_place = np.arange(block)[:, None] + block
    freq_row = np.arange(block)[None, :]
    angle_out = (out_place * freq_row % period) * (2.0 * math.pi / period)
    weight = np.where(freq_row == 0, 1.0, 2.0)
    lower_out = -np.sin(angle_out) * weight
    lower_out[:, 0] = 1.0 - 2.0 * (np.arange(block) % 2)
    inverse = np.concatenate([np.cos(angle_out) * weight, lower_out], axis=1) / period
    return forward.astype(ml_dtypes.bfloat16), inverse.astype(ml_dtypes.bfloat16)


def call(kernel, out, operands, limit, flops, moved, scratch=()):
    return pl.pallas_call(
        kernel,
        out_shape=out,
        in_specs=[VMEM] * len(operands),
        out_specs=jax.tree.map(lambda _: VMEM, out),
        scratch_shapes=scratch,
        compiler_params=pltpu.CompilerParams(vmem_limit_bytes=limit * MIB),
        cost_estimate=pl.CostEstimate(flops=flops, bytes_accessed=moved, transcendentals=0),
    )(*operands)


def chan_sources():
    n_chan, chan = lax.axis_size("chan"), lax.axis_index("chan")
    sources = [chan, chan ^ 1]
    for hop in range(1, n_chan // 2):
        far = (chan - 2 * hop + n_chan) % n_chan
        sources += [far, far ^ 1]
    return sources


def paired(n):
    return n & (n - 1) == 0


def target(me, k, n):
    return me ^ k if paired(n) else (me + k) % n


def origin(me, k, n):
    return me ^ k if paired(n) else (me - k + n) % n


def mirror(k, n):
    return k if paired(n) else -k % n


def rows_at(first, count):
    return pl.ds(pl.multiple_of(first * count, count), count)


def halves_kernel(x_ref, *refs):
    outs, sems = refs[:-1], refs[-1]
    rows = outs[0].shape[0]
    copies = [
        pltpu.make_async_copy(x_ref.at[c * rows : (c + 1) * rows], out, sems.at[c]) for c, out in enumerate(outs)
    ]
    for copy in copies:
        copy.start()
    for copy in copies:
        copy.wait()


def halves(x):
    out = [jax.ShapeDtypeStruct((x.shape[0] // CHUNKS, x.shape[1]), x.dtype)] * CHUNKS
    return pl.pallas_call(
        halves_kernel,
        out_shape=out,
        in_specs=[HBM],
        out_specs=[VMEM] * CHUNKS,
        scratch_shapes=[pltpu.SemaphoreType.DMA((CHUNKS,))],
        compiler_params=pltpu.CompilerParams(vmem_limit_bytes=2 * MIB),
        cost_estimate=pl.CostEstimate(flops=0, bytes_accessed=4 * x.size, transcendentals=0),
        name="halves",
    )(pltpu.with_memory_space_constraint(x, pltpu.HBM))


def prologue_kernel(
    width, skip_hbm, fwd_hbm, inv_hbm, taps_ref, w_ref, fwd_ref, inv_ref, kv_ref, query_ref, out_ref, skip_out, skip_ref, taps_in, prev_ref, sems
):
    block = inv_ref.shape[0]
    cols = rows_at(lax.axis_index("ctx"), width)
    copies = [
        pltpu.make_async_copy(skip_hbm, skip_ref, sems.at[4]),
        pltpu.make_async_copy(fwd_hbm, fwd_ref, sems.at[0]),
        pltpu.make_async_copy(taps_ref.at[:, cols], taps_in, sems.at[1]),
        pltpu.make_async_copy(inv_hbm, inv_ref, sems.at[2]),
        pltpu.make_async_copy(w_ref.at[1:3], kv_ref, sems.at[3]),
        pltpu.make_async_copy(w_ref.at[0], query_ref, sems.at[5]),
    ]
    for copy in copies:
        copy.start()
    prev_ref[...] = jnp.zeros_like(prev_ref)
    for copy in copies[:3]:
        copy.wait()
    for k in range(skip_out.shape[0]):
        skip_out[k, :] = skip_ref[k * width : (k + 1) * width]

    @pl.loop(0, out_ref.shape[0])
    def _(k):
        now = jnp.dot(fwd_ref[...], taps_in[rows_at(k, block), :], preferred_element_type=F32)
        parity = lax.broadcasted_iota(jnp.int32, now.shape, 0) % 2
        out_ref[k] = prev_ref[...] + jnp.where(parity == 0, now, -now)
        prev_ref[...] = now

    for copy in copies[3:]:
        copy.wait()


def prologue(tables, skip, taps, w, n_ctx):
    rows, block = tables[0].shape
    width = w.shape[2] // n_ctx
    count = taps.shape[0] // block
    out = [
        *(jax.ShapeDtypeStruct(t.shape, BF16) for t in tables),
        jax.ShapeDtypeStruct((2, *w.shape[1:]), BF16),
        jax.ShapeDtypeStruct(w.shape[1:], BF16),
        jax.ShapeDtypeStruct((count, rows, width), F32),
        jax.ShapeDtypeStruct((n_ctx, width), F32),
    ]
    return pl.pallas_call(
        functools.partial(prologue_kernel, width),
        out_shape=out,
        in_specs=[HBM] * 5,
        out_specs=[VMEM] * len(out),
        scratch_shapes=[
            pltpu.VMEM(skip.shape, F32),
            pltpu.VMEM((taps.shape[0], width), BF16),
            pltpu.VMEM((rows, width), F32),
            pltpu.SemaphoreType.DMA((6,)),
        ],
        compiler_params=pltpu.CompilerParams(vmem_limit_bytes=6 * MIB),
        cost_estimate=pl.CostEstimate(
            flops=2 * count * rows * block * width,
            bytes_accessed=2 * w.size + count * width * (rows * 4 + block * 2),
            transcendentals=0,
        ),
        name="prologue",
    )(*(pltpu.with_memory_space_constraint(x, pltpu.HBM) for x in (skip, *tables, taps, w)))


def kv_kernel(which, starts, n_ctx, has_before, slices, parts, w_ref, *refs):
    pieces, refs = refs[: len(which)], refs[len(which) :]
    before, outs = (refs[:2], refs[2:]) if has_before else ((), refs)
    tokens = outs[0].shape[0]
    width = w_ref.shape[2] // n_ctx
    depth = pieces[0].shape[1]
    me = lax.axis_index("ctx")
    sources = chan_sources()
    for k in slices or range(n_ctx):
        cols = rows_at(target(me, k, n_ctx), width)
        mine = slice(k * width, (k + 1) * width)
        key, value = (ref[:, mine] for ref in before) if has_before else (None, None)
        for piece, j, start in zip(pieces, which, starts):
            x = piece[start : start + tokens, :]
            rows = rows_at(sources[j], depth)
            a = jnp.dot(x, w_ref[0, rows, cols], preferred_element_type=F32)
            b = jnp.dot(x, w_ref[1, rows, cols], preferred_element_type=F32)
            key = a if key is None else key + a
            value = b if value is None else value + b
        if slices:
            made = (key * value).astype(BF16)
            for p in range(parts):
                cut = slice(p * width // parts, (p + 1) * width // parts)
                outs[slices.index(k) * parts + p][...] = made[:, cut]
        else:
            outs[0][:, mine] = key
            outs[1][:, mine] = value


def keys_values(pieces, which, starts, tokens, w, before, n_ctx, slices=(), parts=1):
    channels = w.shape[2]
    share = len(which) * pieces[0].shape[1]
    if slices:
        out = [jax.ShapeDtypeStruct((tokens, channels // n_ctx // parts), BF16)] * (len(slices) * parts)
    else:
        out = [jax.ShapeDtypeStruct((tokens, channels), F32)] * 2
    return call(
        functools.partial(kv_kernel, tuple(which), tuple(starts), n_ctx, bool(before), slices, parts),
        out,
        [w, *(pieces[j] for j in which), *before],
        6,
        4 * tokens * share * channels * (len(slices) or n_ctx) // n_ctx,
        4 * share * channels + 2 * tokens * share,
    )


def query_kernel(which, starts, n_ctx, has_before, w_ref, *refs):
    pieces, out_ref = refs[: len(which)], refs[-1]
    tokens = out_ref.shape[0]
    depth = pieces[0].shape[1]
    width = out_ref.shape[1] // n_ctx
    me = lax.axis_index("ctx")
    sources = chan_sources()
    for k in range(n_ctx):
        cols = rows_at(target(me, k, n_ctx), width)
        mine = slice(k * width, (k + 1) * width)
        acc = refs[len(which)][:, mine] if has_before else None
        for piece, j, start in zip(pieces, which, starts):
            x = piece[start : start + tokens, :]
            a = jnp.dot(x, w_ref[rows_at(sources[j], depth), cols], preferred_element_type=F32)
            acc = a if acc is None else acc + a
        out_ref[:, mine] = acc.astype(out_ref.dtype)


def queries(pieces, which, starts, tokens, w, before, n_ctx, last):
    channels = w.shape[1]
    share = len(which) * pieces[0].shape[1]
    return call(
        functools.partial(query_kernel, tuple(which), tuple(starts), n_ctx, before is not None),
        jax.ShapeDtypeStruct((tokens, channels), BF16 if last else F32),
        [w, *(pieces[j] for j in which)] + ([] if before is None else [before]),
        6,
        2 * tokens * share * channels,
        2 * share * channels + 2 * tokens * share,
    )


def block_products(g_ref, x_ref, before_ref, after_ref, plan, start, block):
    lags = sorted({lag for _, _, terms in plan for lag, _ in terms})
    slots = sorted({slot for _, _, terms in plan for _, slot in terms})

    def tile(i, first):
        upper = pl.ds(i * 8, 8) if first else rows_at(i, 8)
        lower = pl.ds(block + i * 8, 8) if first else rows_at(block // 8 + i, 8)
        for lane in range(x_ref.shape[2] // LANES):
            cols, own = pl.ds(start + lane * LANES, LANES), pl.ds(lane * LANES, LANES)
            g_re = {b: g_ref[b, upper, cols] for b in lags}
            g_im = {b: g_ref[b, lower, cols] for b in lags}
            x_re = {b: x_ref[b, upper, own] for b in slots}
            x_im = {b: x_ref[b, lower, own] for b in slots}
            g_di = g_re
            if first:
                edge = lax.broadcasted_iota(jnp.int32, (8, LANES), 0) == 0
                g_di = {b: jnp.where(edge, g_im[b], g_re[b]) for b in lags}
                g_im = {b: jnp.where(edge, 0.0, g_im[b]) for b in lags}
            for here, end, terms in plan:
                re = im = None
                if here is not None:
                    re, im = before_ref[here, upper, cols], before_ref[here, lower, cols]
                for lag, slot in terms:
                    up = g_re[lag] * x_re[slot] - g_im[lag] * x_im[slot]
                    down = g_di[lag] * x_im[slot] + g_im[lag] * x_re[slot]
                    re = up if re is None else re + up
                    im = down if im is None else im + down
                after_ref[end, upper, own] = re
                after_ref[end, lower, own] = im

    tile(0, True)
    pl.loop(1, block // 8)(lambda i: tile(i, False))


def part_of(ref, start, width):
    return ref[...] if ref.shape[1] == width else ref[:, start : start + width]


def forward_dft(n_ctx, fwd_ref, ins, x_ref, start):
    me = lax.axis_index("ctx")
    for k in range(n_ctx):
        piece = part_of(ins[k], start, x_ref.shape[2])
        x_ref[origin(me, k, n_ctx)] = jnp.dot(fwd_ref[...], piece, preferred_element_type=F32)


def inverse_dft(n_ctx, inv_ref, y_ref, outs):
    me = lax.axis_index("ctx")
    for k in range(n_ctx):
        spectrum = y_ref[target(me, k, n_ctx)].astype(BF16)
        outs[k][...] = jnp.dot(inv_ref[...], spectrum, preferred_element_type=F32).astype(BF16)


def early_kernel(n_ctx, fwd_ref, g_ref, *refs):
    ins, sum_ref, x_ref = refs[:n_ctx], refs[n_ctx], refs[n_ctx + 1]
    blocks, rows, _ = g_ref.shape
    forward_dft(n_ctx, fwd_ref, ins, x_ref, 0)
    plan = [(None, b, [(b - a, a // 2) for a in range(0, b + 1, 2)]) for b in range(blocks)]
    block_products(g_ref, x_ref, None, sum_ref, plan, 0, rows // 2)


def middle_kernel(n_ctx, start, fwd_ref, inv_ref, g_ref, sum_ref, *refs):
    ins, x_ref, outs, y_ref = refs[:n_ctx], refs[n_ctx], refs[n_ctx + 1 : -1], refs[-1]
    blocks, rows, _ = g_ref.shape
    forward_dft(n_ctx, fwd_ref, ins, x_ref, start)
    plan = [(b, b // 2, [(b - a, a // 2) for a in range(1, b, 2)]) for b in range(0, blocks, 2)]
    block_products(g_ref, x_ref, sum_ref, y_ref, plan, start, rows // 2)
    inverse_dft(n_ctx, inv_ref, y_ref, outs)


def late_kernel(n_ctx, start, inv_ref, g_ref, sum_ref, x_ref, *refs):
    outs, y_ref = refs[:-1], refs[-1]
    blocks, rows, _ = g_ref.shape
    plan = [(b, b // 2, [(b - a, a // 2) for a in range(1, b + 1, 2)]) for b in range(1, blocks, 2)]
    block_products(g_ref, x_ref, sum_ref, y_ref, plan, start, rows // 2)
    inverse_dft(n_ctx, inv_ref, y_ref, outs)


def convolve(forward, inverse, spectra, even, odd, n_ctx):
    blocks, rows, width = spectra.shape
    parts = len(odd)
    share = width // parts
    some = (n_ctx, rows, share)
    piece = jax.ShapeDtypeStruct((rows // 2, share), BF16)
    flops, moved = blocks * rows * rows * width // 2, blocks * rows * width * 8
    sums = call(
        functools.partial(early_kernel, n_ctx),
        jax.ShapeDtypeStruct(spectra.shape, F32),
        [forward, spectra, *even],
        6,
        flops,
        moved,
        [pltpu.VMEM((n_ctx, rows, width), F32)],
    )
    first, second = [], []
    for h in range(parts):
        x, *made = call(
            functools.partial(middle_kernel, n_ctx, h * share),
            [jax.ShapeDtypeStruct(some, F32)] + [piece] * n_ctx,
            [forward, inverse, spectra, sums, *odd[h]],
            6,
            flops // parts,
            moved // parts,
            [pltpu.VMEM(some, F32)],
        )
        first.append(made)
        second.append(
            call(
                functools.partial(late_kernel, n_ctx, h * share),
                [piece] * n_ctx,
                [inverse, spectra, sums, x],
                6,
                flops // parts,
                moved // parts,
                [pltpu.VMEM(some, F32)],
            )
        )
    return [*first, *second]


def gate_kernel(n_ctx, start, skip_ref, q_ref, *refs):
    mixed, conv, out_ref = refs[:n_ctx], refs[n_ctx : 2 * n_ctx], refs[-1]
    share, width = conv[0].shape[1], q_ref.shape[1] // n_ctx
    me = lax.axis_index("ctx")
    for m in range(n_ctx):
        skip = skip_ref[pl.ds(target(me, m, n_ctx), 1), :][:, start : start + share]
        query = q_ref[:, m * width + start : m * width + start + share].astype(F32)
        source = part_of(mixed[m], start, share).astype(F32)
        total = conv[mirror(m, n_ctx)][...].astype(F32) + skip * source
        out_ref[:, m * share : (m + 1) * share] = (query * total).astype(BF16)


def gate(skip, query, mixed, conv, start, n_ctx):
    tokens, share = conv[0].shape
    return call(
        functools.partial(gate_kernel, n_ctx, start),
        jax.ShapeDtypeStruct((tokens, share * n_ctx), BF16),
        [skip, query, *mixed, *conv],
        4,
        3 * tokens * share * n_ctx,
        8 * tokens * share * n_ctx,
    )


def out_kernel(which, parts, has_before, n_ctx, columns, row, w_ref, *refs):
    pieces, out_ref = refs[: len(which) * parts], refs[-1 if row is None else -3]
    share = pieces[0].shape[1] // n_ctx
    width = share * parts
    me = lax.axis_index("ctx")
    sources = chan_sources()
    copies = []
    for i in range(w_ref.shape[1] // columns):
        cols = slice(i * columns, (i + 1) * columns)
        acc = refs[len(pieces)][:, cols] if has_before else None
        for i_piece, j in enumerate(which):
            for m in range(n_ctx):
                w = w_ref[rows_at(sources[j] * n_ctx + target(me, m, n_ctx), width), cols]
                mine = slice(m * share, (m + 1) * share)
                group = pieces[i_piece * parts : (i_piece + 1) * parts]
                x = jnp.concatenate([p[:, mine] for p in group], axis=1)
                a = jnp.dot(x, w, preferred_element_type=F32)
                acc = a if acc is None else acc + a
        if row is None:
            out_ref[:, cols] = acc
            continue
        made_ref, sems = refs[-2:]
        made_ref[:, cols] = acc.astype(BF16)
        there = out_ref.at[row : row + made_ref.shape[0], cols]
        copies.append(pltpu.make_async_copy(made_ref.at[:, cols], there, sems.at[i]))
        copies[-1].start()
    for copy in copies:
        copy.wait()


def project_out(gathered, which, w, before, n_ctx, final=None, columns=256):
    parts = len(gathered)
    tokens = gathered[0][0].shape[0]
    _, out_width = w.shape
    operands = [w, *(pieces[j] for j in which for pieces in gathered)] + ([] if before is None else [before])
    specs = [VMEM] * len(operands)
    aliases, scratch, row = {}, [], None
    out_spec, shape = VMEM, (tokens, out_width)
    if final is not None:
        row, rows, so_far = final
        out_spec, shape = HBM, (rows, out_width)
        scratch = [pltpu.VMEM((tokens, out_width), BF16), pltpu.SemaphoreType.DMA((out_width // columns,))]
        if so_far is not None:
            specs.append(HBM)
            aliases = {len(operands): 0}
            operands.append(so_far)
    share = len(which) * parts * gathered[0][0].shape[1]
    return pl.pallas_call(
        functools.partial(out_kernel, tuple(which), parts, before is not None, n_ctx, columns, row),
        out_shape=jax.ShapeDtypeStruct(shape, F32 if final is None else BF16),
        in_specs=specs,
        out_specs=out_spec,
        scratch_shapes=scratch,
        input_output_aliases=aliases,
        compiler_params=pltpu.CompilerParams(vmem_limit_bytes=6 * MIB),
        cost_estimate=pl.CostEstimate(
            flops=2 * tokens * share * out_width,
            bytes_accessed=2 * share * out_width + 2 * tokens * (share + out_width),
            transcendentals=0,
        ),
        name="out_projection",
    )(*operands)


def shift(x, axis, by):
    n = lax.axis_size(axis)
    return lax.ppermute(x, axis, [(i, (i + by) % n) for i in range(n)])


def swap_cores(x):
    n = lax.axis_size("chan")
    return lax.ppermute(x, "chan", [(i, i ^ 1) for i in range(n)])


def gather_far(x):
    pieces = []
    for hop in range(1, lax.axis_size("chan") // 2):
        far = shift(x, "chan", 2 * hop)
        pieces += [far, swap_cores(far)]
    return pieces


def exchange(parts, first=1):
    out, n = list(parts[:first]), len(parts)
    for k in range(first, n):
        out.append(lax.ppermute(parts[k], "ctx", [(i, target(i, k, n)) for i in range(n)]))
    return out


def layer(features, filter_taps, skip_gain, in_weight, out_weight):
    return layer_body(features, filter_taps, skip_gain, in_weight, out_weight)


def layer_body(features, filter_taps, skip_gain, in_weight, out_weight):
    n_ctx = lax.axis_size("ctx")
    rows = features.shape[0]
    tokens = rows // CHUNKS
    tables = [jnp.asarray(t) for t in real_dft_tables(tokens)]
    w = in_weight.transpose(1, 0, 2)

    own = halves(features)
    far = [gather_far(own[c]) for c in range(CHUNKS)]
    near = swap_cores(features)
    forward, inverse, w_kv, w_q, spectra, skip = prologue(tables, skip_gain, filter_taps, w, n_ctx)

    mixed, query = [], []
    for c in range(CHUNKS):
        pieces = [own[c], near, *far[c]]
        starts = [0, c * tokens] + [0] * len(far[c])
        total = ()
        for part, which in ("a", (0, 1)), ("b", range(2, len(pieces) - 1)):
            total = keys_values(pieces, which, [starts[j] for j in which], tokens, w_kv, total, n_ctx)
        last, made = len(pieces) - 1, {}
        for part, slices, cuts in ("c", tuple(range(2, n_ctx)), c + 1), ("d", (1, 0), 1):
            some = keys_values(pieces, (last,), (starts[last],), tokens, w_kv, total, n_ctx, slices, cuts)
            made.update({k: some[i * cuts : (i + 1) * cuts] for i, k in enumerate(slices)})
        mixed.append([[made[k][h % len(made[k])] for k in range(n_ctx)] for h in range(PARTS)])
        every, before = range(len(pieces)), None
        if c == 0:
            before = queries(pieces, every[:2], starts[:2], tokens, w_q, None, n_ctx, False)
            every = every[2:]
        left = [starts[j] for j in every]
        query.append(queries(pieces, every, left, tokens, w_q, before, n_ctx, True))
    even = exchange(mixed[0][0])
    odd = [exchange(mixed[1][0])]
    odd += [odd[0][:2] + exchange(mixed[1][h], 2)[2:] for h in range(1, PARTS)]
    conv = convolve(forward, inverse, spectra, even, odd, n_ctx)

    gathered = []
    for r in range(CHUNKS * PARTS):
        c, h = r // PARTS, r % PARTS
        back = exchange(conv[r])
        gated = gate(skip, query[c], mixed[c][h], back, h * back[0].shape[1], n_ctx)
        beside = swap_cores(gated)
        gathered.append([gated, beside, *gather_far(gated)])
    every = range(len(gathered[0]))
    out = project_out(gathered[:2], every, out_weight, None, n_ctx, (0, rows, None))
    part = project_out(gathered[2:], every[:2], out_weight, None, n_ctx)
    part = project_out(gathered[2:], every[2:-1], out_weight, part, n_ctx)
    return project_out(gathered[2:], every[-1:], out_weight, part, n_ctx, (tokens, rows, out))


P_SIZE = 128


def dft_tables(block_len):
    period = 2 * block_len
    freq_col = jnp.arange(period, dtype=jnp.int32)[:, None]
    place_row = jnp.arange(period, dtype=jnp.int32)[None, :]
    angles = (freq_col * place_row % period).astype(F32) * (2.0 * math.pi / period)
    forward = jnp.concatenate([jnp.cos(angles), -jnp.sin(angles)], axis=0).astype(BF16)
    out_place = jnp.arange(block_len, dtype=jnp.int32)[:, None] + block_len
    angle_out = (out_place * place_row % period).astype(F32) * (2.0 * math.pi / period)
    inverse = (jnp.concatenate([jnp.cos(angle_out), -jnp.sin(angle_out)], axis=1) / period).astype(BF16)
    return (forward, inverse)


def plain_layer(features, filter_taps, skip_gain, in_weight, out_weight):
    forward, inverse = dft_tables(P_SIZE)
    channels = in_weight.shape[2]
    tok_rows = features.shape[0]
    per_dev = tok_rows // P_SIZE
    period = 2 * P_SIZE
    total_blocks = per_dev * lax.axis_size("ctx")
    first_mine = lax.axis_index("ctx") * per_dev
    padded = jnp.concatenate([jnp.zeros((P_SIZE, channels), BF16), filter_taps], axis=0)
    tap_blocks = padded.reshape(total_blocks + 1, P_SIZE, channels)
    segments = jnp.concatenate([tap_blocks[:-1], tap_blocks[1:]], axis=1)
    lag = jnp.einsum("fn,knc->kfc", forward, segments, preferred_element_type=F32).astype(BF16)
    flipped = jnp.concatenate([lag[::-1], jnp.zeros_like(lag)], axis=0)
    gathered = lax.all_gather(features, "chan", axis=1, tiled=True)
    w = in_weight.transpose(1, 0, 2)
    q, k, v = (jnp.dot(gathered, w[s], preferred_element_type=F32) for s in range(3))
    query = q.astype(BF16)
    mixed = (k * v).astype(BF16)
    everyone = lax.all_gather(mixed, "ctx", axis=0, tiled=True).reshape(total_blocks, P_SIZE, channels)
    source = jnp.einsum("fp,bpc->bfc", forward[:, :P_SIZE], everyone, preferred_element_type=F32)
    source = source.astype(BF16).astype(F32)
    source_re, source_im = source[:, :period], source[:, period:]
    outputs = []
    for out_block in range(per_dev):
        start = total_blocks - 1 - (first_mine + out_block)
        window = lax.dynamic_slice_in_dim(flipped, start, total_blocks, 0).astype(F32)
        lag_re, lag_im = window[:, :period], window[:, period:]
        out_re = jnp.sum(lag_re * source_re - lag_im * source_im, axis=0)
        out_im = jnp.sum(lag_re * source_im + lag_im * source_re, axis=0)
        outputs.append(jnp.concatenate([out_re, out_im], axis=0))
    spectra = jnp.stack(outputs).astype(BF16)
    conv = jnp.einsum("tf,bfc->btc", inverse, spectra, preferred_element_type=F32)
    conv = conv.reshape(tok_rows, channels)
    gated = (query.astype(F32) * (conv + skip_gain[None, :] * mixed.astype(F32))).astype(BF16)
    everything = lax.all_gather(gated, "chan", axis=1, tiled=True)
    return jnp.dot(everything, out_weight, preferred_element_type=F32).astype(BF16)


def shards(features, filter_taps, skip_gain, in_weight, out_weight):
    slices = lax.axis_size("ctx") > 2 and in_weight.shape[2] % (lax.axis_size("ctx") * PARTS * LANES) == 0
    cores = lax.axis_size("chan") % 2 == 0 and lax.axis_size("chan") > 2
    blocks = features.shape[0] % (CHUNKS * LANES) == 0
    chosen = layer if slices and cores and blocks else plain_layer
    return chosen(features, filter_taps, skip_gain, in_weight, out_weight)


def solution(mesh):
    return jax.shard_map(
        shards,
        mesh=mesh,
        in_specs=(
            P(("grp", "ctx"), "chan"),
            P(None, "chan"),
            P("chan"),
            P(None, None, "chan"),
            P(None, "chan"),
        ),
        out_specs=P(("grp", "ctx"), "chan"),
        check_vma=False,
    )
```

```python
import functools
import math

import jax
import jax.numpy as jnp
import ml_dtypes
import numpy as np
from jax import lax
from jax.experimental import pallas as pl
from jax.experimental.pallas import tpu as pltpu
from jax.sharding import PartitionSpec as P


BF16 = jnp.bfloat16
F32 = jnp.float32
LANES = 128
MIB = 1 << 20
CHUNKS = 2
PARTS = 2
VMEM = pl.BlockSpec(memory_space=pltpu.VMEM)
HBM = pl.BlockSpec(memory_space=pltpu.HBM)


def real_dft_tables(block):
    period = 2 * block
    freq = np.arange(block)[:, None]
    place = np.arange(block)[None, :]
    angle = (freq * place % period) * (2.0 * math.pi / period)
    lower = -np.sin(angle)
    lower[0] = 1.0 - 2.0 * (np.arange(block) % 2)
    forward = np.concatenate([np.cos(angle), lower], axis=0)
    out_place = np.arange(block)[:, None] + block
    freq_row = np.arange(block)[None, :]
    angle_out = (out_place * freq_row % period) * (2.0 * math.pi / period)
    weight = np.where(freq_row == 0, 1.0, 2.0)
    lower_out = -np.sin(angle_out) * weight
    lower_out[:, 0] = 1.0 - 2.0 * (np.arange(block) % 2)
    inverse = np.concatenate([np.cos(angle_out) * weight, lower_out], axis=1) / period
    return forward.astype(ml_dtypes.bfloat16), inverse.astype(ml_dtypes.bfloat16)


def call(kernel, out, operands, limit, flops, moved, scratch=()):
    return pl.pallas_call(
        kernel,
        out_shape=out,
        in_specs=[VMEM] * len(operands),
        out_specs=jax.tree.map(lambda _: VMEM, out),
        scratch_shapes=scratch,
        compiler_params=pltpu.CompilerParams(vmem_limit_bytes=limit * MIB),
        cost_estimate=pl.CostEstimate(flops=flops, bytes_accessed=moved, transcendentals=0),
    )(*operands)


def chan_sources():
    n_chan, chan = lax.axis_size("chan"), lax.axis_index("chan")
    sources = [chan, chan ^ 1]
    for hop in range(1, n_chan // 2):
        far = (chan - 2 * hop + n_chan) % n_chan
        sources += [far, far ^ 1]
    return sources


def paired(n):
    return n & (n - 1) == 0


def target(me, k, n):
    return me ^ k if paired(n) else (me + k) % n


def origin(me, k, n):
    return me ^ k if paired(n) else (me - k + n) % n


def mirror(k, n):
    return k if paired(n) else -k % n


def rows_at(first, count):
    return pl.ds(pl.multiple_of(first * count, count), count)


def halves_kernel(x_ref, *refs):
    outs, sems = refs[:-1], refs[-1]
    rows = outs[0].shape[0]
    copies = [
        pltpu.make_async_copy(x_ref.at[c * rows : (c + 1) * rows], out, sems.at[c]) for c, out in enumerate(outs)
    ]
    for copy in copies:
        copy.start()
    for copy in copies:
        copy.wait()


def halves(x):
    out = [jax.ShapeDtypeStruct((x.shape[0] // CHUNKS, x.shape[1]), x.dtype)] * CHUNKS
    return pl.pallas_call(
        halves_kernel,
        out_shape=out,
        in_specs=[HBM],
        out_specs=[VMEM] * CHUNKS,
        scratch_shapes=[pltpu.SemaphoreType.DMA((CHUNKS,))],
        compiler_params=pltpu.CompilerParams(vmem_limit_bytes=2 * MIB),
        cost_estimate=pl.CostEstimate(flops=0, bytes_accessed=4 * x.size, transcendentals=0),
        name="halves",
    )(pltpu.with_memory_space_constraint(x, pltpu.HBM))


def prologue_kernel(
    width, skip_hbm, fwd_hbm, inv_hbm, taps_ref, w_ref, fwd_ref, inv_ref, kv_ref, query_ref, out_ref, skip_out, skip_ref, taps_in, prev_ref, sems
):
    block = inv_ref.shape[0]
    cols = rows_at(lax.axis_index("ctx"), width)
    copies = [
        pltpu.make_async_copy(skip_hbm, skip_ref, sems.at[4]),
        pltpu.make_async_copy(fwd_hbm, fwd_ref, sems.at[0]),
        pltpu.make_async_copy(taps_ref.at[:, cols], taps_in, sems.at[1]),
        pltpu.make_async_copy(inv_hbm, inv_ref, sems.at[2]),
        pltpu.make_async_copy(w_ref.at[1:3], kv_ref, sems.at[3]),
        pltpu.make_async_copy(w_ref.at[0], query_ref, sems.at[5]),
    ]
    for copy in copies:
        copy.start()
    prev_ref[...] = jnp.zeros_like(prev_ref)
    for copy in copies[:3]:
        copy.wait()
    for k in range(skip_out.shape[0]):
        skip_out[k, :] = skip_ref[k * width : (k + 1) * width]

    @pl.loop(0, out_ref.shape[0])
    def _(k):
        now = jnp.dot(fwd_ref[...], taps_in[rows_at(k, block), :], preferred_element_type=F32)
        parity = lax.broadcasted_iota(jnp.int32, now.shape, 0) % 2
        out_ref[k] = prev_ref[...] + jnp.where(parity == 0, now, -now)
        prev_ref[...] = now

    for copy in copies[3:]:
        copy.wait()


def prologue(tables, skip, taps, w, n_ctx):
    rows, block = tables[0].shape
    width = w.shape[2] // n_ctx
    count = taps.shape[0] // block
    out = [
        *(jax.ShapeDtypeStruct(t.shape, BF16) for t in tables),
        jax.ShapeDtypeStruct((2, *w.shape[1:]), BF16),
        jax.ShapeDtypeStruct(w.shape[1:], BF16),
        jax.ShapeDtypeStruct((count, rows, width), F32),
        jax.ShapeDtypeStruct((n_ctx, width), F32),
    ]
    return pl.pallas_call(
        functools.partial(prologue_kernel, width),
        out_shape=out,
        in_specs=[HBM] * 5,
        out_specs=[VMEM] * len(out),
        scratch_shapes=[
            pltpu.VMEM(skip.shape, F32),
            pltpu.VMEM((taps.shape[0], width), BF16),
            pltpu.VMEM((rows, width), F32),
            pltpu.SemaphoreType.DMA((6,)),
        ],
        compiler_params=pltpu.CompilerParams(vmem_limit_bytes=6 * MIB),
        cost_estimate=pl.CostEstimate(
            flops=2 * count * rows * block * width,
            bytes_accessed=2 * w.size + count * width * (rows * 4 + block * 2),
            transcendentals=0,
        ),
        name="prologue",
    )(*(pltpu.with_memory_space_constraint(x, pltpu.HBM) for x in (skip, *tables, taps, w)))


def kv_kernel(which, starts, n_ctx, has_before, slices, parts, w_ref, *refs):
    pieces, refs = refs[: len(which)], refs[len(which) :]
    before, outs = (refs[:2], refs[2:]) if has_before else ((), refs)
    tokens = outs[0].shape[0]
    width = w_ref.shape[2] // n_ctx
    depth = pieces[0].shape[1]
    me = lax.axis_index("ctx")
    sources = chan_sources()
    for k in slices or range(n_ctx):
        cols = rows_at(target(me, k, n_ctx), width)
        mine = slice(k * width, (k + 1) * width)
        key, value = (ref[:, mine] for ref in before) if has_before else (None, None)
        for piece, j, start in zip(pieces, which, starts):
            x = piece[start : start + tokens, :]
            rows = rows_at(sources[j], depth)
            a = jnp.dot(x, w_ref[0, rows, cols], preferred_element_type=F32)
            b = jnp.dot(x, w_ref[1, rows, cols], preferred_element_type=F32)
            key = a if key is None else key + a
            value = b if value is None else value + b
        if slices:
            made = (key * value).astype(BF16)
            for p in range(parts):
                cut = slice(p * width // parts, (p + 1) * width // parts)
                outs[slices.index(k) * parts + p][...] = made[:, cut]
        else:
            outs[0][:, mine] = key
            outs[1][:, mine] = value


def keys_values(pieces, which, starts, tokens, w, before, n_ctx, slices=(), parts=1):
    channels = w.shape[2]
    share = len(which) * pieces[0].shape[1]
    if slices:
        out = [jax.ShapeDtypeStruct((tokens, channels // n_ctx // parts), BF16)] * (len(slices) * parts)
    else:
        out = [jax.ShapeDtypeStruct((tokens, channels), F32)] * 2
    return call(
        functools.partial(kv_kernel, tuple(which), tuple(starts), n_ctx, bool(before), slices, parts),
        out,
        [w, *(pieces[j] for j in which), *before],
        6,
        4 * tokens * share * channels * (len(slices) or n_ctx) // n_ctx,
        4 * share * channels + 2 * tokens * share,
    )


def query_kernel(which, starts, n_ctx, has_before, w_ref, *refs):
    pieces, out_ref = refs[: len(which)], refs[-1]
    tokens = out_ref.shape[0]
    depth = pieces[0].shape[1]
    width = out_ref.shape[1] // n_ctx
    me = lax.axis_index("ctx")
    sources = chan_sources()
    for k in range(n_ctx):
        cols = rows_at(target(me, k, n_ctx), width)
        mine = slice(k * width, (k + 1) * width)
        acc = refs[len(which)][:, mine] if has_before else None
        for piece, j, start in zip(pieces, which, starts):
            x = piece[start : start + tokens, :]
            a = jnp.dot(x, w_ref[rows_at(sources[j], depth), cols], preferred_element_type=F32)
            acc = a if acc is None else acc + a
        out_ref[:, mine] = acc.astype(out_ref.dtype)


def queries(pieces, which, starts, tokens, w, before, n_ctx, last):
    channels = w.shape[1]
    share = len(which) * pieces[0].shape[1]
    return call(
        functools.partial(query_kernel, tuple(which), tuple(starts), n_ctx, before is not None),
        jax.ShapeDtypeStruct((tokens, channels), BF16 if last else F32),
        [w, *(pieces[j] for j in which)] + ([] if before is None else [before]),
        6,
        2 * tokens * share * channels,
        2 * share * channels + 2 * tokens * share,
    )


def block_products(g_ref, x_ref, before_ref, after_ref, plan, start, block):
    lags = sorted({lag for _, _, terms in plan for lag, _ in terms})
    slots = sorted({slot for _, _, terms in plan for _, slot in terms})

    def tile(i, first):
        upper = pl.ds(i * 8, 8) if first else rows_at(i, 8)
        lower = pl.ds(block + i * 8, 8) if first else rows_at(block // 8 + i, 8)
        for lane in range(x_ref.shape[2] // LANES):
            cols, own = pl.ds(start + lane * LANES, LANES), pl.ds(lane * LANES, LANES)
            g_re = {b: g_ref[b, upper, cols] for b in lags}
            g_im = {b: g_ref[b, lower, cols] for b in lags}
            x_re = {b: x_ref[b, upper, own] for b in slots}
            x_im = {b: x_ref[b, lower, own] for b in slots}
            g_di = g_re
            if first:
                edge = lax.broadcasted_iota(jnp.int32, (8, LANES), 0) == 0
                g_di = {b: jnp.where(edge, g_im[b], g_re[b]) for b in lags}
                g_im = {b: jnp.where(edge, 0.0, g_im[b]) for b in lags}
            for here, end, terms in plan:
                re = im = None
                if here is not None:
                    re, im = before_ref[here, upper, cols], before_ref[here, lower, cols]
                for lag, slot in terms:
                    up = g_re[lag] * x_re[slot] - g_im[lag] * x_im[slot]
                    down = g_di[lag] * x_im[slot] + g_im[lag] * x_re[slot]
                    re = up if re is None else re + up
                    im = down if im is None else im + down
                after_ref[end, upper, own] = re
                after_ref[end, lower, own] = im

    tile(0, True)
    pl.loop(1, block // 8)(lambda i: tile(i, False))


def part_of(ref, start, width):
    return ref[...] if ref.shape[1] == width else ref[:, start : start + width]


def forward_dft(n_ctx, fwd_ref, ins, x_ref, start):
    me = lax.axis_index("ctx")
    for k in range(n_ctx):
        piece = part_of(ins[k], start, x_ref.shape[2])
        x_ref[origin(me, k, n_ctx)] = jnp.dot(fwd_ref[...], piece, preferred_element_type=F32)


def inverse_dft(n_ctx, inv_ref, y_ref, outs):
    me = lax.axis_index("ctx")
    for k in range(n_ctx):
        spectrum = y_ref[target(me, k, n_ctx)].astype(BF16)
        outs[k][...] = jnp.dot(inv_ref[...], spectrum, preferred_element_type=F32).astype(BF16)


def early_kernel(n_ctx, fwd_ref, g_ref, *refs):
    ins, sum_ref, x_ref = refs[:n_ctx], refs[n_ctx], refs[n_ctx + 1]
    blocks, rows, _ = g_ref.shape
    forward_dft(n_ctx, fwd_ref, ins, x_ref, 0)
    plan = [(None, b, [(b - a, a // 2) for a in range(0, b + 1, 2)]) for b in range(blocks)]
    block_products(g_ref, x_ref, None, sum_ref, plan, 0, rows // 2)


def middle_kernel(n_ctx, start, fwd_ref, inv_ref, g_ref, sum_ref, *refs):
    ins, x_ref, outs, y_ref = refs[:n_ctx], refs[n_ctx], refs[n_ctx + 1 : -1], refs[-1]
    blocks, rows, _ = g_ref.shape
    forward_dft(n_ctx, fwd_ref, ins, x_ref, start)
    plan = [(b, b // 2, [(b - a, a // 2) for a in range(1, b, 2)]) for b in range(0, blocks, 2)]
    block_products(g_ref, x_ref, sum_ref, y_ref, plan, start, rows // 2)
    inverse_dft(n_ctx, inv_ref, y_ref, outs)


def late_kernel(n_ctx, start, inv_ref, g_ref, sum_ref, x_ref, *refs):
    others, outs, y_ref = refs[: -n_ctx - 1], list(refs[-n_ctx - 1 : -1]), refs[-1]
    share = x_ref.shape[2]
    for h, other in enumerate(others):
        outs[1][:, h * share : (h + 1) * share] = other[...]
    if others:
        outs[1] = outs[1].at[:, len(others) * share :]
    blocks, rows, _ = g_ref.shape
    plan = [(b, b // 2, [(b - a, a // 2) for a in range(1, b + 1, 2)]) for b in range(1, blocks, 2)]
    block_products(g_ref, x_ref, sum_ref, y_ref, plan, start, rows // 2)
    inverse_dft(n_ctx, inv_ref, y_ref, outs)


def convolve(forward, inverse, spectra, even, odd, n_ctx):
    blocks, rows, width = spectra.shape
    parts = len(odd)
    share = width // parts
    some = (n_ctx, rows, share)
    piece = jax.ShapeDtypeStruct((rows // 2, share), BF16)
    flops, moved = blocks * rows * rows * width // 2, blocks * rows * width * 8
    sums = call(
        functools.partial(early_kernel, n_ctx),
        jax.ShapeDtypeStruct(spectra.shape, F32),
        [forward, spectra, *even],
        6,
        flops,
        moved,
        [pltpu.VMEM((n_ctx, rows, width), F32)],
    )
    first, second = [], []
    for h in range(parts):
        x, *made = call(
            functools.partial(middle_kernel, n_ctx, h * share),
            [jax.ShapeDtypeStruct(some, F32)] + [piece] * n_ctx,
            [forward, inverse, spectra, sums, *odd[h]],
            6,
            flops // parts,
            moved // parts,
            [pltpu.VMEM(some, F32)],
        )
        first.append(made)
        others = [made[1] for made in second] if h == parts - 1 else []
        together = jax.ShapeDtypeStruct((rows // 2, share * (1 + len(others))), BF16)
        second.append(
            call(
                functools.partial(late_kernel, n_ctx, h * share),
                [piece, together] + [piece] * (n_ctx - 2),
                [inverse, spectra, sums, x, *others],
                6,
                flops // parts,
                moved // parts,
                [pltpu.VMEM(some, F32)],
            )
        )
    return [*first, *second]


def gate_kernel(n_ctx, start, skip_ref, q_ref, *refs):
    mixed, conv, out_ref = refs[:n_ctx], refs[n_ctx : 2 * n_ctx], refs[-1]
    share, width = conv[0].shape[1], q_ref.shape[1] // n_ctx
    me = lax.axis_index("ctx")
    for m in range(n_ctx):
        skip = skip_ref[pl.ds(target(me, m, n_ctx), 1), :][:, start : start + share]
        query = q_ref[:, m * width + start : m * width + start + share].astype(F32)
        source = part_of(mixed[m], start, share).astype(F32)
        total = part_of(conv[mirror(m, n_ctx)], start, share).astype(F32) + skip * source
        out_ref[:, m * share : (m + 1) * share] = (query * total).astype(BF16)


def gate(skip, query, mixed, conv, start, n_ctx):
    tokens, share = conv[0].shape
    return call(
        functools.partial(gate_kernel, n_ctx, start),
        jax.ShapeDtypeStruct((tokens, share * n_ctx), BF16),
        [skip, query, *mixed, *conv],
        4,
        3 * tokens * share * n_ctx,
        8 * tokens * share * n_ctx,
    )


def out_kernel(which, parts, has_before, n_ctx, columns, row, w_ref, *refs):
    pieces, out_ref = refs[: len(which) * parts], refs[-1 if row is None else -3]
    share = pieces[0].shape[1] // n_ctx
    width = share * parts
    me = lax.axis_index("ctx")
    sources = chan_sources()
    copies = []
    for i in range(w_ref.shape[1] // columns):
        cols = slice(i * columns, (i + 1) * columns)
        acc = refs[len(pieces)][:, cols] if has_before else None
        for i_piece, j in enumerate(which):
            for m in range(n_ctx):
                w = w_ref[rows_at(sources[j] * n_ctx + target(me, m, n_ctx), width), cols]
                mine = slice(m * share, (m + 1) * share)
                group = pieces[i_piece * parts : (i_piece + 1) * parts]
                x = jnp.concatenate([p[:, mine] for p in group], axis=1)
                a = jnp.dot(x, w, preferred_element_type=F32)
                acc = a if acc is None else acc + a
        if row is None:
            out_ref[:, cols] = acc
            continue
        made_ref, sems = refs[-2:]
        made_ref[:, cols] = acc.astype(BF16)
        there = out_ref.at[row : row + made_ref.shape[0], cols]
        copies.append(pltpu.make_async_copy(made_ref.at[:, cols], there, sems.at[i]))
        copies[-1].start()
    for copy in copies:
        copy.wait()


def project_out(gathered, which, w, before, n_ctx, final=None, columns=256):
    parts = len(gathered)
    tokens = gathered[0][0].shape[0]
    _, out_width = w.shape
    operands = [w, *(pieces[j] for j in which for pieces in gathered)] + ([] if before is None else [before])
    specs = [VMEM] * len(operands)
    aliases, scratch, row = {}, [], None
    out_spec, shape = VMEM, (tokens, out_width)
    if final is not None:
        row, rows, so_far = final
        out_spec, shape = HBM, (rows, out_width)
        scratch = [pltpu.VMEM((tokens, out_width), BF16), pltpu.SemaphoreType.DMA((out_width // columns,))]
        if so_far is not None:
            specs.append(HBM)
            aliases = {len(operands): 0}
            operands.append(so_far)
    share = len(which) * parts * gathered[0][0].shape[1]
    return pl.pallas_call(
        functools.partial(out_kernel, tuple(which), parts, before is not None, n_ctx, columns, row),
        out_shape=jax.ShapeDtypeStruct(shape, F32 if final is None else BF16),
        in_specs=specs,
        out_specs=out_spec,
        scratch_shapes=scratch,
        input_output_aliases=aliases,
        compiler_params=pltpu.CompilerParams(vmem_limit_bytes=6 * MIB),
        cost_estimate=pl.CostEstimate(
            flops=2 * tokens * share * out_width,
            bytes_accessed=2 * share * out_width + 2 * tokens * (share + out_width),
            transcendentals=0,
        ),
        name="out_projection",
    )(*operands)


def shift(x, axis, by):
    n = lax.axis_size(axis)
    return lax.ppermute(x, axis, [(i, (i + by) % n) for i in range(n)])


def swap_cores(x):
    n = lax.axis_size("chan")
    return lax.ppermute(x, "chan", [(i, i ^ 1) for i in range(n)])


def gather_far(x):
    pieces = []
    for hop in range(1, lax.axis_size("chan") // 2):
        far = shift(x, "chan", 2 * hop)
        pieces += [far, swap_cores(far)]
    return pieces


def exchange(parts, first=1):
    out, n = list(parts[:first]), len(parts)
    for k in range(first, n):
        out.append(lax.ppermute(parts[k], "ctx", [(i, target(i, k, n)) for i in range(n)]))
    return out


def layer(features, filter_taps, skip_gain, in_weight, out_weight):
    return layer_body(features, filter_taps, skip_gain, in_weight, out_weight)


def layer_body(features, filter_taps, skip_gain, in_weight, out_weight):
    n_ctx = lax.axis_size("ctx")
    rows = features.shape[0]
    tokens = rows // CHUNKS
    tables = [jnp.asarray(t) for t in real_dft_tables(tokens)]
    w = in_weight.transpose(1, 0, 2)

    own = halves(features)
    far = [gather_far(own[c]) for c in range(CHUNKS)]
    near = swap_cores(features)
    forward, inverse, w_kv, w_q, spectra, skip = prologue(tables, skip_gain, filter_taps, w, n_ctx)

    mixed, query = [], []
    for c in range(CHUNKS):
        pieces = [own[c], near, *far[c]]
        starts = [0, c * tokens] + [0] * len(far[c])
        total = ()
        for part, which in ("a", (0, 1)), ("b", range(2, len(pieces) - 1)):
            total = keys_values(pieces, which, [starts[j] for j in which], tokens, w_kv, total, n_ctx)
        last, made = len(pieces) - 1, {}
        for part, slices, cuts in ("c", tuple(range(2, n_ctx)), c + 1), ("d", (1, 0), 1):
            some = keys_values(pieces, (last,), (starts[last],), tokens, w_kv, total, n_ctx, slices, cuts)
            made.update({k: some[i * cuts : (i + 1) * cuts] for i, k in enumerate(slices)})
        mixed.append([[made[k][h % len(made[k])] for k in range(n_ctx)] for h in range(PARTS)])
        every, before = range(len(pieces)), None
        if c == 0:
            before = queries(pieces, every[:2], starts[:2], tokens, w_q, None, n_ctx, False)
            every = every[2:]
        left = [starts[j] for j in every]
        query.append(queries(pieces, every, left, tokens, w_q, before, n_ctx, True))
    even = exchange(mixed[0][0])
    odd = [exchange(mixed[1][0])]
    odd += [odd[0][:2] + exchange(mixed[1][h], 2)[2:] for h in range(1, PARTS)]
    conv = convolve(forward, inverse, spectra, even, odd, n_ctx)

    joint = lax.ppermute(conv[-1][1], "ctx", [(i, target(i, 1, n_ctx)) for i in range(n_ctx)])
    gathered = []
    for r in range(CHUNKS * PARTS):
        c, h = r // PARTS, r % PARTS
        back = exchange(conv[r], 1 if c == 0 else 2)
        if c > 0:
            back[1] = joint
        gated = gate(skip, query[c], mixed[c][h], back, h * back[0].shape[1], n_ctx)
        beside = swap_cores(gated)
        gathered.append([gated, beside, *gather_far(gated)])
    every = range(len(gathered[0]))
    out = project_out(gathered[:2], every, out_weight, None, n_ctx, (0, rows, None))
    part = project_out(gathered[2:], every[:2], out_weight, None, n_ctx)
    part = project_out(gathered[2:], every[2:-1], out_weight, part, n_ctx)
    return project_out(gathered[2:], every[-1:], out_weight, part, n_ctx, (tokens, rows, out))


P_SIZE = 128


def dft_tables(block_len):
    period = 2 * block_len
    freq_col = jnp.arange(period, dtype=jnp.int32)[:, None]
    place_row = jnp.arange(period, dtype=jnp.int32)[None, :]
    angles = (freq_col * place_row % period).astype(F32) * (2.0 * math.pi / period)
    forward = jnp.concatenate([jnp.cos(angles), -jnp.sin(angles)], axis=0).astype(BF16)
    out_place = jnp.arange(block_len, dtype=jnp.int32)[:, None] + block_len
    angle_out = (out_place * place_row % period).astype(F32) * (2.0 * math.pi / period)
    inverse = (jnp.concatenate([jnp.cos(angle_out), -jnp.sin(angle_out)], axis=1) / period).astype(BF16)
    return (forward, inverse)


def plain_layer(features, filter_taps, skip_gain, in_weight, out_weight):
    forward, inverse = dft_tables(P_SIZE)
    channels = in_weight.shape[2]
    tok_rows = features.shape[0]
    per_dev = tok_rows // P_SIZE
    period = 2 * P_SIZE
    total_blocks = per_dev * lax.axis_size("ctx")
    first_mine = lax.axis_index("ctx") * per_dev
    padded = jnp.concatenate([jnp.zeros((P_SIZE, channels), BF16), filter_taps], axis=0)
    tap_blocks = padded.reshape(total_blocks + 1, P_SIZE, channels)
    segments = jnp.concatenate([tap_blocks[:-1], tap_blocks[1:]], axis=1)
    lag = jnp.einsum("fn,knc->kfc", forward, segments, preferred_element_type=F32).astype(BF16)
    flipped = jnp.concatenate([lag[::-1], jnp.zeros_like(lag)], axis=0)
    gathered = lax.all_gather(features, "chan", axis=1, tiled=True)
    w = in_weight.transpose(1, 0, 2)
    q, k, v = (jnp.dot(gathered, w[s], preferred_element_type=F32) for s in range(3))
    query = q.astype(BF16)
    mixed = (k * v).astype(BF16)
    everyone = lax.all_gather(mixed, "ctx", axis=0, tiled=True).reshape(total_blocks, P_SIZE, channels)
    source = jnp.einsum("fp,bpc->bfc", forward[:, :P_SIZE], everyone, preferred_element_type=F32)
    source = source.astype(BF16).astype(F32)
    source_re, source_im = source[:, :period], source[:, period:]
    outputs = []
    for out_block in range(per_dev):
        start = total_blocks - 1 - (first_mine + out_block)
        window = lax.dynamic_slice_in_dim(flipped, start, total_blocks, 0).astype(F32)
        lag_re, lag_im = window[:, :period], window[:, period:]
        out_re = jnp.sum(lag_re * source_re - lag_im * source_im, axis=0)
        out_im = jnp.sum(lag_re * source_im + lag_im * source_re, axis=0)
        outputs.append(jnp.concatenate([out_re, out_im], axis=0))
    spectra = jnp.stack(outputs).astype(BF16)
    conv = jnp.einsum("tf,bfc->btc", inverse, spectra, preferred_element_type=F32)
    conv = conv.reshape(tok_rows, channels)
    gated = (query.astype(F32) * (conv + skip_gain[None, :] * mixed.astype(F32))).astype(BF16)
    everything = lax.all_gather(gated, "chan", axis=1, tiled=True)
    return jnp.dot(everything, out_weight, preferred_element_type=F32).astype(BF16)


def shards(features, filter_taps, skip_gain, in_weight, out_weight):
    slices = lax.axis_size("ctx") > 2 and in_weight.shape[2] % (lax.axis_size("ctx") * PARTS * LANES) == 0
    cores = lax.axis_size("chan") % 2 == 0 and lax.axis_size("chan") > 2
    blocks = features.shape[0] % (CHUNKS * LANES) == 0
    chosen = layer if slices and cores and blocks else plain_layer
    return chosen(features, filter_taps, skip_gain, in_weight, out_weight)


def solution(mesh):
    return jax.shard_map(
        shards,
        mesh=mesh,
        in_specs=(
            P(("grp", "ctx"), "chan"),
            P(None, "chan"),
            P("chan"),
            P(None, None, "chan"),
            P(None, "chan"),
        ),
        out_specs=P(("grp", "ctx"), "chan"),
        check_vma=False,
    )
```

```python
import functools
import math

import jax
import jax.numpy as jnp
import ml_dtypes
import numpy as np
from jax import lax
from jax.experimental import pallas as pl
from jax.experimental.pallas import tpu as pltpu
from jax.sharding import PartitionSpec as P


BF16 = jnp.bfloat16
F32 = jnp.float32
LANES = 128
MIB = 1 << 20
CHUNKS = 2
PARTS = 2
VMEM = pl.BlockSpec(memory_space=pltpu.VMEM)
HBM = pl.BlockSpec(memory_space=pltpu.HBM)


def real_dft_tables(block):
    period = 2 * block
    freq = np.arange(block)[:, None]
    place = np.arange(block)[None, :]
    angle = (freq * place % period) * (2.0 * math.pi / period)
    lower = -np.sin(angle)
    lower[0] = 1.0 - 2.0 * (np.arange(block) % 2)
    forward = np.concatenate([np.cos(angle), lower], axis=0)
    out_place = np.arange(block)[:, None] + block
    freq_row = np.arange(block)[None, :]
    angle_out = (out_place * freq_row % period) * (2.0 * math.pi / period)
    weight = np.where(freq_row == 0, 1.0, 2.0)
    lower_out = -np.sin(angle_out) * weight
    lower_out[:, 0] = 1.0 - 2.0 * (np.arange(block) % 2)
    inverse = np.concatenate([np.cos(angle_out) * weight, lower_out], axis=1) / period
    return forward.astype(ml_dtypes.bfloat16), inverse.astype(ml_dtypes.bfloat16)


def call(kernel, out, operands, limit, flops, moved, scratch=()):
    return pl.pallas_call(
        kernel,
        out_shape=out,
        in_specs=[VMEM] * len(operands),
        out_specs=jax.tree.map(lambda _: VMEM, out),
        scratch_shapes=scratch,
        compiler_params=pltpu.CompilerParams(vmem_limit_bytes=limit * MIB),
        cost_estimate=pl.CostEstimate(flops=flops, bytes_accessed=moved, transcendentals=0),
    )(*operands)


def chan_sources():
    n_chan, chan = lax.axis_size("chan"), lax.axis_index("chan")
    sources = [chan, chan ^ 1]
    for hop in range(1, n_chan // 2):
        far = (chan - 2 * hop + n_chan) % n_chan
        sources += [far, far ^ 1]
    return sources


def paired(n):
    return n & (n - 1) == 0


def target(me, k, n):
    return me ^ k if paired(n) else (me + k) % n


def origin(me, k, n):
    return me ^ k if paired(n) else (me - k + n) % n


def mirror(k, n):
    return k if paired(n) else -k % n


def rows_at(first, count):
    return pl.ds(pl.multiple_of(first * count, count), count)


def halves_kernel(x_ref, *refs):
    outs, sems = refs[:-1], refs[-1]
    rows = outs[0].shape[0]
    copies = [
        pltpu.make_async_copy(x_ref.at[c * rows : (c + 1) * rows], out, sems.at[c]) for c, out in enumerate(outs)
    ]
    for copy in copies:
        copy.start()
    for copy in copies:
        copy.wait()


def halves(x):
    out = [jax.ShapeDtypeStruct((x.shape[0] // CHUNKS, x.shape[1]), x.dtype)] * CHUNKS
    return pl.pallas_call(
        halves_kernel,
        out_shape=out,
        in_specs=[HBM],
        out_specs=[VMEM] * CHUNKS,
        scratch_shapes=[pltpu.SemaphoreType.DMA((CHUNKS,))],
        compiler_params=pltpu.CompilerParams(vmem_limit_bytes=2 * MIB),
        cost_estimate=pl.CostEstimate(flops=0, bytes_accessed=4 * x.size, transcendentals=0),
        name="halves",
    )(pltpu.with_memory_space_constraint(x, pltpu.HBM))


def prologue_kernel(
    width, skip_hbm, fwd_hbm, inv_hbm, taps_ref, w_ref, fwd_ref, inv_ref, kv_ref, query_ref, out_ref, skip_out, skip_ref, taps_in, prev_ref, sems
):
    block = inv_ref.shape[0]
    cols = rows_at(lax.axis_index("ctx"), width)
    copies = [
        pltpu.make_async_copy(skip_hbm, skip_ref, sems.at[4]),
        pltpu.make_async_copy(fwd_hbm, fwd_ref, sems.at[0]),
        pltpu.make_async_copy(taps_ref.at[:, cols], taps_in, sems.at[1]),
        pltpu.make_async_copy(inv_hbm, inv_ref, sems.at[2]),
        pltpu.make_async_copy(w_ref.at[1:3], kv_ref, sems.at[3]),
        pltpu.make_async_copy(w_ref.at[0], query_ref, sems.at[5]),
    ]
    for copy in copies:
        copy.start()
    prev_ref[...] = jnp.zeros_like(prev_ref)
    for copy in copies[:3]:
        copy.wait()
    for k in range(skip_out.shape[0]):
        skip_out[k, :] = skip_ref[k * width : (k + 1) * width]

    @pl.loop(0, out_ref.shape[0])
    def _(k):
        now = jnp.dot(fwd_ref[...], taps_in[rows_at(k, block), :], preferred_element_type=F32)
        parity = lax.broadcasted_iota(jnp.int32, now.shape, 0) % 2
        out_ref[k] = prev_ref[...] + jnp.where(parity == 0, now, -now)
        prev_ref[...] = now

    for copy in copies[3:]:
        copy.wait()


def prologue(tables, skip, taps, w, n_ctx):
    rows, block = tables[0].shape
    width = w.shape[2] // n_ctx
    count = taps.shape[0] // block
    out = [
        *(jax.ShapeDtypeStruct(t.shape, BF16) for t in tables),
        jax.ShapeDtypeStruct((2, *w.shape[1:]), BF16),
        jax.ShapeDtypeStruct(w.shape[1:], BF16),
        jax.ShapeDtypeStruct((count, rows, width), F32),
        jax.ShapeDtypeStruct((n_ctx, width), F32),
    ]
    return pl.pallas_call(
        functools.partial(prologue_kernel, width),
        out_shape=out,
        in_specs=[HBM] * 5,
        out_specs=[VMEM] * len(out),
        scratch_shapes=[
            pltpu.VMEM(skip.shape, F32),
            pltpu.VMEM((taps.shape[0], width), BF16),
            pltpu.VMEM((rows, width), F32),
            pltpu.SemaphoreType.DMA((6,)),
        ],
        compiler_params=pltpu.CompilerParams(vmem_limit_bytes=6 * MIB),
        cost_estimate=pl.CostEstimate(
            flops=2 * count * rows * block * width,
            bytes_accessed=2 * w.size + count * width * (rows * 4 + block * 2),
            transcendentals=0,
        ),
        name="prologue",
    )(*(pltpu.with_memory_space_constraint(x, pltpu.HBM) for x in (skip, *tables, taps, w)))


def kv_kernel(which, starts, n_ctx, has_before, slices, parts, w_ref, *refs):
    pieces, refs = refs[: len(which)], refs[len(which) :]
    before, outs = (refs[:2], refs[2:]) if has_before else ((), refs)
    tokens = outs[0].shape[0]
    width = w_ref.shape[2] // n_ctx
    depth = pieces[0].shape[1]
    me = lax.axis_index("ctx")
    sources = chan_sources()
    for k in slices or range(n_ctx):
        cols = rows_at(target(me, k, n_ctx), width)
        mine = slice(k * width, (k + 1) * width)
        key, value = (ref[:, mine] for ref in before) if has_before else (None, None)
        for piece, j, start in zip(pieces, which, starts):
            x = piece[start : start + tokens, :]
            rows = rows_at(sources[j], depth)
            a = jnp.dot(x, w_ref[0, rows, cols], preferred_element_type=F32)
            b = jnp.dot(x, w_ref[1, rows, cols], preferred_element_type=F32)
            key = a if key is None else key + a
            value = b if value is None else value + b
        if slices:
            made = (key * value).astype(BF16)
            for p in range(parts):
                cut = slice(p * width // parts, (p + 1) * width // parts)
                outs[slices.index(k) * parts + p][...] = made[:, cut]
        else:
            outs[0][:, mine] = key
            outs[1][:, mine] = value


def keys_values(pieces, which, starts, tokens, w, before, n_ctx, slices=(), parts=1):
    channels = w.shape[2]
    share = len(which) * pieces[0].shape[1]
    if slices:
        out = [jax.ShapeDtypeStruct((tokens, channels // n_ctx // parts), BF16)] * (len(slices) * parts)
    else:
        out = [jax.ShapeDtypeStruct((tokens, channels), F32)] * 2
    return call(
        functools.partial(kv_kernel, tuple(which), tuple(starts), n_ctx, bool(before), slices, parts),
        out,
        [w, *(pieces[j] for j in which), *before],
        6,
        4 * tokens * share * channels * (len(slices) or n_ctx) // n_ctx,
        4 * share * channels + 2 * tokens * share,
    )


def query_kernel(which, starts, n_ctx, has_before, w_ref, *refs):
    pieces, out_ref = refs[: len(which)], refs[-1]
    tokens = out_ref.shape[0]
    depth = pieces[0].shape[1]
    width = out_ref.shape[1] // n_ctx
    me = lax.axis_index("ctx")
    sources = chan_sources()
    for k in range(n_ctx):
        cols = rows_at(target(me, k, n_ctx), width)
        mine = slice(k * width, (k + 1) * width)
        acc = refs[len(which)][:, mine] if has_before else None
        for piece, j, start in zip(pieces, which, starts):
            x = piece[start : start + tokens, :]
            a = jnp.dot(x, w_ref[rows_at(sources[j], depth), cols], preferred_element_type=F32)
            acc = a if acc is None else acc + a
        out_ref[:, mine] = acc.astype(out_ref.dtype)


def queries(pieces, which, starts, tokens, w, before, n_ctx, last):
    channels = w.shape[1]
    share = len(which) * pieces[0].shape[1]
    return call(
        functools.partial(query_kernel, tuple(which), tuple(starts), n_ctx, before is not None),
        jax.ShapeDtypeStruct((tokens, channels), BF16 if last else F32),
        [w, *(pieces[j] for j in which)] + ([] if before is None else [before]),
        6,
        2 * tokens * share * channels,
        2 * share * channels + 2 * tokens * share,
    )


def block_products(g_ref, x_ref, before_ref, after_ref, plan, start, block):
    lags = sorted({lag for _, _, terms in plan for lag, _ in terms})
    slots = sorted({slot for _, _, terms in plan for _, slot in terms})

    def tile(i, first):
        upper = pl.ds(i * 8, 8) if first else rows_at(i, 8)
        lower = pl.ds(block + i * 8, 8) if first else rows_at(block // 8 + i, 8)
        for lane in range(x_ref.shape[2] // LANES):
            cols, own = pl.ds(start + lane * LANES, LANES), pl.ds(lane * LANES, LANES)
            g_re = {b: g_ref[b, upper, cols] for b in lags}
            g_im = {b: g_ref[b, lower, cols] for b in lags}
            x_re = {b: x_ref[b, upper, own] for b in slots}
            x_im = {b: x_ref[b, lower, own] for b in slots}
            g_di = g_re
            if first:
                edge = lax.broadcasted_iota(jnp.int32, (8, LANES), 0) == 0
                g_di = {b: jnp.where(edge, g_im[b], g_re[b]) for b in lags}
                g_im = {b: jnp.where(edge, 0.0, g_im[b]) for b in lags}
            for here, end, terms in plan:
                re = im = None
                if here is not None:
                    re, im = before_ref[here, upper, cols], before_ref[here, lower, cols]
                for lag, slot in terms:
                    up = g_re[lag] * x_re[slot] - g_im[lag] * x_im[slot]
                    down = g_di[lag] * x_im[slot] + g_im[lag] * x_re[slot]
                    re = up if re is None else re + up
                    im = down if im is None else im + down
                after_ref[end, upper, own] = re
                after_ref[end, lower, own] = im

    tile(0, True)
    pl.loop(1, block // 8)(lambda i: tile(i, False))


def part_of(ref, start, width):
    return ref[...] if ref.shape[1] == width else ref[:, start : start + width]


def forward_dft(n_ctx, fwd_ref, ins, x_ref, start):
    me = lax.axis_index("ctx")
    for k in range(n_ctx):
        piece = part_of(ins[k], start, x_ref.shape[2])
        x_ref[origin(me, k, n_ctx)] = jnp.dot(fwd_ref[...], piece, preferred_element_type=F32)


def inverse_dft(n_ctx, inv_ref, y_ref, outs):
    me = lax.axis_index("ctx")
    for k in range(n_ctx):
        spectrum = y_ref[target(me, k, n_ctx)].astype(BF16)
        made = jnp.dot(inv_ref[...], spectrum, preferred_element_type=F32).astype(BF16)
        share = outs[k][0].shape[1]
        for h, out in enumerate(outs[k]):
            out[...] = made[:, h * share : (h + 1) * share]


def early_kernel(n_ctx, fwd_ref, g_ref, *refs):
    ins, sum_ref, x_ref = refs[:n_ctx], refs[n_ctx], refs[n_ctx + 1]
    blocks, rows, _ = g_ref.shape
    forward_dft(n_ctx, fwd_ref, ins, x_ref, 0)
    plan = [(None, b, [(b - a, a // 2) for a in range(0, b + 1, 2)]) for b in range(blocks)]
    block_products(g_ref, x_ref, None, sum_ref, plan, 0, rows // 2)


def middle_kernel(n_ctx, start, fwd_ref, inv_ref, g_ref, sum_ref, *refs):
    ins, x_ref, outs, y_ref = refs[:n_ctx], refs[n_ctx], refs[n_ctx + 1 : -1], refs[-1]
    blocks, rows, _ = g_ref.shape
    forward_dft(n_ctx, fwd_ref, ins, x_ref, start)
    plan = [(b, b // 2, [(b - a, a // 2) for a in range(1, b, 2)]) for b in range(0, blocks, 2)]
    block_products(g_ref, x_ref, sum_ref, y_ref, plan, start, rows // 2)
    inverse_dft(n_ctx, inv_ref, y_ref, [[out] for out in outs])


def late_kernel(n_ctx, parts, inv_ref, g_ref, sum_ref, *refs):
    xs, outs, y_ref = refs[:parts], refs[parts:-1], refs[-1]
    blocks, rows, width = g_ref.shape
    share = width // parts
    plan = [(b, b // 2, [(b - a, a // 2) for a in range(1, b + 1, 2)]) for b in range(1, blocks, 2)]
    for h, x_ref in enumerate(xs):
        mine = y_ref.at[:, :, h * share : (h + 1) * share]
        block_products(g_ref, x_ref, sum_ref, mine, plan, h * share, rows // 2)
    cut = [outs[2 + i * parts : 2 + (i + 1) * parts] for i in range(n_ctx - 2)]
    inverse_dft(n_ctx, inv_ref, y_ref, [outs[:1], outs[1:2], *cut])


def convolve(forward, inverse, spectra, even, odd, n_ctx):
    blocks, rows, width = spectra.shape
    parts = len(odd)
    share = width // parts
    some = (n_ctx, rows, share)
    piece = jax.ShapeDtypeStruct((rows // 2, share), BF16)
    flops, moved = blocks * rows * rows * width // 2, blocks * rows * width * 8
    sums = call(
        functools.partial(early_kernel, n_ctx),
        jax.ShapeDtypeStruct(spectra.shape, F32),
        [forward, spectra, *even],
        6,
        flops,
        moved,
        [pltpu.VMEM((n_ctx, rows, width), F32)],
    )
    first, xs = [], []
    for h in range(parts):
        x, *made = call(
            functools.partial(middle_kernel, n_ctx, h * share),
            [jax.ShapeDtypeStruct(some, F32)] + [piece] * n_ctx,
            [forward, inverse, spectra, sums, *odd[h]],
            6,
            flops // parts,
            moved // parts,
            [pltpu.VMEM(some, F32)],
        )
        first.append(made)
        xs.append(x)
    whole = jax.ShapeDtypeStruct((rows // 2, width), BF16)
    made = call(
        functools.partial(late_kernel, n_ctx, parts),
        [whole] * 2 + [piece] * ((n_ctx - 2) * parts),
        [inverse, spectra, sums, *xs],
        6,
        flops,
        moved,
        [pltpu.VMEM((n_ctx, rows, width), F32)],
    )
    return [*first, *(made[:2] + made[2 + h :: parts] for h in range(parts))]


def gate_kernel(n_ctx, start, share, skip_ref, q_ref, *refs):
    mixed, conv, out_ref = refs[:n_ctx], refs[n_ctx : 2 * n_ctx], refs[-1]
    width = q_ref.shape[1] // n_ctx
    me = lax.axis_index("ctx")
    for m in range(n_ctx):
        skip = skip_ref[pl.ds(target(me, m, n_ctx), 1), :][:, start : start + share]
        query = q_ref[:, m * width + start : m * width + start + share].astype(F32)
        source = part_of(mixed[m], start, share).astype(F32)
        total = part_of(conv[mirror(m, n_ctx)], start, share).astype(F32) + skip * source
        out_ref[:, m * share : (m + 1) * share] = (query * total).astype(BF16)


def gate(skip, query, mixed, conv, start, share, n_ctx):
    tokens = conv[0].shape[0]
    return call(
        functools.partial(gate_kernel, n_ctx, start, share),
        jax.ShapeDtypeStruct((tokens, share * n_ctx), BF16),
        [skip, query, *mixed, *conv],
        4,
        3 * tokens * share * n_ctx,
        8 * tokens * share * n_ctx,
    )


def out_kernel(which, parts, has_before, n_ctx, columns, row, w_ref, *refs):
    pieces, out_ref = refs[: sum(len(some) for _, some in which)], refs[-1 if row is None else -3]
    share = pieces[0].shape[1] // n_ctx
    width = share * parts
    me = lax.axis_index("ctx")
    sources = chan_sources()
    copies = []
    for i in range(w_ref.shape[1] // columns):
        cols = slice(i * columns, (i + 1) * columns)
        acc = refs[len(pieces)][:, cols] if has_before else None
        used = 0
        for j, some in which:
            group = pieces[used : used + len(some)]
            used += len(some)
            for m in range(n_ctx):
                first = (sources[j] * n_ctx + target(me, m, n_ctx)) * width + some[0] * share
                w = w_ref[pl.ds(pl.multiple_of(first, share), len(some) * share), cols]
                mine = slice(m * share, (m + 1) * share)
                x = jnp.concatenate([p[:, mine] for p in group], axis=1)
                a = jnp.dot(x, w, preferred_element_type=F32)
                acc = a if acc is None else acc + a
        if row is None:
            out_ref[:, cols] = acc
            continue
        made_ref, sems = refs[-2:]
        made_ref[:, cols] = acc.astype(BF16)
        there = out_ref.at[row : row + made_ref.shape[0], cols]
        copies.append(pltpu.make_async_copy(made_ref.at[:, cols], there, sems.at[i]))
        copies[-1].start()
    for copy in copies:
        copy.wait()


def project_out(gathered, which, w, before, n_ctx, final=None, columns=256):
    parts = len(gathered)
    tokens = gathered[0][0].shape[0]
    _, out_width = w.shape
    operands = [w, *(gathered[h][j] for j, some in which for h in some)] + ([] if before is None else [before])
    specs = [VMEM] * len(operands)
    aliases, scratch, row = {}, [], None
    out_spec, shape = VMEM, (tokens, out_width)
    if final is not None:
        row, rows, so_far = final
        out_spec, shape = HBM, (rows, out_width)
        scratch = [pltpu.VMEM((tokens, out_width), BF16), pltpu.SemaphoreType.DMA((out_width // columns,))]
        if so_far is not None:
            specs.append(HBM)
            aliases = {len(operands): 0}
            operands.append(so_far)
    share = sum(len(some) for _, some in which) * gathered[0][0].shape[1]
    return pl.pallas_call(
        functools.partial(out_kernel, tuple(which), parts, before is not None, n_ctx, columns, row),
        out_shape=jax.ShapeDtypeStruct(shape, F32 if final is None else BF16),
        in_specs=specs,
        out_specs=out_spec,
        scratch_shapes=scratch,
        input_output_aliases=aliases,
        compiler_params=pltpu.CompilerParams(vmem_limit_bytes=6 * MIB),
        cost_estimate=pl.CostEstimate(
            flops=2 * tokens * share * out_width,
            bytes_accessed=2 * share * out_width + 2 * tokens * (share + out_width),
            transcendentals=0,
        ),
        name="out_projection",
    )(*operands)


def shift(x, axis, by):
    n = lax.axis_size(axis)
    return lax.ppermute(x, axis, [(i, (i + by) % n) for i in range(n)])


def swap_cores(x):
    n = lax.axis_size("chan")
    return lax.ppermute(x, "chan", [(i, i ^ 1) for i in range(n)])


def gather_far(x):
    pieces = []
    for hop in range(1, lax.axis_size("chan") // 2):
        far = shift(x, "chan", 2 * hop)
        pieces += [far, swap_cores(far)]
    return pieces


def exchange(parts, first=1):
    out, n = list(parts[:first]), len(parts)
    for k in range(first, n):
        out.append(lax.ppermute(parts[k], "ctx", [(i, target(i, k, n)) for i in range(n)]))
    return out


def layer(features, filter_taps, skip_gain, in_weight, out_weight):
    return layer_body(features, filter_taps, skip_gain, in_weight, out_weight)


def layer_body(features, filter_taps, skip_gain, in_weight, out_weight):
    n_ctx = lax.axis_size("ctx")
    rows = features.shape[0]
    tokens = rows // CHUNKS
    tables = [jnp.asarray(t) for t in real_dft_tables(tokens)]
    w = in_weight.transpose(1, 0, 2)

    own = halves(features)
    far = [gather_far(own[c]) for c in range(CHUNKS)]
    near = swap_cores(features)
    forward, inverse, w_kv, w_q, spectra, skip = prologue(tables, skip_gain, filter_taps, w, n_ctx)

    mixed, query = [], []
    for c in range(CHUNKS):
        pieces = [own[c], near, *far[c]]
        starts = [0, c * tokens] + [0] * len(far[c])
        total = ()
        for part, which in ("a", (0, 1)), ("b", range(2, len(pieces) - 1)):
            total = keys_values(pieces, which, [starts[j] for j in which], tokens, w_kv, total, n_ctx)
        last, made = len(pieces) - 1, {}
        for part, slices, cuts in ("c", tuple(range(2, n_ctx)), c + 1), ("d", (1, 0), 1):
            some = keys_values(pieces, (last,), (starts[last],), tokens, w_kv, total, n_ctx, slices, cuts)
            made.update({k: some[i * cuts : (i + 1) * cuts] for i, k in enumerate(slices)})
        mixed.append([[made[k][h % len(made[k])] for k in range(n_ctx)] for h in range(PARTS)])
        every, before = range(len(pieces)), None
        if c == 0:
            before = queries(pieces, every[:2], starts[:2], tokens, w_q, None, n_ctx, False)
            every = every[2:]
        left = [starts[j] for j in every]
        query.append(queries(pieces, every, left, tokens, w_q, before, n_ctx, True))
    even = exchange(mixed[0][0])
    odd = [exchange(mixed[1][0])]
    odd += [odd[0][:2] + exchange(mixed[1][h], 2)[2:] for h in range(1, PARTS)]
    conv = convolve(forward, inverse, spectra, even, odd, n_ctx)

    joint = lax.ppermute(conv[-1][1], "ctx", [(i, target(i, 1, n_ctx)) for i in range(n_ctx)])
    gathered = []
    for r in range(CHUNKS * PARTS):
        c, h = r // PARTS, r % PARTS
        back = exchange(conv[r], 1 if c == 0 else 2)
        if c > 0:
            back[1] = joint
        share = back[2].shape[1]
        gated = gate(skip, query[c], mixed[c][h], back, h * share, share, n_ctx)
        beside = swap_cores(gated)
        gathered.append([gated, beside, *gather_far(gated)])
    both = tuple(range(PARTS))
    every = [(j, both) for j in range(len(gathered[0]))]
    last = every[-1][0]
    even, odd = gathered[:PARTS], gathered[PARTS:]
    out = project_out(even, every, out_weight, None, n_ctx, (0, rows, None))
    part = project_out(odd, every[:2], out_weight, None, n_ctx)
    part = project_out(odd, [*every[2:-1], (last, both[:-1])], out_weight, part, n_ctx)
    return project_out(odd, [(last, both[-1:])], out_weight, part, n_ctx, (tokens, rows, out))


P_SIZE = 128


def dft_tables(block_len):
    period = 2 * block_len
    freq_col = jnp.arange(period, dtype=jnp.int32)[:, None]
    place_row = jnp.arange(period, dtype=jnp.int32)[None, :]
    angles = (freq_col * place_row % period).astype(F32) * (2.0 * math.pi / period)
    forward = jnp.concatenate([jnp.cos(angles), -jnp.sin(angles)], axis=0).astype(BF16)
    out_place = jnp.arange(block_len, dtype=jnp.int32)[:, None] + block_len
    angle_out = (out_place * place_row % period).astype(F32) * (2.0 * math.pi / period)
    inverse = (jnp.concatenate([jnp.cos(angle_out), -jnp.sin(angle_out)], axis=1) / period).astype(BF16)
    return (forward, inverse)


def plain_layer(features, filter_taps, skip_gain, in_weight, out_weight):
    forward, inverse = dft_tables(P_SIZE)
    channels = in_weight.shape[2]
    tok_rows = features.shape[0]
    per_dev = tok_rows // P_SIZE
    period = 2 * P_SIZE
    total_blocks = per_dev * lax.axis_size("ctx")
    first_mine = lax.axis_index("ctx") * per_dev
    padded = jnp.concatenate([jnp.zeros((P_SIZE, channels), BF16), filter_taps], axis=0)
    tap_blocks = padded.reshape(total_blocks + 1, P_SIZE, channels)
    segments = jnp.concatenate([tap_blocks[:-1], tap_blocks[1:]], axis=1)
    lag = jnp.einsum("fn,knc->kfc", forward, segments, preferred_element_type=F32).astype(BF16)
    flipped = jnp.concatenate([lag[::-1], jnp.zeros_like(lag)], axis=0)
    gathered = lax.all_gather(features, "chan", axis=1, tiled=True)
    w = in_weight.transpose(1, 0, 2)
    q, k, v = (jnp.dot(gathered, w[s], preferred_element_type=F32) for s in range(3))
    query = q.astype(BF16)
    mixed = (k * v).astype(BF16)
    everyone = lax.all_gather(mixed, "ctx", axis=0, tiled=True).reshape(total_blocks, P_SIZE, channels)
    source = jnp.einsum("fp,bpc->bfc", forward[:, :P_SIZE], everyone, preferred_element_type=F32)
    source = source.astype(BF16).astype(F32)
    source_re, source_im = source[:, :period], source[:, period:]
    outputs = []
    for out_block in range(per_dev):
        start = total_blocks - 1 - (first_mine + out_block)
        window = lax.dynamic_slice_in_dim(flipped, start, total_blocks, 0).astype(F32)
        lag_re, lag_im = window[:, :period], window[:, period:]
        out_re = jnp.sum(lag_re * source_re - lag_im * source_im, axis=0)
        out_im = jnp.sum(lag_re * source_im + lag_im * source_re, axis=0)
        outputs.append(jnp.concatenate([out_re, out_im], axis=0))
    spectra = jnp.stack(outputs).astype(BF16)
    conv = jnp.einsum("tf,bfc->btc", inverse, spectra, preferred_element_type=F32)
    conv = conv.reshape(tok_rows, channels)
    gated = (query.astype(F32) * (conv + skip_gain[None, :] * mixed.astype(F32))).astype(BF16)
    everything = lax.all_gather(gated, "chan", axis=1, tiled=True)
    return jnp.dot(everything, out_weight, preferred_element_type=F32).astype(BF16)


def shards(features, filter_taps, skip_gain, in_weight, out_weight):
    slices = lax.axis_size("ctx") > 2 and in_weight.shape[2] % (lax.axis_size("ctx") * PARTS * LANES) == 0
    cores = lax.axis_size("chan") % 2 == 0 and lax.axis_size("chan") > 2
    blocks = features.shape[0] % (CHUNKS * LANES) == 0
    chosen = layer if slices and cores and blocks else plain_layer
    return chosen(features, filter_taps, skip_gain, in_weight, out_weight)


def solution(mesh):
    return jax.shard_map(
        shards,
        mesh=mesh,
        in_specs=(
            P(("grp", "ctx"), "chan"),
            P(None, "chan"),
            P("chan"),
            P(None, None, "chan"),
            P(None, "chan"),
        ),
        out_specs=P(("grp", "ctx"), "chan"),
        check_vma=False,
    )
```

```python
import functools
import math

import jax
import jax.numpy as jnp
import ml_dtypes
import numpy as np
from jax import lax
from jax.experimental import pallas as pl
from jax.experimental.pallas import tpu as pltpu
from jax.sharding import PartitionSpec as P


BF16 = jnp.bfloat16
F32 = jnp.float32
LANES = 128
MIB = 1 << 20
CHUNKS = 2
PARTS = 2
VMEM = pl.BlockSpec(memory_space=pltpu.VMEM)
HBM = pl.BlockSpec(memory_space=pltpu.HBM)


def real_dft_tables(block):
    period = 2 * block
    freq = np.arange(block)[:, None]
    place = np.arange(block)[None, :]
    angle = (freq * place % period) * (2.0 * math.pi / period)
    lower = -np.sin(angle)
    lower[0] = 1.0 - 2.0 * (np.arange(block) % 2)
    forward = np.concatenate([np.cos(angle), lower], axis=0)
    out_place = np.arange(block)[:, None] + block
    freq_row = np.arange(block)[None, :]
    angle_out = (out_place * freq_row % period) * (2.0 * math.pi / period)
    weight = np.where(freq_row == 0, 1.0, 2.0)
    lower_out = -np.sin(angle_out) * weight
    lower_out[:, 0] = 1.0 - 2.0 * (np.arange(block) % 2)
    inverse = np.concatenate([np.cos(angle_out) * weight, lower_out], axis=1) / period
    return forward.astype(ml_dtypes.bfloat16), inverse.astype(ml_dtypes.bfloat16)


def call(kernel, out, operands, limit, flops, moved, scratch=()):
    return pl.pallas_call(
        kernel,
        out_shape=out,
        in_specs=[VMEM] * len(operands),
        out_specs=jax.tree.map(lambda _: VMEM, out),
        scratch_shapes=scratch,
        compiler_params=pltpu.CompilerParams(vmem_limit_bytes=limit * MIB),
        cost_estimate=pl.CostEstimate(flops=flops, bytes_accessed=moved, transcendentals=0),
    )(*operands)


def chan_sources():
    n_chan, chan = lax.axis_size("chan"), lax.axis_index("chan")
    sources = [chan, chan ^ 1]
    for hop in range(1, n_chan // 2):
        far = (chan - 2 * hop + n_chan) % n_chan
        sources += [far, far ^ 1]
    return sources


def paired(n):
    return n & (n - 1) == 0


def target(me, k, n):
    return me ^ k if paired(n) else (me + k) % n


def origin(me, k, n):
    return me ^ k if paired(n) else (me - k + n) % n


def mirror(k, n):
    return k if paired(n) else -k % n


def rows_at(first, count):
    return pl.ds(pl.multiple_of(first * count, count), count)


def halves_kernel(x_ref, *refs):
    outs, sems = refs[:-1], refs[-1]
    rows = outs[0].shape[0]
    copies = [
        pltpu.make_async_copy(x_ref.at[c * rows : (c + 1) * rows], out, sems.at[c]) for c, out in enumerate(outs)
    ]
    for copy in copies:
        copy.start()
    for copy in copies:
        copy.wait()


def halves(x):
    out = [jax.ShapeDtypeStruct((x.shape[0] // CHUNKS, x.shape[1]), x.dtype)] * CHUNKS
    return pl.pallas_call(
        halves_kernel,
        out_shape=out,
        in_specs=[HBM],
        out_specs=[VMEM] * CHUNKS,
        scratch_shapes=[pltpu.SemaphoreType.DMA((CHUNKS,))],
        compiler_params=pltpu.CompilerParams(vmem_limit_bytes=2 * MIB),
        cost_estimate=pl.CostEstimate(flops=0, bytes_accessed=4 * x.size, transcendentals=0),
        name="halves",
    )(pltpu.with_memory_space_constraint(x, pltpu.HBM))


def prologue_kernel(
    width, skip_hbm, fwd_hbm, inv_hbm, taps_ref, w_ref, fwd_ref, inv_ref, kv_ref, query_ref, out_ref, skip_out, skip_ref, taps_in, prev_ref, sems
):
    block = inv_ref.shape[0]
    cols = rows_at(lax.axis_index("ctx"), width)
    copies = [
        pltpu.make_async_copy(skip_hbm, skip_ref, sems.at[4]),
        pltpu.make_async_copy(fwd_hbm, fwd_ref, sems.at[0]),
        pltpu.make_async_copy(taps_ref.at[:, cols], taps_in, sems.at[1]),
        pltpu.make_async_copy(inv_hbm, inv_ref, sems.at[2]),
        pltpu.make_async_copy(w_ref.at[1:3], kv_ref, sems.at[3]),
        pltpu.make_async_copy(w_ref.at[0], query_ref, sems.at[5]),
    ]
    for copy in copies:
        copy.start()
    prev_ref[...] = jnp.zeros_like(prev_ref)
    for copy in copies[:3]:
        copy.wait()
    for k in range(skip_out.shape[0]):
        skip_out[k, :] = skip_ref[k * width : (k + 1) * width]

    @pl.loop(0, out_ref.shape[0])
    def _(k):
        now = jnp.dot(fwd_ref[...], taps_in[rows_at(k, block), :], preferred_element_type=F32)
        parity = lax.broadcasted_iota(jnp.int32, now.shape, 0) % 2
        out_ref[k] = prev_ref[...] + jnp.where(parity == 0, now, -now)
        prev_ref[...] = now

    for copy in copies[3:]:
        copy.wait()


def prologue(tables, skip, taps, w, n_ctx):
    rows, block = tables[0].shape
    width = w.shape[2] // n_ctx
    count = taps.shape[0] // block
    out = [
        *(jax.ShapeDtypeStruct(t.shape, BF16) for t in tables),
        jax.ShapeDtypeStruct((2, *w.shape[1:]), BF16),
        jax.ShapeDtypeStruct(w.shape[1:], BF16),
        jax.ShapeDtypeStruct((count, rows, width), F32),
        jax.ShapeDtypeStruct((n_ctx, width), F32),
    ]
    return pl.pallas_call(
        functools.partial(prologue_kernel, width),
        out_shape=out,
        in_specs=[HBM] * 5,
        out_specs=[VMEM] * len(out),
        scratch_shapes=[
            pltpu.VMEM(skip.shape, F32),
            pltpu.VMEM((taps.shape[0], width), BF16),
            pltpu.VMEM((rows, width), F32),
            pltpu.SemaphoreType.DMA((6,)),
        ],
        compiler_params=pltpu.CompilerParams(vmem_limit_bytes=6 * MIB),
        cost_estimate=pl.CostEstimate(
            flops=2 * count * rows * block * width,
            bytes_accessed=2 * w.size + count * width * (rows * 4 + block * 2),
            transcendentals=0,
        ),
        name="prologue",
    )(*(pltpu.with_memory_space_constraint(x, pltpu.HBM) for x in (skip, *tables, taps, w)))


def kv_kernel(which, starts, n_ctx, has_before, slices, parts, w_ref, *refs):
    pieces, refs = refs[: len(which)], refs[len(which) :]
    before, outs = (refs[:2], refs[2:]) if has_before else ((), refs)
    tokens = outs[0].shape[0]
    width = w_ref.shape[2] // n_ctx
    depth = pieces[0].shape[1]
    me = lax.axis_index("ctx")
    sources = chan_sources()
    for k in slices or range(n_ctx):
        cols = rows_at(target(me, k, n_ctx), width)
        mine = slice(k * width, (k + 1) * width)
        key, value = (ref[:, mine] for ref in before) if has_before else (None, None)
        for piece, j, start in zip(pieces, which, starts):
            x = piece[start : start + tokens, :]
            rows = rows_at(sources[j], depth)
            a = jnp.dot(x, w_ref[0, rows, cols], preferred_element_type=F32)
            b = jnp.dot(x, w_ref[1, rows, cols], preferred_element_type=F32)
            key = a if key is None else key + a
            value = b if value is None else value + b
        if slices:
            made = (key * value).astype(BF16)
            for p in range(parts):
                cut = slice(p * width // parts, (p + 1) * width // parts)
                outs[slices.index(k) * parts + p][...] = made[:, cut]
        else:
            outs[0][:, mine] = key
            outs[1][:, mine] = value


def keys_values(pieces, which, starts, tokens, w, before, n_ctx, slices=(), parts=1):
    channels = w.shape[2]
    share = len(which) * pieces[0].shape[1]
    if slices:
        out = [jax.ShapeDtypeStruct((tokens, channels // n_ctx // parts), BF16)] * (len(slices) * parts)
    else:
        out = [jax.ShapeDtypeStruct((tokens, channels), F32)] * 2
    return call(
        functools.partial(kv_kernel, tuple(which), tuple(starts), n_ctx, bool(before), slices, parts),
        out,
        [w, *(pieces[j] for j in which), *before],
        6,
        4 * tokens * share * channels * (len(slices) or n_ctx) // n_ctx,
        4 * share * channels + 2 * tokens * share,
    )


def query_kernel(which, starts, n_ctx, has_before, w_ref, *refs):
    pieces, out_ref = refs[: len(which)], refs[-1]
    tokens = out_ref.shape[0]
    depth = pieces[0].shape[1]
    width = out_ref.shape[1] // n_ctx
    me = lax.axis_index("ctx")
    sources = chan_sources()
    for k in range(n_ctx):
        cols = rows_at(target(me, k, n_ctx), width)
        mine = slice(k * width, (k + 1) * width)
        acc = refs[len(which)][:, mine] if has_before else None
        for piece, j, start in zip(pieces, which, starts):
            x = piece[start : start + tokens, :]
            a = jnp.dot(x, w_ref[rows_at(sources[j], depth), cols], preferred_element_type=F32)
            acc = a if acc is None else acc + a
        out_ref[:, mine] = acc.astype(out_ref.dtype)


def queries(pieces, which, starts, tokens, w, before, n_ctx, last):
    channels = w.shape[1]
    share = len(which) * pieces[0].shape[1]
    return call(
        functools.partial(query_kernel, tuple(which), tuple(starts), n_ctx, before is not None),
        jax.ShapeDtypeStruct((tokens, channels), BF16 if last else F32),
        [w, *(pieces[j] for j in which)] + ([] if before is None else [before]),
        6,
        2 * tokens * share * channels,
        2 * share * channels + 2 * tokens * share,
    )


def block_products(g_ref, x_ref, before_ref, after_ref, plan, start, block):
    lags = sorted({lag for _, _, terms in plan for lag, _ in terms})
    slots = sorted({slot for _, _, terms in plan for _, slot in terms})

    def tile(i, first):
        upper = pl.ds(i * 8, 8) if first else rows_at(i, 8)
        lower = pl.ds(block + i * 8, 8) if first else rows_at(block // 8 + i, 8)
        for lane in range(x_ref.shape[2] // LANES):
            cols, own = pl.ds(start + lane * LANES, LANES), pl.ds(lane * LANES, LANES)
            g_re = {b: g_ref[b, upper, cols] for b in lags}
            g_im = {b: g_ref[b, lower, cols] for b in lags}
            x_re = {b: x_ref[b, upper, own] for b in slots}
            x_im = {b: x_ref[b, lower, own] for b in slots}
            g_di = g_re
            if first:
                edge = lax.broadcasted_iota(jnp.int32, (8, LANES), 0) == 0
                g_di = {b: jnp.where(edge, g_im[b], g_re[b]) for b in lags}
                g_im = {b: jnp.where(edge, 0.0, g_im[b]) for b in lags}
            for here, end, terms in plan:
                re = im = None
                if here is not None:
                    re, im = before_ref[here, upper, cols], before_ref[here, lower, cols]
                for lag, slot in terms:
                    up = g_re[lag] * x_re[slot] - g_im[lag] * x_im[slot]
                    down = g_di[lag] * x_im[slot] + g_im[lag] * x_re[slot]
                    re = up if re is None else re + up
                    im = down if im is None else im + down
                after_ref[end, upper, own] = re
                after_ref[end, lower, own] = im

    tile(0, True)
    pl.loop(1, block // 8)(lambda i: tile(i, False))


def part_of(ref, start, width):
    return ref[...] if ref.shape[1] == width else ref[:, start : start + width]


def forward_dft(n_ctx, fwd_ref, ins, x_ref, start):
    me = lax.axis_index("ctx")
    for k in range(n_ctx):
        piece = part_of(ins[k], start, x_ref.shape[2])
        x_ref[origin(me, k, n_ctx)] = jnp.dot(fwd_ref[...], piece, preferred_element_type=F32)


def inverse_dft(n_ctx, inv_ref, y_ref, outs):
    me = lax.axis_index("ctx")
    for k in range(n_ctx):
        spectrum = y_ref[target(me, k, n_ctx)].astype(BF16)
        made = jnp.dot(inv_ref[...], spectrum, preferred_element_type=F32).astype(BF16)
        share = outs[k][0].shape[1]
        for h, out in enumerate(outs[k]):
            out[...] = made[:, h * share : (h + 1) * share]


def early_kernel(n_ctx, fwd_ref, g_ref, *refs):
    ins, sum_ref, x_ref = refs[:n_ctx], refs[n_ctx], refs[n_ctx + 1]
    blocks, rows, _ = g_ref.shape
    forward_dft(n_ctx, fwd_ref, ins, x_ref, 0)
    plan = [(None, b, [(b - a, a // 2) for a in range(0, b + 1, 2)]) for b in range(blocks)]
    block_products(g_ref, x_ref, None, sum_ref, plan, 0, rows // 2)


def middle_kernel(n_ctx, start, fwd_ref, inv_ref, g_ref, sum_ref, *refs):
    ins, x_ref, outs, y_ref = refs[:n_ctx], refs[n_ctx], refs[n_ctx + 1 : -1], refs[-1]
    blocks, rows, _ = g_ref.shape
    forward_dft(n_ctx, fwd_ref, ins, x_ref, start)
    plan = [(b, b // 2, [(b - a, a // 2) for a in range(1, b, 2)]) for b in range(0, blocks, 2)]
    block_products(g_ref, x_ref, sum_ref, y_ref, plan, start, rows // 2)
    inverse_dft(n_ctx, inv_ref, y_ref, [[out] for out in outs])


def late_kernel(n_ctx, parts, inv_ref, g_ref, sum_ref, *refs):
    xs, outs, y_ref = refs[:parts], refs[parts:-1], refs[-1]
    blocks, rows, width = g_ref.shape
    share = width // parts
    plan = [(b, b // 2, [(b - a, a // 2) for a in range(1, b + 1, 2)]) for b in range(1, blocks, 2)]
    for h, x_ref in enumerate(xs):
        mine = y_ref.at[:, :, h * share : (h + 1) * share]
        block_products(g_ref, x_ref, sum_ref, mine, plan, h * share, rows // 2)
    inverse_dft(n_ctx, inv_ref, y_ref, [outs[k * parts : (k + 1) * parts] for k in range(n_ctx)])


def convolve(forward, inverse, spectra, even, odd, n_ctx):
    blocks, rows, width = spectra.shape
    parts = len(odd)
    share = width // parts
    some = (n_ctx, rows, share)
    piece = jax.ShapeDtypeStruct((rows // 2, share), BF16)
    flops, moved = blocks * rows * rows * width // 2, blocks * rows * width * 8
    sums = call(
        functools.partial(early_kernel, n_ctx),
        jax.ShapeDtypeStruct(spectra.shape, F32),
        [forward, spectra, *even],
        6,
        flops,
        moved,
        [pltpu.VMEM((n_ctx, rows, width), F32)],
    )
    first, xs = [], []
    for h in range(parts):
        x, *made = call(
            functools.partial(middle_kernel, n_ctx, h * share),
            [jax.ShapeDtypeStruct(some, F32)] + [piece] * n_ctx,
            [forward, inverse, spectra, sums, *odd[h]],
            6,
            flops // parts,
            moved // parts,
            [pltpu.VMEM(some, F32)],
        )
        first.append(made)
        xs.append(x)
    made = call(
        functools.partial(late_kernel, n_ctx, parts),
        [piece] * (n_ctx * parts),
        [inverse, spectra, sums, *xs],
        6,
        flops,
        moved,
        [pltpu.VMEM((n_ctx, rows, width), F32)],
    )
    return [*first, *(made[h::parts] for h in range(parts))]


def gate_kernel(n_ctx, start, share, skip_ref, q_ref, *refs):
    mixed, conv, out_ref = refs[:n_ctx], refs[n_ctx : 2 * n_ctx], refs[-1]
    width = q_ref.shape[1] // n_ctx
    me = lax.axis_index("ctx")
    for m in range(n_ctx):
        skip = skip_ref[pl.ds(target(me, m, n_ctx), 1), :][:, start : start + share]
        query = q_ref[:, m * width + start : m * width + start + share].astype(F32)
        source = part_of(mixed[m], start, share).astype(F32)
        total = part_of(conv[mirror(m, n_ctx)], start, share).astype(F32) + skip * source
        out_ref[:, m * share : (m + 1) * share] = (query * total).astype(BF16)


def gate(skip, query, mixed, conv, start, share, n_ctx):
    tokens = conv[0].shape[0]
    return call(
        functools.partial(gate_kernel, n_ctx, start, share),
        jax.ShapeDtypeStruct((tokens, share * n_ctx), BF16),
        [skip, query, *mixed, *conv],
        4,
        3 * tokens * share * n_ctx,
        8 * tokens * share * n_ctx,
    )


def out_kernel(which, parts, has_before, n_ctx, columns, row, w_ref, *refs):
    pieces, out_ref = refs[: sum(len(some) for _, some in which)], refs[-1 if row is None else -3]
    share = pieces[0].shape[1] // n_ctx
    width = share * parts
    me = lax.axis_index("ctx")
    sources = chan_sources()
    copies = []
    for i in range(w_ref.shape[1] // columns):
        cols = slice(i * columns, (i + 1) * columns)
        acc = refs[len(pieces)][:, cols] if has_before else None
        used = 0
        for j, some in which:
            group = pieces[used : used + len(some)]
            used += len(some)
            for m in range(n_ctx):
                first = (sources[j] * n_ctx + target(me, m, n_ctx)) * width + some[0] * share
                w = w_ref[pl.ds(pl.multiple_of(first, share), len(some) * share), cols]
                mine = slice(m * share, (m + 1) * share)
                x = jnp.concatenate([p[:, mine] for p in group], axis=1)
                a = jnp.dot(x, w, preferred_element_type=F32)
                acc = a if acc is None else acc + a
        if row is None:
            out_ref[:, cols] = acc
            continue
        made_ref, sems = refs[-2:]
        made_ref[:, cols] = acc.astype(BF16)
        there = out_ref.at[row : row + made_ref.shape[0], cols]
        copies.append(pltpu.make_async_copy(made_ref.at[:, cols], there, sems.at[i]))
        copies[-1].start()
    for copy in copies:
        copy.wait()


def project_out(gathered, which, w, before, n_ctx, final=None, columns=256):
    parts = len(gathered)
    tokens = gathered[0][0].shape[0]
    _, out_width = w.shape
    operands = [w, *(gathered[h][j] for j, some in which for h in some)] + ([] if before is None else [before])
    specs = [VMEM] * len(operands)
    aliases, scratch, row = {}, [], None
    out_spec, shape = VMEM, (tokens, out_width)
    if final is not None:
        row, rows, so_far = final
        out_spec, shape = HBM, (rows, out_width)
        scratch = [pltpu.VMEM((tokens, out_width), BF16), pltpu.SemaphoreType.DMA((out_width // columns,))]
        if so_far is not None:
            specs.append(HBM)
            aliases = {len(operands): 0}
            operands.append(so_far)
    share = sum(len(some) for _, some in which) * gathered[0][0].shape[1]
    return pl.pallas_call(
        functools.partial(out_kernel, tuple(which), parts, before is not None, n_ctx, columns, row),
        out_shape=jax.ShapeDtypeStruct(shape, F32 if final is None else BF16),
        in_specs=specs,
        out_specs=out_spec,
        scratch_shapes=scratch,
        input_output_aliases=aliases,
        compiler_params=pltpu.CompilerParams(vmem_limit_bytes=6 * MIB),
        cost_estimate=pl.CostEstimate(
            flops=2 * tokens * share * out_width,
            bytes_accessed=2 * share * out_width + 2 * tokens * (share + out_width),
            transcendentals=0,
        ),
        name="out_projection",
    )(*operands)


def shift(x, axis, by):
    n = lax.axis_size(axis)
    return lax.ppermute(x, axis, [(i, (i + by) % n) for i in range(n)])


def swap_cores(x):
    n = lax.axis_size("chan")
    return lax.ppermute(x, "chan", [(i, i ^ 1) for i in range(n)])


def gather_far(x):
    pieces = []
    for hop in range(1, lax.axis_size("chan") // 2):
        far = shift(x, "chan", 2 * hop)
        pieces += [far, swap_cores(far)]
    return pieces


def exchange(parts, first=1):
    out, n = list(parts[:first]), len(parts)
    for k in range(first, n):
        out.append(lax.ppermute(parts[k], "ctx", [(i, target(i, k, n)) for i in range(n)]))
    return out


def layer(features, filter_taps, skip_gain, in_weight, out_weight):
    return layer_body(features, filter_taps, skip_gain, in_weight, out_weight)


def layer_body(features, filter_taps, skip_gain, in_weight, out_weight):
    n_ctx = lax.axis_size("ctx")
    rows = features.shape[0]
    tokens = rows // CHUNKS
    tables = [jnp.asarray(t) for t in real_dft_tables(tokens)]
    w = in_weight.transpose(1, 0, 2)

    own = halves(features)
    far = [gather_far(own[c]) for c in range(CHUNKS)]
    near = swap_cores(features)
    forward, inverse, w_kv, w_q, spectra, skip = prologue(tables, skip_gain, filter_taps, w, n_ctx)

    mixed, query = [], []
    for c in range(CHUNKS):
        pieces = [own[c], near, *far[c]]
        starts = [0, c * tokens] + [0] * len(far[c])
        total = ()
        for part, which in ("a", (0, 1)), ("b", range(2, len(pieces) - 1)):
            total = keys_values(pieces, which, [starts[j] for j in which], tokens, w_kv, total, n_ctx)
        last, made = len(pieces) - 1, {}
        for part, slices, cuts in ("c", tuple(range(2, n_ctx)), c + 1), ("d", (1, 0), 1):
            some = keys_values(pieces, (last,), (starts[last],), tokens, w_kv, total, n_ctx, slices, cuts)
            made.update({k: some[i * cuts : (i + 1) * cuts] for i, k in enumerate(slices)})
        mixed.append([[made[k][h % len(made[k])] for k in range(n_ctx)] for h in range(PARTS)])
        every, before = range(len(pieces)), None
        if c == 0:
            before = queries(pieces, every[:2], starts[:2], tokens, w_q, None, n_ctx, False)
            every = every[2:]
        left = [starts[j] for j in every]
        query.append(queries(pieces, every, left, tokens, w_q, before, n_ctx, True))
    even = exchange(mixed[0][0])
    odd = [exchange(mixed[1][0])]
    odd += [odd[0][:2] + exchange(mixed[1][h], 2)[2:] for h in range(1, PARTS)]
    conv = convolve(forward, inverse, spectra, even, odd, n_ctx)

    gathered = []
    for r in range(CHUNKS * PARTS):
        c, h = r // PARTS, r % PARTS
        back = exchange(conv[r])
        share = back[0].shape[1]
        gated = gate(skip, query[c], mixed[c][h], back, h * share, share, n_ctx)
        beside = swap_cores(gated)
        gathered.append([gated, beside, *gather_far(gated)])
    both = tuple(range(PARTS))
    every = [(j, both) for j in range(len(gathered[0]))]
    last = every[-1][0]
    even, odd = gathered[:PARTS], gathered[PARTS:]
    out = project_out(even, every, out_weight, None, n_ctx, (0, rows, None))
    part = project_out(odd, every[:2], out_weight, None, n_ctx)
    part = project_out(odd, [*every[2:-1], (last, both[:-1])], out_weight, part, n_ctx)
    return project_out(odd, [(last, both[-1:])], out_weight, part, n_ctx, (tokens, rows, out))


P_SIZE = 128


def dft_tables(block_len):
    period = 2 * block_len
    freq_col = jnp.arange(period, dtype=jnp.int32)[:, None]
    place_row = jnp.arange(period, dtype=jnp.int32)[None, :]
    angles = (freq_col * place_row % period).astype(F32) * (2.0 * math.pi / period)
    forward = jnp.concatenate([jnp.cos(angles), -jnp.sin(angles)], axis=0).astype(BF16)
    out_place = jnp.arange(block_len, dtype=jnp.int32)[:, None] + block_len
    angle_out = (out_place * place_row % period).astype(F32) * (2.0 * math.pi / period)
    inverse = (jnp.concatenate([jnp.cos(angle_out), -jnp.sin(angle_out)], axis=1) / period).astype(BF16)
    return (forward, inverse)


def plain_layer(features, filter_taps, skip_gain, in_weight, out_weight):
    forward, inverse = dft_tables(P_SIZE)
    channels = in_weight.shape[2]
    tok_rows = features.shape[0]
    per_dev = tok_rows // P_SIZE
    period = 2 * P_SIZE
    total_blocks = per_dev * lax.axis_size("ctx")
    first_mine = lax.axis_index("ctx") * per_dev
    padded = jnp.concatenate([jnp.zeros((P_SIZE, channels), BF16), filter_taps], axis=0)
    tap_blocks = padded.reshape(total_blocks + 1, P_SIZE, channels)
    segments = jnp.concatenate([tap_blocks[:-1], tap_blocks[1:]], axis=1)
    lag = jnp.einsum("fn,knc->kfc", forward, segments, preferred_element_type=F32).astype(BF16)
    flipped = jnp.concatenate([lag[::-1], jnp.zeros_like(lag)], axis=0)
    gathered = lax.all_gather(features, "chan", axis=1, tiled=True)
    w = in_weight.transpose(1, 0, 2)
    q, k, v = (jnp.dot(gathered, w[s], preferred_element_type=F32) for s in range(3))
    query = q.astype(BF16)
    mixed = (k * v).astype(BF16)
    everyone = lax.all_gather(mixed, "ctx", axis=0, tiled=True).reshape(total_blocks, P_SIZE, channels)
    source = jnp.einsum("fp,bpc->bfc", forward[:, :P_SIZE], everyone, preferred_element_type=F32)
    source = source.astype(BF16).astype(F32)
    source_re, source_im = source[:, :period], source[:, period:]
    outputs = []
    for out_block in range(per_dev):
        start = total_blocks - 1 - (first_mine + out_block)
        window = lax.dynamic_slice_in_dim(flipped, start, total_blocks, 0).astype(F32)
        lag_re, lag_im = window[:, :period], window[:, period:]
        out_re = jnp.sum(lag_re * source_re - lag_im * source_im, axis=0)
        out_im = jnp.sum(lag_re * source_im + lag_im * source_re, axis=0)
        outputs.append(jnp.concatenate([out_re, out_im], axis=0))
    spectra = jnp.stack(outputs).astype(BF16)
    conv = jnp.einsum("tf,bfc->btc", inverse, spectra, preferred_element_type=F32)
    conv = conv.reshape(tok_rows, channels)
    gated = (query.astype(F32) * (conv + skip_gain[None, :] * mixed.astype(F32))).astype(BF16)
    everything = lax.all_gather(gated, "chan", axis=1, tiled=True)
    return jnp.dot(everything, out_weight, preferred_element_type=F32).astype(BF16)


def shards(features, filter_taps, skip_gain, in_weight, out_weight):
    slices = lax.axis_size("ctx") > 2 and in_weight.shape[2] % (lax.axis_size("ctx") * PARTS * LANES) == 0
    cores = lax.axis_size("chan") % 2 == 0 and lax.axis_size("chan") > 2
    blocks = features.shape[0] % (CHUNKS * LANES) == 0
    chosen = layer if slices and cores and blocks else plain_layer
    return chosen(features, filter_taps, skip_gain, in_weight, out_weight)


def solution(mesh):
    return jax.shard_map(
        shards,
        mesh=mesh,
        in_specs=(
            P(("grp", "ctx"), "chan"),
            P(None, "chan"),
            P("chan"),
            P(None, None, "chan"),
            P(None, "chan"),
        ),
        out_specs=P(("grp", "ctx"), "chan"),
        check_vma=False,
    )
```
